32 devices in a mesh: dp: 8 (over y, x, core), fsdp: 4 (over z).
Axes of the slice: x: 2, y: 2, z: 4, core: 2. Of those that a mesh axis runs over, the one named last changes fastest.
Arguments:
- patches: bfloat16 [16384, 1024], P(('dp', 'fsdp')), may hold values from -6 to 6
- cotangent: bfloat16 [16384, 1024], P(('dp', 'fsdp')), may hold values from -6 to 6
- ln1_gain: bfloat16 [1024], P('fsdp'), may hold values from 0.5 to 1.5
- ln1_bias: bfloat16 [1024], P('fsdp'), may hold values from -1.75 to 1.75
- w_qkv: bfloat16 [1024, 3072], P('fsdp'), may hold values from -0.1875 to 0.1875
- w_out: bfloat16 [1024, 1024], P('fsdp'), may hold values from -0.5 to 0.5
- ln2_gain: bfloat16 [1024], P('fsdp'), may hold values from 0.5 to 1.5
- ln2_bias: bfloat16 [1024], P('fsdp'), may hold values from -1.75 to 1.75
- w_fc1: bfloat16 [1024, 4096], P('fsdp'), may hold values from -0.1875 to 0.1875
- fc1_bias: bfloat16 [4096], P('fsdp'), may hold values from -3 to 3
- w_fc2: bfloat16 [4096, 1024], P('fsdp'), may hold values from -0.09375 to 0.09375
- pos_table: bfloat16 [50, 1024], P(None, 'fsdp'), may hold values from -3 to 3
- pos_index: int32 [145, 4], replicated, may hold values from 0 to 49, as said below
- pos_weight: float32 [145, 4], replicated, may hold values from 0.1 to 0.6
Outputs:
- block_out: bfloat16 [16384, 1024], P(('dp', 'fsdp'))
- input_grad: bfloat16 [16384, 1024], P(('dp', 'fsdp'))
- ln1_gain_grad: float32 [1024], P('fsdp')
- ln1_bias_grad: float32 [1024], P('fsdp')
- qkv_grad: float32 [1024, 3072], P('fsdp')
- out_proj_grad: float32 [1024, 1024], P('fsdp')
- ln2_gain_grad: float32 [1024], P('fsdp')
- ln2_bias_grad: float32 [1024], P('fsdp')
- fc1_grad: float32 [1024, 4096], P('fsdp')
- fc1_bias_grad: float32 [4096], P('fsdp')
- fc2_grad: float32 [4096, 1024], P('fsdp')
- table_grad: float32 [50, 1024], P(None, 'fsdp')
The draws below stay inside these ranges and needn't reach their ends.
Inputs may be any that keep to these rules, and one draw needn't show every extreme that they name: `pos_index`: row 0 names row 0 four times; every other row names rows 1 + 7i + j, 2 + 7i + j, 8 + 7i + j, 9 + 7i + j for some i, j in 0 to 5.
All inputs are finite; a program needn't handle non-finite values.
Results may differ from the reference program's by a relative error of at most 0.018.
Values may be sent and summed in bfloat16 or wider, within the bound.
No kernel may reach another device: no remote copies, remote signals or barrier semaphores. Data moves between devices by JAX's collectives and lax.ppermute only.
A program may use at most 192 MiB of HBM per device.

```python
import jax
import jax.numpy as jnp
from jax import lax

D = 1024
HEADS = 16
HDIM = 64
FF = 4096
POS = 50
HIGH_LEN = 145
ROWS = 512
LOW_DP = 3
TOKENS = 16384
N_DP = 8
N_FSDP = 4


def draw_pos_index(key, part):
    grid_side = 7
    first_key, second_key = jax.random.split(jax.random.fold_in(key, 11))
    across = jax.random.randint(first_key, (HIGH_LEN,), 0, grid_side - 1)
    down = jax.random.randint(second_key, (HIGH_LEN,), 0, grid_side - 1)
    corner = 1 + grid_side * across + down
    rows = jnp.arange(HIGH_LEN, dtype=jnp.int32)
    corner = jnp.where(rows == HIGH_LEN - 1, 1 + grid_side * (grid_side - 2) + grid_side - 2, corner)
    stacked = jnp.stack([corner, corner + 1, corner + grid_side, corner + grid_side + 1], axis=1)
    return jnp.where((rows == 0)[:, None], 0, stacked).astype(jnp.int32)


def steps_of(rng, shape, shards, least, top_value):
    def one(axis_at, parts):
        draws = jax.random.uniform(jax.random.fold_in(jax.random.fold_in(rng, 6), axis_at), (parts,), jnp.float32, least / len(shards), top_value / len(shards))
        return jnp.repeat(jnp.exp(draws), shape[axis_at] // parts).reshape((-1,) + (1,) * (len(shape) - axis_at - 1))

    level = one(*shards[0])
    for cut in shards[1:]:
        level = level * one(*cut)
    return level


def bell_draw(key, extent, scale, most, shards=(), held_as=jnp.bfloat16):
    array = jax.random.normal(key, extent, jnp.float32) * scale
    if len(shards) > 0:
        array = steps_of(key, extent, shards, -0.22, 0.18) * array
    return jnp.clip(array, min=-most, max=most).astype(held_as)


def setup_inputs(seed: int = 0) -> dict:
    seeds = jax.random.split(jax.random.key(seed), 15)
    return {
        "patches": bell_draw(seeds[0], (TOKENS, D), 1.0, 6.0, ((0, 32),)),
        "cotangent": bell_draw(seeds[1], (TOKENS, D), 1.0, 6.0, ((0, 32),)),
        "ln1_gain": jnp.clip(1.0 + 0.1 * jax.random.normal(seeds[2], (D,), jnp.float32), 0.5, 1.5).astype(jnp.bfloat16),
        "ln1_bias": bell_draw(seeds[3], (D,), 0.3, 1.75, ((0, 4),)),
        "w_qkv": bell_draw(seeds[4], (D, 3 * D), D ** -0.5, 0.1875, ((0, 4),)),
        "w_out": bell_draw(seeds[5], (D, D), (D // 8) ** -0.5, 0.5, ((0, 4),)),
        "ln2_gain": jnp.clip(1.0 + 0.1 * jax.random.normal(seeds[6], (D,), jnp.float32), 0.5, 1.5).astype(jnp.bfloat16),
        "ln2_bias": bell_draw(seeds[7], (D,), 0.3, 1.75, ((0, 4),)),
        "w_fc1": bell_draw(seeds[8], (D, FF), D ** -0.5, 0.1875, ((0, 4),)),
        "fc1_bias": bell_draw(seeds[9], (FF,), 0.5, 3.0, ((0, 4),)),
        "w_fc2": bell_draw(seeds[10], (FF, D), FF ** -0.5, 0.09375, ((0, 4),)),
        "pos_table": bell_draw(seeds[11], (POS, D), 0.5, 3.0, ((1, 4),)),
        "pos_index": draw_pos_index(jax.random.fold_in(seeds[14], 71), 0),
        "pos_weight": jnp.clip(jax.random.uniform(seeds[13], (HIGH_LEN, 4), jnp.float32, 0.1, 0.6), 0.1, 0.6),
    }


@jax.custom_vjp
def low(v):
    return lax.optimization_barrier(v.astype(jnp.bfloat16)).astype(jnp.float32)

@jax.custom_vjp
def low_back(v):
    return v

def low_keep(v):
    return (low(v), None)

def low_pass(kept, grad):
    return (grad,)

def back_keep(v):
    return (v, None)

def back_low(kept, grad):
    return (low(grad),)
low.defvjp(low_keep, low_pass)
low_back.defvjp(back_keep, back_low)
highest = lax.Precision.HIGHEST

def layer_norm(hidden, gain, shift):
    centre = hidden - lax.optimization_barrier(jnp.mean(hidden, axis=-1, keepdims=True))
    spread = lax.optimization_barrier(jnp.mean(centre * centre, axis=-1, keepdims=True))
    return centre * lax.rsqrt(spread + 1e-06) * gain + shift

def place_rows(rows, low_flag, interp):
    offsets = jnp.arange(rows, dtype=jnp.int32)
    table_ids = jnp.arange(POS, dtype=jnp.int32)
    high_ids = jnp.arange(HIGH_LEN, dtype=jnp.int32)
    low_valid = offsets < rows // POS * POS
    high_valid = offsets < rows // HIGH_LEN * HIGH_LEN
    low_place = (((offsets % POS)[:, None] == table_ids[None, :]) & low_valid[:, None]).astype(jnp.float32)
    high_pick = (((offsets % HIGH_LEN)[:, None] == high_ids[None, :]) & high_valid[:, None]).astype(jnp.float32)
    high_place = jnp.dot(high_pick, interp, precision=highest)
    place = jnp.where(low_flag, low_place, high_place)
    valid = jnp.where(low_flag, low_valid, high_valid)
    segment = jnp.where(low_flag, jnp.where(low_valid, offsets // POS, -1), jnp.where(high_valid, offsets // HIGH_LEN, -1))
    return (place, valid, segment[:, None] == segment[None, :])

def block_forward(patch_rows, low_flag, interp, params):
    gain_one, bias_one, w_qkv, w_out, gain_two, bias_two, w_fc1, fc1_bias, w_fc2, pos_table = params
    place, valid, mask = place_rows(ROWS, low_flag, interp)
    hidden_in = patch_rows + jnp.dot(place, pos_table, precision=highest)
    normed_one = low(layer_norm(hidden_in, gain_one, bias_one))
    projected = low_back(low(jnp.dot(normed_one, w_qkv, precision=highest)))
    queries = projected[:, :D].reshape(ROWS, HEADS, HDIM)
    keys = projected[:, D:2 * D].reshape(ROWS, HEADS, HDIM)
    values = projected[:, 2 * D:].reshape(ROWS, HEADS, HDIM)
    scores = low_back(jnp.einsum('qhd,khd->hqk', queries, keys, precision=highest) * HDIM ** (-0.5))
    scores = jnp.where(mask[None], scores, -1e+30)
    probs = low(jax.nn.softmax(scores, axis=-1))
    attended = jnp.einsum('hqk,khd->qhd', probs, values, precision=highest).reshape(ROWS, D)
    attended = low_back(low(attended))
    hidden_mid = hidden_in + low_back(jnp.dot(attended, w_out, precision=highest))
    normed_two = low(layer_norm(hidden_mid, gain_two, bias_two))
    pre_act = low_back(jnp.dot(normed_two, w_fc1, precision=highest) + fc1_bias)
    activated = low(jax.nn.gelu(pre_act, approximate=False))
    branch_out = jnp.dot(activated, w_fc2, precision=highest)
    return jnp.where(valid[:, None], hidden_mid + branch_out, 0.0)

def reference(patches, cotangent, ln1_gain, ln1_bias, w_qkv, w_out, ln2_gain, ln2_bias, w_fc1, fc1_bias, w_fc2, pos_table, pos_index, pos_weight):
    table_ids = jnp.arange(POS, dtype=jnp.int32)
    picks = (pos_index[:, :, None] == table_ids[None, None, :]).astype(jnp.float32)
    interp = lax.optimization_barrier(jnp.sum(pos_weight.astype(jnp.float32)[:, :, None] * picks, axis=1))
    blocks = N_DP * N_FSDP
    flags = jnp.arange(blocks, dtype=jnp.int32) // N_FSDP < LOW_DP

    def whole(patch_all, gain_one, bias_one, qkv_mat, out_mat, gain_two, bias_two, fc1_mat, fc1_shift, fc2_mat, table):
        params = (gain_one, bias_one, qkv_mat, out_mat, gain_two, bias_two, fc1_mat, fc1_shift, fc2_mat, table)

        def step(carry, item):
            return (carry, block_forward(item[0], item[1], interp, params))
        _, outs = lax.scan(jax.checkpoint(step), jnp.zeros((), jnp.float32), (patch_all.reshape(blocks, ROWS, D), flags))
        return outs.reshape(blocks * ROWS, D)
    floats = [patches, ln1_gain, ln1_bias, w_qkv, w_out, ln2_gain, ln2_bias, w_fc1, fc1_bias, w_fc2, pos_table]
    floats = [item.astype(jnp.float32) for item in floats]
    result, pull = jax.vjp(whole, *floats)
    grads = pull(cotangent.astype(jnp.float32))
    return (result.astype(jnp.bfloat16), grads[0].astype(jnp.bfloat16), grads[1], grads[2], grads[3], grads[4], grads[5], grads[6], grads[7], grads[8], grads[9], grads[10])
```

```python
import jax
import jax.numpy as jnp
from jax import lax
from jax.sharding import PartitionSpec as P

HEADS = 16
HDIM = 64
POS = 50
HIGH_LEN = 145


highest = lax.Precision.HIGHEST


def layer_norm(hidden, gain, shift):
    centre = hidden - jnp.mean(hidden, axis=-1, keepdims=True)
    spread = jnp.mean(centre * centre, axis=-1, keepdims=True)
    return centre * lax.rsqrt(spread + 1e-06) * gain + shift


def place_rows(rows, low_flag, pos_index, pos_weight):
    offsets = jnp.arange(rows, dtype=jnp.int32)
    table_ids = jnp.arange(POS, dtype=jnp.int32)
    high_ids = jnp.arange(HIGH_LEN, dtype=jnp.int32)
    picks = (pos_index[:, :, None] == table_ids[None, None, :]).astype(jnp.float32)
    interp = jnp.sum(pos_weight[:, :, None] * picks, axis=1)
    low_valid = offsets < rows // POS * POS
    high_valid = offsets < rows // HIGH_LEN * HIGH_LEN
    low_place = (((offsets % POS)[:, None] == table_ids[None, :]) & low_valid[:, None]).astype(
        jnp.float32
    )
    high_pick = (((offsets % HIGH_LEN)[:, None] == high_ids[None, :]) & high_valid[:, None]).astype(
        jnp.float32
    )
    high_place = jnp.dot(high_pick, interp, precision=highest)
    place = jnp.where(low_flag, low_place, high_place)
    valid = jnp.where(low_flag, low_valid, high_valid)
    segment = jnp.where(
        low_flag,
        jnp.where(low_valid, offsets // POS, -1),
        jnp.where(high_valid, offsets // HIGH_LEN, -1),
    )
    return (place, valid, segment[:, None] == segment[None, :])


def split_pairs(block):
    return block.reshape(block.shape[0], HEADS // 2, 2, HDIM).transpose(1, 0, 2, 3)


def join_pairs(block):
    return block.transpose(1, 0, 2, 3).reshape(block.shape[1], HEADS * HDIM)


def masked_scores(query_pair, key_pair, mask):
    scores = jnp.einsum(
        "qhd,khd->hqk", query_pair, key_pair, preferred_element_type=jnp.float32
    ) * HDIM ** (-0.5)
    return jnp.where(mask[None], scores, -1e30)


def forward(patches, params, place, mask):
    gain_one, bias_one, w_qkv, w_out, gain_two, bias_two, w_fc1, fc1_bias, w_fc2, pos_table = params
    width = w_out.shape[0]
    hidden_in = patches.astype(jnp.float32) + jnp.dot(
        place, pos_table.astype(jnp.float32), precision=highest
    )
    normed_one = layer_norm(
        hidden_in, gain_one.astype(jnp.float32), bias_one.astype(jnp.float32)
    ).astype(jnp.bfloat16)
    projected = jnp.dot(normed_one, w_qkv, preferred_element_type=jnp.float32).astype(jnp.bfloat16)
    queries = split_pairs(projected[:, :width])
    keys = split_pairs(projected[:, width : 2 * width])
    values = split_pairs(projected[:, 2 * width :])

    def attend(items):
        query_pair, key_pair, value_pair = items
        scores = masked_scores(query_pair, key_pair, mask)
        peak = jnp.max(scores, axis=-1, keepdims=True)
        expo = jnp.exp(scores - peak)
        total = jnp.sum(expo, axis=-1, keepdims=True)
        probs = (expo / total).astype(jnp.bfloat16)
        mixed = jnp.einsum("hqk,khd->qhd", probs, value_pair, preferred_element_type=jnp.float32)
        return (mixed.astype(jnp.bfloat16), (peak + jnp.log(total))[..., 0])

    attended, log_norm = lax.map(attend, (queries, keys, values))
    attn_rows = join_pairs(attended)
    hidden_mid = hidden_in + jnp.dot(attn_rows, w_out, preferred_element_type=jnp.float32)
    normed_two = layer_norm(
        hidden_mid, gain_two.astype(jnp.float32), bias_two.astype(jnp.float32)
    ).astype(jnp.bfloat16)
    pre_act = jnp.dot(normed_two, w_fc1, preferred_element_type=jnp.float32) + fc1_bias.astype(
        jnp.float32
    )
    activated = jax.nn.gelu(pre_act, approximate=False).astype(jnp.bfloat16)
    branch_out = jnp.dot(activated, w_fc2, preferred_element_type=jnp.float32)
    return (
        hidden_in,
        normed_one,
        projected,
        log_norm,
        attn_rows,
        hidden_mid,
        normed_two,
        pre_act,
        activated,
        branch_out,
    )


def backward(kept, params, place, mask, grad_out):
    gain_one, bias_one, w_qkv, w_out, gain_two, bias_two, w_fc1, fc1_bias, w_fc2, pos_table = params
    (
        hidden_in,
        normed_one,
        projected,
        log_norm,
        attn_rows,
        hidden_mid,
        normed_two,
        pre_act,
        activated,
        branch_out,
    ) = kept
    width = w_out.shape[0]
    grad_fc2 = jnp.einsum("rf,rd->fd", activated, grad_out, preferred_element_type=jnp.float32)
    grad_act = jnp.einsum("rd,fd->rf", grad_out, w_fc2, preferred_element_type=jnp.float32)
    _, pull_gelu = jax.vjp(lambda inner: jax.nn.gelu(inner, approximate=False), pre_act)
    grad_pre = pull_gelu(grad_act)[0].astype(jnp.bfloat16)
    grad_fc1_bias = jnp.sum(grad_pre.astype(jnp.float32), axis=0)
    grad_fc1 = jnp.einsum("rd,rf->df", normed_two, grad_pre, preferred_element_type=jnp.float32)
    grad_norm_two = jnp.einsum("rf,df->rd", grad_pre, w_fc1, preferred_element_type=jnp.float32)
    _, pull_two = jax.vjp(
        layer_norm, hidden_mid, gain_two.astype(jnp.float32), bias_two.astype(jnp.float32)
    )
    back_mid, grad_gain_two, grad_bias_two = pull_two(grad_norm_two)
    grad_mid = grad_out.astype(jnp.float32) + back_mid
    grad_branch = grad_mid.astype(jnp.bfloat16)
    grad_wout = jnp.einsum("rd,re->de", attn_rows, grad_branch, preferred_element_type=jnp.float32)
    grad_attn = jnp.einsum(
        "re,de->rd", grad_branch, w_out, preferred_element_type=jnp.float32
    ).astype(jnp.bfloat16)
    queries = split_pairs(projected[:, :width])
    keys = split_pairs(projected[:, width : 2 * width])
    values = split_pairs(projected[:, 2 * width :])
    grad_pairs = split_pairs(grad_attn)

    def attend_back(items):
        query_pair, key_pair, value_pair, grad_pair, log_pair = items
        scores = masked_scores(query_pair, key_pair, mask)
        probs = jnp.exp(scores - log_pair[..., None])
        probs_low = probs.astype(jnp.bfloat16)
        grad_probs = jnp.einsum(
            "qhd,khd->hqk", grad_pair, value_pair, preferred_element_type=jnp.float32
        )
        centre = jnp.sum(probs * grad_probs, axis=-1, keepdims=True)
        grad_scores = (probs * (grad_probs - centre)).astype(jnp.bfloat16)
        grad_query = jnp.einsum(
            "hqk,khd->qhd", grad_scores, key_pair, preferred_element_type=jnp.float32
        ) * HDIM ** (-0.5)
        grad_key = jnp.einsum(
            "hqk,qhd->khd", grad_scores, query_pair, preferred_element_type=jnp.float32
        ) * HDIM ** (-0.5)
        grad_value = jnp.einsum(
            "hqk,qhd->khd", probs_low, grad_pair, preferred_element_type=jnp.float32
        )
        return (grad_query, grad_key, grad_value)

    grad_query, grad_key, grad_value = lax.map(
        attend_back, (queries, keys, values, grad_pairs, log_norm)
    )
    grad_proj = jnp.concatenate(
        [join_pairs(grad_query), join_pairs(grad_key), join_pairs(grad_value)], axis=1
    ).astype(jnp.bfloat16)
    grad_qkv = jnp.einsum("rd,re->de", normed_one, grad_proj, preferred_element_type=jnp.float32)
    grad_norm_one = jnp.einsum("re,de->rd", grad_proj, w_qkv, preferred_element_type=jnp.float32)
    _, pull_one = jax.vjp(
        layer_norm, hidden_in, gain_one.astype(jnp.float32), bias_one.astype(jnp.float32)
    )
    back_in, grad_gain_one, grad_bias_one = pull_one(grad_norm_one)
    grad_in = grad_mid + back_in
    grad_table = jnp.dot(place.T, grad_in, precision=highest)
    grads = (
        grad_gain_one,
        grad_bias_one,
        grad_qkv,
        grad_wout,
        grad_gain_two,
        grad_bias_two,
        grad_fc1,
        grad_fc1_bias,
        grad_fc2,
        grad_table,
    )
    return (grad_in.astype(jnp.bfloat16), grads)


def hop_bit(core, stage, bits):
    return 1 + stage if core == 0 else bits - stage


def hop_pairs(n_dp, stage):
    bits = n_dp.bit_length() - 2
    return [(i, i ^ (1 << hop_bit(i % 2, stage, bits))) for i in range(n_dp)]


def swap_core(block, n_dp):
    return lax.ppermute(block, "dp", [(i, i ^ 1) for i in range(n_dp)])


def ahead(block, n_line, step):
    return lax.ppermute(block, "fsdp", [(i, (i + step) % n_line) for i in range(n_line)])


def line_gather(unit, n_line):
    if n_line <= 4:
        return jnp.stack([ahead(unit, n_line, step) for step in range(1, n_line)])
    every = lax.all_gather(unit, "fsdp", axis=0)
    order = (lax.axis_index("fsdp") - jnp.arange(1, n_line)) % n_line
    return jnp.take(every, order, axis=0)


def spread(parts, n_dp):
    for stage in range(n_dp.bit_length() - 2):
        send = jnp.concatenate(parts) if len(parts) > 1 else parts[0]
        parts = parts + [lax.ppermute(send, "dp", hop_pairs(n_dp, stage))]
    return parts + [swap_core(jnp.concatenate(parts), n_dp)]


def add_up(terms):
    total = terms[0].astype(jnp.float32)
    for term in terms[1:]:
        total = total + term.astype(jnp.float32)
    return total


def reduce_units(away, keep, n_dp, n_line):
    terms = [keep, swap_core(away, n_dp)]
    half = keep.shape[0] // 2
    for stage in range(n_dp.bit_length() - 2):
        send = add_up([term[half:] for term in terms]).astype(jnp.bfloat16)
        terms = [term[:half] for term in terms] + [lax.ppermute(send, "dp", hop_pairs(n_dp, stage))]
        half //= 2
    terms = [term[0] for term in terms]
    if n_line <= 4:
        arrived = [
            ahead(add_up([term[step] for term in terms]).astype(jnp.bfloat16), n_line, step)
            for step in range(1, n_line)
        ]
        total = add_up([term[0] for term in terms] + arrived)
    else:
        order = (jnp.arange(n_line) - lax.axis_index("fsdp")) % n_line
        line = jnp.take(add_up(terms).astype(jnp.bfloat16), order, axis=0)
        total = lax.psum_scatter(line, "fsdp", scatter_dimension=0)
    return jnp.concatenate(spread([total.astype(jnp.bfloat16)[None]], n_dp))


def place_of(n_dp, me, flip):
    bits = n_dp.bit_length() - 2
    core = me % 2
    halves = []
    for other in range(2):
        place = jnp.arange(1 << bits, dtype=jnp.int32)
        owner = jnp.full((1 << bits,), me ^ other, jnp.int32)
        for stage in range(bits):
            at = bits - 1 - stage if flip else stage
            low = 1 << hop_bit(0, stage, bits)
            high = 1 << hop_bit(1, stage, bits)
            mask = jnp.where((core ^ other) == 0, low, high)
            owner = owner ^ (((place >> at) & 1) * mask)
        halves.append(owner)
    return jnp.concatenate(halves)


def inverse(owner, n):
    return jnp.argmax(owner[None, :] == jnp.arange(n)[:, None], axis=1)


def per_device(
    patches,
    cotangent,
    ln1_gain,
    ln1_bias,
    w_qkv,
    w_out,
    ln2_gain,
    ln2_bias,
    w_fc1,
    fc1_bias,
    w_fc2,
    pos_table,
    pos_index,
    pos_weight,
):
    bf16 = jnp.bfloat16
    n_dp = lax.axis_size("dp")
    n_line = lax.axis_size("fsdp")
    dp = lax.axis_index("dp")
    line = lax.axis_index("fsdp")
    low_flag = dp < n_dp * 7 // 16
    rows = patches.shape[0]
    width = patches.shape[1]
    shard = width // n_line
    place, valid, mask = place_rows(rows, low_flag, pos_index, pos_weight)

    def column_units(matrix):
        return matrix.reshape(matrix.shape[0], n_dp, -1).transpose(1, 0, 2)

    def row_units(matrix):
        return matrix.reshape(n_dp, -1, matrix.shape[1])

    own_one = jnp.concatenate([column_units(w_qkv), column_units(w_out)], axis=2)
    own_two = column_units(w_fc1)
    own_three = row_units(w_fc2)
    deep, wide = own_one.shape[1:]
    smalls = jnp.concatenate(
        [
            jnp.stack([ln1_gain, ln1_bias, ln2_gain, ln2_bias]),
            fc1_bias.reshape(-1, shard),
            pos_table,
        ]
    )
    n_small = smalls.shape[0]
    fold = wide // shard
    small_rows = -(-n_small // (16 * fold)) * 16
    smalls = jnp.pad(smalls, ((0, small_rows * fold - n_small), (0, 0)))
    packed = lax.optimization_barrier(
        jnp.concatenate([smalls[i * small_rows : (i + 1) * small_rows] for i in range(fold)], axis=1)
    )

    def pick(units):
        return lax.dynamic_index_in_dim(units, dp, 0, keepdims=False)

    first = line_gather(jnp.concatenate([pick(own_one), packed]), n_line)
    got_one = spread([first[:, :deep][None]], n_dp)
    got_two = spread([line_gather(pick(own_two), n_line)[None]], n_dp)
    got_three = spread([line_gather(pick(own_three), n_line)[None]], n_dp)

    unplace = inverse(place_of(n_dp, dp, False), n_dp)
    unline = (line - jnp.arange(n_line)) % n_line

    def whole(own, got):
        every = jnp.concatenate([jnp.take(own, place_of(n_dp, dp, False), axis=0)[:, None], jnp.concatenate(got)], axis=1)
        return jnp.take(jnp.take(every, unplace, axis=0), unline, axis=1)

    def by_columns(units):
        return units.transpose(1, 2, 0, 3).reshape(n_line * units.shape[2], -1)

    full_one = whole(own_one, got_one)
    cut = w_qkv.shape[1] // n_dp
    full_qkv = by_columns(full_one[..., :cut])
    full_out = by_columns(full_one[..., cut:])
    full_fc1 = by_columns(whole(own_two, got_two))
    full_fc2 = whole(own_three, got_three).transpose(1, 0, 2, 3).reshape(-1, width)
    far = jnp.concatenate(
        [first[:, deep:, i * shard : (i + 1) * shard] for i in range(fold)], axis=1
    )
    table = jnp.take(jnp.concatenate([smalls[None], far]), unline, axis=0)

    def across(block):
        return block.transpose(1, 0, 2).reshape(block.shape[1], width)

    vectors = across(table[:, :4])
    full_bias = table[:, 4 : 4 + fc1_bias.size // shard].reshape(-1)
    full_table = across(table[:, 4 + fc1_bias.size // shard : n_small])
    params = (
        vectors[0],
        vectors[1],
        full_qkv,
        full_out,
        vectors[2],
        vectors[3],
        full_fc1,
        full_bias,
        full_fc2,
        full_table,
    )
    kept = forward(patches, params, place, mask)
    block_out = jnp.where(valid[:, None], kept[5] + kept[9], 0.0).astype(bf16)
    grad_out = jnp.where(valid[:, None], cotangent, jnp.zeros_like(cotangent))
    input_grad, grads = backward(kept, params, place, mask, grad_out)

    send_place = place_of(n_dp, dp, True)
    send_line = (line + jnp.arange(n_line)) % n_line

    def reduced(units):
        units = jnp.take(jnp.take(units, send_place, axis=0), send_line, axis=1)
        half = n_dp // 2
        done = reduce_units(units[half:], units[:half], n_dp, n_line)
        return jnp.take(done, unplace, axis=0)

    def grad_columns(grad):
        return grad.astype(bf16).reshape(n_line, -1, n_dp, grad.shape[1] // n_dp).transpose(2, 0, 1, 3)

    sum_three = reduced(grads[8].astype(bf16).reshape(n_line, n_dp, -1, width).transpose(1, 0, 2, 3))
    sum_two = reduced(grad_columns(grads[6]))

    def split(block):
        return block.reshape(-1, n_line, shard).transpose(1, 0, 2)

    rows_small = jnp.concatenate(
        [
            split(jnp.stack([grads[0], grads[1], grads[4], grads[5]])),
            grads[7].reshape(n_line, -1, shard),
            split(grads[9]),
        ],
        axis=1,
    ).astype(bf16)
    per_dp = -(-n_small // n_dp)
    rows_small = jnp.pad(rows_small, ((0, 0), (0, per_dp * n_dp - n_small), (0, 0)))
    rows_small = rows_small.reshape(n_line, n_dp, per_dp, shard).transpose(1, 0, 2, 3)
    extra = -(-per_dp // 16) * 16
    rows_small = lax.optimization_barrier(
        jnp.pad(rows_small, ((0, 0), (0, 0), (0, extra - per_dp), (0, wide - shard)))
    )
    sum_one = reduced(
        jnp.concatenate(
            [
                jnp.concatenate([grad_columns(grads[2]), grad_columns(grads[3])], axis=3),
                rows_small,
            ],
            axis=2,
        )
    )

    def flat_columns(units):
        return units.transpose(1, 0, 2).reshape(units.shape[1], -1).astype(jnp.float32)

    small = sum_one[:, deep : deep + per_dp, :shard].reshape(-1, shard)[:n_small]
    small = small.astype(jnp.float32)
    n_bias = fc1_bias.size // shard
    return (
        block_out,
        input_grad,
        small[0],
        small[1],
        flat_columns(sum_one[:, :deep, :cut]),
        flat_columns(sum_one[:, :deep, cut:]),
        small[2],
        small[3],
        flat_columns(sum_two),
        small[4 : 4 + n_bias].reshape(-1),
        sum_three.reshape(-1, width).astype(jnp.float32),
        small[4 + n_bias :],
    )


def solution(mesh):
    return jax.shard_map(
        per_device,
        mesh=mesh,
        in_specs=(
            P(("dp", "fsdp"), None),
            P(("dp", "fsdp"), None),
            P("fsdp"),
            P("fsdp"),
            P("fsdp", None),
            P("fsdp", None),
            P("fsdp"),
            P("fsdp"),
            P("fsdp", None),
            P("fsdp"),
            P("fsdp", None),
            P(None, "fsdp"),
            P(),
            P(),
        ),
        out_specs=(
            P(("dp", "fsdp"), None),
            P(("dp", "fsdp"), None),
            P("fsdp"),
            P("fsdp"),
            P("fsdp", None),
            P("fsdp", None),
            P("fsdp"),
            P("fsdp"),
            P("fsdp", None),
            P("fsdp"),
            P("fsdp", None),
            P(None, "fsdp"),
        ),
        check_vma=False,
    )
```

```python
import jax
import jax.numpy as jnp
from jax import lax
from jax.experimental import pallas as pl
from jax.experimental.pallas import tpu as pltpu
from jax.sharding import PartitionSpec as P

HEADS = 16
HDIM = 64
POS = 50
HIGH_LEN = 145
TILE = 128


highest = lax.Precision.HIGHEST


def layer_norm(hidden, gain, shift):
    centre = hidden - jnp.mean(hidden, axis=-1, keepdims=True)
    spread = jnp.mean(centre * centre, axis=-1, keepdims=True)
    return centre * lax.rsqrt(spread + 1e-06) * gain + shift


def place_rows(rows, low_flag, pos_index, pos_weight):
    offsets = jnp.arange(rows, dtype=jnp.int32)
    table_ids = jnp.arange(POS, dtype=jnp.int32)
    high_ids = jnp.arange(HIGH_LEN, dtype=jnp.int32)
    picks = (pos_index[:, :, None] == table_ids[None, None, :]).astype(jnp.float32)
    interp = jnp.sum(pos_weight[:, :, None] * picks, axis=1)
    low_valid = offsets < rows // POS * POS
    high_valid = offsets < rows // HIGH_LEN * HIGH_LEN
    low_place = (((offsets % POS)[:, None] == table_ids[None, :]) & low_valid[:, None]).astype(
        jnp.float32
    )
    high_pick = (((offsets % HIGH_LEN)[:, None] == high_ids[None, :]) & high_valid[:, None]).astype(
        jnp.float32
    )
    high_place = jnp.dot(high_pick, interp, precision=highest)
    place = jnp.where(low_flag, low_place, high_place)
    valid = jnp.where(low_flag, low_valid, high_valid)
    segment = jnp.where(
        low_flag,
        jnp.where(low_valid, offsets // POS, -1),
        jnp.where(high_valid, offsets // HIGH_LEN, -1),
    )
    return (place, valid, segment)


def key_windows(rows):
    out = []
    for start in range(0, rows, TILE):
        least, most = rows, 0
        for size in (POS, HIGH_LEN):
            used = rows // size * size
            for row in (start, start + TILE - 1):
                image = row // size
                begin = image * size if row < used else used
                end = begin + size if row < used else rows
                least, most = min(least, begin), max(most, end)
        out.append((start, least // TILE * TILE, -(-most // TILE) * TILE))
    return out


def times_t(left, right):
    return lax.dot_general(left, right, (((1,), (1,)), ((), ())), preferred_element_type=jnp.float32)


def t_times(left, right):
    return lax.dot_general(left, right, (((0,), (0,)), ((), ())), preferred_element_type=jnp.float32)


def halves(block, scale=None):
    lane = lax.broadcasted_iota(jnp.int32, block.shape, 1)
    if scale is not None:
        block = block * jnp.asarray(scale, block.dtype)
    zero = jnp.zeros_like(block)
    return (jnp.where(lane < HDIM, block, zero), jnp.where(lane < HDIM, zero, block))


def soft(query, keys, same):
    scores = jnp.where(same, times_t(query, keys), -1e30)
    expo = jnp.exp(scores - jnp.max(scores, axis=-1, keepdims=True))
    return expo * (1.0 / jnp.sum(expo, axis=-1, keepdims=True))


def attend_body(windows, col_ref, row_ref, q_ref, k_ref, v_ref, out_ref):
    values = halves(v_ref[...])
    for start, lo, hi in windows:
        rows = slice(start, start + TILE)
        same = col_ref[rows, :] == row_ref[:, lo:hi]
        keys = k_ref[lo:hi, :]
        total = None
        for query, value in zip(halves(q_ref[rows, :], HDIM ** (-0.5)), values):
            probs = soft(query, keys, same).astype(jnp.bfloat16)
            part = jnp.dot(probs, value[lo:hi], preferred_element_type=jnp.float32)
            total = part if total is None else total + part
        out_ref[rows, :] = total.astype(jnp.bfloat16)


def attend_back_body(windows, col_ref, row_ref, q_ref, k_ref, v_ref, g_ref, out_ref, dk_ref, dv_ref):
    width = q_ref.shape[1]
    full = out_ref.shape[1] // 3
    at = pl.program_id(0) * width
    dk_ref[...] = jnp.zeros_like(dk_ref)
    dv_ref[...] = jnp.zeros_like(dv_ref)
    scaled = halves(k_ref[...], HDIM ** (-0.5))
    for start, lo, hi in windows:
        rows = slice(start, start + TILE)
        same = col_ref[rows, :] == row_ref[:, lo:hi]
        keys = k_ref[lo:hi, :]
        values = v_ref[lo:hi, :]
        total = None
        queries = halves(q_ref[rows, :], HDIM ** (-0.5))
        grads = halves(g_ref[rows, :])
        for query, grad, key in zip(queries, grads, scaled):
            probs = soft(query, keys, same)
            grad_probs = times_t(grad, values)
            centre = jnp.sum(probs * grad_probs, axis=-1, keepdims=True)
            grad_scores = (probs * (grad_probs - centre)).astype(jnp.bfloat16)
            part = jnp.dot(grad_scores, key[lo:hi], preferred_element_type=jnp.float32)
            total = part if total is None else total + part
            dk_ref[lo:hi, :] += t_times(grad_scores, query)
            dv_ref[lo:hi, :] += t_times(probs.astype(jnp.bfloat16), grad)
        out_ref[rows, pl.ds(pl.multiple_of(at, width), width)] = total.astype(jnp.bfloat16)
    out_ref[:, pl.ds(pl.multiple_of(full + at, width), width)] = dk_ref[...].astype(jnp.bfloat16)
    out_ref[:, pl.ds(pl.multiple_of(2 * full + at, width), width)] = dv_ref[...].astype(jnp.bfloat16)


def pair_specs(rows, pairs):
    pair = 2 * HDIM
    whole = [
        pl.BlockSpec((rows, 1), lambda i: (0, 0)),
        pl.BlockSpec((1, rows), lambda i: (0, 0)),
    ]
    return whole + [
        pl.BlockSpec((rows, pair), lambda i, j=j: (0, j * pairs + i)) for j in range(3)
    ]


def attend(projected, segment):
    rows = projected.shape[0]
    pairs = HEADS // 2
    windows = key_windows(rows)

    def body(*refs):
        attend_body(windows, *refs)

    return pl.pallas_call(
        body,
        grid=(pairs,),
        in_specs=pair_specs(rows, pairs),
        out_specs=pl.BlockSpec((rows, 2 * HDIM), lambda i: (0, i)),
        out_shape=jax.ShapeDtypeStruct((rows, HEADS * HDIM), jnp.bfloat16),
        name="attend",
    )(segment[:, None], segment[None, :], projected, projected, projected)


def attend_back(projected, grad_attn, segment):
    rows = projected.shape[0]
    pairs = HEADS // 2
    windows = key_windows(rows)

    def body(*refs):
        attend_back_body(windows, *refs)

    return pl.pallas_call(
        body,
        grid=(pairs,),
        in_specs=pair_specs(rows, pairs) + [pl.BlockSpec((rows, 2 * HDIM), lambda i: (0, i))],
        out_specs=pl.BlockSpec((rows, 3 * HEADS * HDIM), lambda i: (0, 0)),
        out_shape=jax.ShapeDtypeStruct((rows, 3 * HEADS * HDIM), jnp.bfloat16),
        scratch_shapes=[pltpu.VMEM((rows, 2 * HDIM), jnp.float32)] * 2,
        name="attend_back",
    )(segment[:, None], segment[None, :], projected, projected, projected, grad_attn)


def copies(pairs_of, sems):
    moves = [
        pltpu.make_async_copy(source, target, sems.at[i])
        for i, (source, target) in enumerate(pairs_of)
    ]
    for move in moves:
        move.start()
    for move in moves:
        move.wait()


def assemble(owns, parts, table, n_line, unit):
    n_places = sum(part.shape[0] for part in parts)
    n_own = len(owns)
    n_parts = len(parts)
    ends = []
    for own in owns:
        ends.append((ends[-1] if ends else 0) + own.shape[1])
    count = n_own * (1 + n_places * (n_line - 1))

    def body(table_ref, *refs):
        own_refs = refs[:n_own]
        part_refs = refs[n_own : n_own + n_parts]
        out_refs = refs[n_own + n_parts : 2 * n_own + n_parts]
        sems = refs[-1]
        todo = []
        for own_ref, out_ref, end in zip(own_refs, out_refs, ends):
            shard_rows = own_ref.shape[0]
            columns = pl.ds(end - own_ref.shape[1], own_ref.shape[1])
            first = pl.multiple_of(table_ref[n_places * n_line] * unit, unit)
            todo.append((own_ref, out_ref.at[pl.ds(first, shard_rows), :]))
            place = 0
            for part_ref in part_refs:
                for k in range(part_ref.shape[0]):
                    for step in range(1, n_line):
                        row = pl.multiple_of(table_ref[place * n_line + step] * unit, unit)
                        todo.append(
                            (
                                part_ref.at[k, step - 1, pl.ds(0, unit), columns],
                                out_ref.at[pl.ds(row, unit), :],
                            )
                        )
                    place += 1
        copies(todo, sems)

    anywhere = pl.BlockSpec(memory_space=pl.ANY)
    return pl.pallas_call(
        body,
        in_specs=[pl.BlockSpec(memory_space=pltpu.SMEM)] + [anywhere] * (n_own + n_parts),
        out_specs=[anywhere] * n_own,
        out_shape=[
            jax.ShapeDtypeStruct((own.shape[0] * n_line, own.shape[1]), own.dtype) for own in owns
        ],
        scratch_shapes=[pltpu.SemaphoreType.DMA((count,))],
        name="assemble",
    )(table, *owns, *parts)


def column_order(block, table, unit):
    count = block.shape[1] // unit

    def body(table_ref, in_ref, out_ref, sems):
        copies(
            [
                (
                    in_ref.at[:, pl.ds(pl.multiple_of(table_ref[i] * unit, unit), unit)],
                    out_ref.at[:, pl.ds(i * unit, unit)],
                )
                for i in range(count)
            ],
            sems,
        )

    anywhere = pl.BlockSpec(memory_space=pl.ANY)
    return pl.pallas_call(
        body,
        in_specs=[pl.BlockSpec(memory_space=pltpu.SMEM), anywhere],
        out_specs=anywhere,
        out_shape=jax.ShapeDtypeStruct(block.shape, block.dtype),
        scratch_shapes=[pltpu.SemaphoreType.DMA((count,))],
        name="column_order",
    )(table, block)


def finish(parts, owner, cuts):
    unit = parts[0].shape[1]
    n_places = sum(part.shape[0] for part in parts)

    def body(owner_ref, *refs):
        part_refs = refs[: len(parts)]
        out_refs = refs[len(parts) :]
        place = 0
        for part_ref in part_refs:
            for k in range(part_ref.shape[0]):
                row = pl.multiple_of(owner_ref[place] * unit, unit)
                at = 0
                for out_ref, cut in zip(out_refs, cuts):
                    out_ref[pl.ds(row, unit), :] = part_ref[k, :, at : at + cut].astype(jnp.float32)
                    at += cut
                place += 1

    return pl.pallas_call(
        body,
        in_specs=[pl.BlockSpec(memory_space=pltpu.SMEM)]
        + [pl.BlockSpec(memory_space=pltpu.VMEM)] * len(parts),
        out_specs=[pl.BlockSpec(memory_space=pltpu.VMEM)] * len(cuts),
        out_shape=[jax.ShapeDtypeStruct((n_places * unit, cut), jnp.float32) for cut in cuts],
        name="finish",
    )(owner, *parts)


def hop_bit(core, stage, bits):
    return 1 + stage if core == 0 else bits - stage


def hop_pairs(n_dp, stage):
    bits = n_dp.bit_length() - 2
    return [(i, i ^ (1 << hop_bit(i % 2, stage, bits))) for i in range(n_dp)]


def swap_core(block, n_dp):
    return lax.ppermute(block, "dp", [(i, i ^ 1) for i in range(n_dp)])


def ahead(block, n_line, step):
    return lax.ppermute(block, "fsdp", [(i, (i + step) % n_line) for i in range(n_line)])


def line_gather(unit, n_line):
    return jnp.stack([ahead(unit, n_line, step) for step in range(1, n_line)])


def spread(part, n_dp):
    parts = [part]
    for stage in range(n_dp.bit_length() - 2):
        parts = parts + [lax.ppermute(item, "dp", hop_pairs(n_dp, stage)) for item in parts]
    return parts + [swap_core(item, n_dp) for item in parts]


def add_up(terms):
    total = terms[0].astype(jnp.float32)
    for term in terms[1:]:
        total = total + term.astype(jnp.float32)
    return total


def reduce_units(away, keep, n_dp, n_line):
    terms = [keep, swap_core(away, n_dp)]
    half = keep.shape[0] // 2
    for stage in range(n_dp.bit_length() - 2):
        send = add_up([term[half:] for term in terms]).astype(jnp.bfloat16)
        terms = [term[:half] for term in terms] + [lax.ppermute(send, "dp", hop_pairs(n_dp, stage))]
        half //= 2
    terms = [term[0] for term in terms]
    arrived = [
        ahead(add_up([term[step] for term in terms]).astype(jnp.bfloat16), n_line, step)
        for step in range(1, n_line)
    ]
    total = add_up([term[0] for term in terms] + arrived)
    return spread(total.astype(jnp.bfloat16)[None], n_dp)


def place_of(n_dp, me, flip):
    bits = n_dp.bit_length() - 2
    core = me % 2
    halves = []
    for other in range(2):
        place = jnp.arange(1 << bits, dtype=jnp.int32)
        owner = jnp.full((1 << bits,), me ^ other, jnp.int32)
        for stage in range(bits):
            at = bits - 1 - stage if flip else stage
            low = 1 << hop_bit(0, stage, bits)
            high = 1 << hop_bit(1, stage, bits)
            mask = jnp.where((core ^ other) == 0, low, high)
            owner = owner ^ (((place >> at) & 1) * mask)
        halves.append(owner)
    return jnp.concatenate(halves)


class Wide:
    def __init__(self, shard):
        self.shard = shard

    def gather(self, w_qkv, w_out, w_fc1, w_fc2, smalls):
        def full(matrix):
            return lax.all_gather(matrix, "fsdp", axis=0, tiled=True)

        table = lax.all_gather(smalls, "fsdp", axis=0)
        return (table, full(w_qkv), full(w_out), full(w_fc1), full(w_fc2))

    def rows(self, block):
        return block

    def wide_columns(self, block):
        return block

    def total(self, terms):
        bf16 = jnp.bfloat16
        outs = []
        for left, right in terms:
            grad = t_times(left, right).astype(bf16)
            own = lax.psum_scatter(grad, "fsdp", scatter_dimension=0, tiled=True)
            outs.append(lax.psum(own, "dp").astype(jnp.float32))
        return outs

    def total_small(self, terms, smalls):
        own = lax.psum_scatter(
            smalls.astype(jnp.bfloat16), "fsdp", scatter_dimension=0, tiled=False
        )
        return self.total(terms) + [lax.psum(own, "dp").astype(jnp.float32)]


class Staged:
    def __init__(self, n_dp, n_line, dp, line, width):
        self.n_dp = n_dp
        self.n_line = n_line
        self.dp = dp
        self.line = line
        self.unit = width // n_line // n_dp
        steps = jnp.arange(n_line, dtype=jnp.int32)
        owner = place_of(n_dp, dp, False)
        self.owner = owner
        self.unline = (line - steps) % n_line
        first = line * n_dp
        got = self.unline[None, :] * n_dp + owner[:, None]
        self.got_table = jnp.concatenate([got.reshape(-1), first[None]]).astype(jnp.int32)
        send_line = (line + steps) % n_line
        send = send_line[None, :] * n_dp + place_of(n_dp, dp, True)[:, None]
        self.send_table = send.reshape(-1).astype(jnp.int32)
        natural = jnp.arange(width, dtype=jnp.int32)
        arranged = (
            self.send_table[:, None] * self.unit + jnp.arange(self.unit, dtype=jnp.int32)[None, :]
        ).reshape(-1)
        self.order = (natural[:, None] == arranged[None, :]).astype(jnp.bfloat16)

    def pick(self, shard):
        size = shard.shape[0] // self.n_dp
        return lax.dynamic_slice_in_dim(shard, self.dp * size, size, 0)

    def gather(self, w_qkv, w_out, w_fc1, w_fc2, smalls):
        n_dp = self.n_dp
        n_line = self.n_line
        shard = smalls.shape[1]
        wide = w_qkv.shape[1] + w_out.shape[1]
        fold = wide // shard
        small_rows = -(-smalls.shape[0] // (16 * fold)) * 16
        padded = jnp.pad(smalls, ((0, small_rows * fold - smalls.shape[0]), (0, 0)))
        packed = jnp.concatenate(
            [padded[i * small_rows : (i + 1) * small_rows] for i in range(fold)], axis=1
        )
        unit_one = jnp.concatenate(
            [jnp.concatenate([self.pick(w_qkv), self.pick(w_out)], axis=1), packed]
        )
        unit_two, unit_three = (self.pick(w_fc1), self.pick(w_fc2))
        first = line_gather(unit_one, n_line)
        first, unit_two = lax.optimization_barrier((first, unit_two))
        second = line_gather(unit_two, n_line)
        second, unit_three = lax.optimization_barrier((second, unit_three))
        third = line_gather(unit_three, n_line)
        size = self.unit
        got_one = spread(first[None, :, :size], n_dp)
        got_two = spread(second[None], n_dp)
        got_three = spread(third[None], n_dp)
        full_qkv, full_out = assemble([w_qkv, w_out], got_one, self.got_table, n_line, size)
        (full_fc1,) = assemble([w_fc1], got_two, self.got_table, n_line, size)
        (full_fc2,) = assemble([w_fc2], got_three, self.got_table, n_line, third.shape[1])
        far = jnp.concatenate(
            [first[:, size:, i * shard : (i + 1) * shard] for i in range(fold)], axis=1
        )
        table = jnp.take(jnp.concatenate([padded[None], far]), self.unline, axis=0)
        return (table, full_qkv, full_out, full_fc1, full_fc2)

    def rows(self, block):
        return jnp.dot(block, self.order, preferred_element_type=jnp.float32).astype(jnp.bfloat16)

    def wide_columns(self, block):
        return column_order(block, self.send_table, block.shape[1] // (self.n_dp * self.n_line))

    def total(self, terms, extra=None):
        n_dp = self.n_dp
        n_line = self.n_line
        sides = []
        for side in (1, 0):
            grads = []
            for left, right in terms:
                half = left.shape[1] // 2
                grad = t_times(left[:, side * half : (side + 1) * half], right).astype(jnp.bfloat16)
                grads.append(grad.reshape(n_dp // 2, n_line, -1, right.shape[1]))
            if extra is not None:
                half = n_dp // 2
                grads.append(extra[side * half : (side + 1) * half])
            sides.append(jnp.concatenate(grads, axis=3) if len(grads) > 1 else grads[0])
        done = reduce_units(sides[0], sides[1], n_dp, n_line)
        cuts = [right.shape[1] for left, right in terms]
        if extra is not None:
            cuts.append(extra.shape[3])
        return list(finish(done, self.owner.astype(jnp.int32), cuts))

    def total_small(self, terms, smalls):
        n_dp = self.n_dp
        n_line = self.n_line
        n_small, shard = smalls.shape[1:]
        per_dp = -(-n_small // n_dp)
        size = self.unit
        columns = -(-per_dp * shard // (size * TILE)) * TILE
        units = jnp.pad(smalls, ((0, 0), (0, per_dp * n_dp - n_small), (0, 0)))
        units = units.reshape(n_line * n_dp, per_dp * shard).astype(jnp.bfloat16)
        units = jnp.pad(units, ((0, 0), (0, size * columns - per_dp * shard)))
        ids = jnp.arange(n_line * n_dp, dtype=jnp.int32)
        choose = (self.send_table[:, None] == ids[None, :]).astype(jnp.bfloat16)
        units = jnp.dot(choose, units, preferred_element_type=jnp.float32).astype(jnp.bfloat16)
        outs = self.total(terms, units.reshape(n_dp, n_line, size, columns))
        small = outs[-1].reshape(n_dp, size * columns)[:, : per_dp * shard]
        return outs[:-1] + [small.reshape(-1, shard)[:n_small]]


def per_device(
    patches,
    cotangent,
    ln1_gain,
    ln1_bias,
    w_qkv,
    w_out,
    ln2_gain,
    ln2_bias,
    w_fc1,
    fc1_bias,
    w_fc2,
    pos_table,
    pos_index,
    pos_weight,
):
    bf16 = jnp.bfloat16
    f32 = jnp.float32
    n_dp = lax.axis_size("dp")
    n_line = lax.axis_size("fsdp")
    dp = lax.axis_index("dp")
    line = lax.axis_index("fsdp")
    low_flag = dp < n_dp * 7 // 16
    rows = patches.shape[0]
    width = patches.shape[1]
    shard = width // n_line
    place, valid, segment = place_rows(rows, low_flag, pos_index, pos_weight)
    if n_line <= 4 and shard % (16 * n_dp) == 0:
        plan = Staged(n_dp, n_line, dp, line, width)
    else:
        plan = Wide(shard)
    n_bias = fc1_bias.size // shard
    smalls = jnp.concatenate(
        [
            jnp.stack([ln1_gain, ln1_bias, ln2_gain, ln2_bias]),
            fc1_bias.reshape(-1, shard),
            pos_table,
        ]
    )
    n_small = smalls.shape[0]
    table, full_qkv, full_out, full_fc1, full_fc2 = plan.gather(w_qkv, w_out, w_fc1, w_fc2, smalls)

    def across(block):
        return block.transpose(1, 0, 2).reshape(block.shape[1], width).astype(f32)

    gain_one, bias_one, gain_two, bias_two = across(table[:, :4])
    full_bias = table[:, 4 : 4 + n_bias].reshape(-1).astype(f32)
    full_table = across(table[:, 4 + n_bias : n_small])

    hidden_in = patches.astype(f32) + jnp.dot(place, full_table, precision=highest)
    normed_one = layer_norm(hidden_in, gain_one, bias_one).astype(bf16)
    projected = jnp.dot(normed_one, full_qkv, preferred_element_type=f32).astype(bf16)
    attn_rows = attend(projected, segment)
    hidden_mid = hidden_in + jnp.dot(attn_rows, full_out, preferred_element_type=f32)
    normed_two = layer_norm(hidden_mid, gain_two, bias_two).astype(bf16)
    pre_act = jnp.dot(normed_two, full_fc1, preferred_element_type=f32) + full_bias
    share = 0.5 * (1.0 + lax.erf(pre_act * 0.5**0.5))
    bell = jnp.exp(-0.5 * pre_act * pre_act) * (0.5 / jnp.pi) ** 0.5
    activated = (pre_act * share).astype(bf16)
    slope = (share + pre_act * bell).astype(bf16)
    branch_out = jnp.dot(activated, full_fc2, preferred_element_type=f32)
    block_out = jnp.where(valid[:, None], hidden_mid + branch_out, 0.0).astype(bf16)
    grad_out = jnp.where(valid[:, None], cotangent, jnp.zeros_like(cotangent))

    (sum_fc2,) = plan.total([(plan.wide_columns(activated), grad_out)])
    grad_pre = (times_t(grad_out, full_fc2) * slope.astype(f32)).astype(bf16)
    grad_fc1_bias = jnp.sum(grad_pre.astype(f32), axis=0)
    (sum_fc1,) = plan.total([(plan.rows(normed_two), grad_pre)])
    grad_norm_two = times_t(grad_pre, full_fc1)
    _, pull_two = jax.vjp(layer_norm, hidden_mid, gain_two, bias_two)
    back_mid, grad_gain_two, grad_bias_two = pull_two(grad_norm_two)
    grad_mid = grad_out.astype(f32) + back_mid
    grad_branch = grad_mid.astype(bf16)
    (sum_out,) = plan.total([(plan.rows(attn_rows), grad_branch)])
    grad_attn = times_t(grad_branch, full_out).astype(bf16)
    grad_proj = attend_back(projected, grad_attn, segment)
    grad_norm_one = times_t(grad_proj, full_qkv)
    _, pull_one = jax.vjp(layer_norm, hidden_in, gain_one, bias_one)
    back_in, grad_gain_one, grad_bias_one = pull_one(grad_norm_one)
    grad_in = grad_mid + back_in
    grad_table = jnp.dot(place.T, grad_in, precision=highest)

    def split(block):
        return block.reshape(-1, n_line, shard).transpose(1, 0, 2)

    rows_small = jnp.concatenate(
        [
            split(jnp.stack([grad_gain_one, grad_bias_one, grad_gain_two, grad_bias_two])),
            grad_fc1_bias.reshape(n_line, -1, shard),
            split(grad_table),
        ],
        axis=1,
    )
    sum_qkv, small = plan.total_small([(plan.rows(normed_one), grad_proj)], rows_small)
    return (
        block_out,
        grad_in.astype(bf16),
        small[0],
        small[1],
        sum_qkv,
        sum_out,
        small[2],
        small[3],
        sum_fc1,
        small[4 : 4 + n_bias].reshape(-1),
        sum_fc2,
        small[4 + n_bias :],
    )


def solution(mesh):
    return jax.shard_map(
        per_device,
        mesh=mesh,
        in_specs=(
            P(("dp", "fsdp"), None),
            P(("dp", "fsdp"), None),
            P("fsdp"),
            P("fsdp"),
            P("fsdp", None),
            P("fsdp", None),
            P("fsdp"),
            P("fsdp"),
            P("fsdp", None),
            P("fsdp"),
            P("fsdp", None),
            P(None, "fsdp"),
            P(),
            P(),
        ),
        out_specs=(
            P(("dp", "fsdp"), None),
            P(("dp", "fsdp"), None),
            P("fsdp"),
            P("fsdp"),
            P("fsdp", None),
            P("fsdp", None),
            P("fsdp"),
            P("fsdp"),
            P("fsdp", None),
            P("fsdp"),
            P("fsdp", None),
            P(None, "fsdp"),
        ),
        check_vma=False,
    )
```

```python
import jax
import jax.numpy as jnp
from jax import lax
from jax.experimental import pallas as pl
from jax.experimental.pallas import tpu as pltpu
from jax.sharding import PartitionSpec as P

HEADS = 16
HDIM = 64
POS = 50
HIGH_LEN = 145
TILE = 128


highest = lax.Precision.HIGHEST


def layer_norm(hidden, gain, shift):
    centre = hidden - jnp.mean(hidden, axis=-1, keepdims=True)
    spread = jnp.mean(centre * centre, axis=-1, keepdims=True)
    return centre * lax.rsqrt(spread + 1e-06) * gain + shift


def place_rows(rows, low_flag, pos_index, pos_weight):
    offsets = jnp.arange(rows, dtype=jnp.int32)
    table_ids = jnp.arange(POS, dtype=jnp.int32)
    high_ids = jnp.arange(HIGH_LEN, dtype=jnp.int32)
    picks = (pos_index[:, :, None] == table_ids[None, None, :]).astype(jnp.float32)
    interp = jnp.sum(pos_weight[:, :, None] * picks, axis=1)
    low_valid = offsets < rows // POS * POS
    high_valid = offsets < rows // HIGH_LEN * HIGH_LEN
    low_place = (((offsets % POS)[:, None] == table_ids[None, :]) & low_valid[:, None]).astype(
        jnp.float32
    )
    high_pick = (((offsets % HIGH_LEN)[:, None] == high_ids[None, :]) & high_valid[:, None]).astype(
        jnp.float32
    )
    high_place = jnp.dot(high_pick, interp, precision=highest)
    place = jnp.where(low_flag, low_place, high_place)
    valid = jnp.where(low_flag, low_valid, high_valid)
    segment = jnp.where(
        low_flag,
        jnp.where(low_valid, offsets // POS, -1),
        jnp.where(high_valid, offsets // HIGH_LEN, -1),
    )
    return (place, valid, segment)


def key_windows(rows):
    out = []
    for start in range(0, rows, TILE):
        least, most = rows, 0
        for size in (POS, HIGH_LEN):
            used = rows // size * size
            for row in (start, start + TILE - 1):
                image = row // size
                begin = image * size if row < used else used
                end = begin + size if row < used else rows
                least, most = min(least, begin), max(most, end)
        out.append((start, least // TILE * TILE, -(-most // TILE) * TILE))
    return out


def times_t(left, right):
    return lax.dot_general(left, right, (((1,), (1,)), ((), ())), preferred_element_type=jnp.float32)


def t_times(left, right):
    return lax.dot_general(left, right, (((0,), (0,)), ((), ())), preferred_element_type=jnp.float32)


def halves(block, scale=None):
    lane = lax.broadcasted_iota(jnp.int32, block.shape, 1)
    if scale is not None:
        block = block * jnp.asarray(scale, block.dtype)
    zero = jnp.zeros_like(block)
    return (jnp.where(lane < HDIM, block, zero), jnp.where(lane < HDIM, zero, block))


def soft(query, keys, same):
    scores = jnp.where(same, times_t(query, keys), -1e30)
    expo = jnp.exp(scores - jnp.max(scores, axis=-1, keepdims=True))
    return expo * (1.0 / jnp.sum(expo, axis=-1, keepdims=True))


def attend_body(windows, col_ref, row_ref, q_ref, k_ref, v_ref, out_ref):
    values = halves(v_ref[...])
    for start, lo, hi in windows:
        rows = slice(start, start + TILE)
        same = col_ref[rows, :] == row_ref[:, lo:hi]
        keys = k_ref[lo:hi, :]
        total = None
        for query, value in zip(halves(q_ref[rows, :], HDIM ** (-0.5)), values):
            probs = soft(query, keys, same).astype(jnp.bfloat16)
            part = jnp.dot(probs, value[lo:hi], preferred_element_type=jnp.float32)
            total = part if total is None else total + part
        out_ref[rows, :] = total.astype(jnp.bfloat16)


def attend_back_body(windows, col_ref, row_ref, q_ref, k_ref, v_ref, g_ref, out_ref, dk_ref, dv_ref):
    width = q_ref.shape[1]
    full = out_ref.shape[1] // 3
    at = pl.program_id(0) * width
    dk_ref[...] = jnp.zeros_like(dk_ref)
    dv_ref[...] = jnp.zeros_like(dv_ref)
    scaled = halves(k_ref[...], HDIM ** (-0.5))
    for start, lo, hi in windows:
        rows = slice(start, start + TILE)
        same = col_ref[rows, :] == row_ref[:, lo:hi]
        keys = k_ref[lo:hi, :]
        values = v_ref[lo:hi, :]
        total = None
        queries = halves(q_ref[rows, :], HDIM ** (-0.5))
        grads = halves(g_ref[rows, :])
        for query, grad, key in zip(queries, grads, scaled):
            probs = soft(query, keys, same)
            grad_probs = times_t(grad, values)
            centre = jnp.sum(probs * grad_probs, axis=-1, keepdims=True)
            grad_scores = (probs * (grad_probs - centre)).astype(jnp.bfloat16)
            part = jnp.dot(grad_scores, key[lo:hi], preferred_element_type=jnp.float32)
            total = part if total is None else total + part
            dk_ref[lo:hi, :] += t_times(grad_scores, query)
            dv_ref[lo:hi, :] += t_times(probs.astype(jnp.bfloat16), grad)
        out_ref[rows, pl.ds(pl.multiple_of(at, width), width)] = total.astype(jnp.bfloat16)
    out_ref[:, pl.ds(pl.multiple_of(full + at, width), width)] = dk_ref[...].astype(jnp.bfloat16)
    out_ref[:, pl.ds(pl.multiple_of(2 * full + at, width), width)] = dv_ref[...].astype(jnp.bfloat16)


def pair_specs(rows, pairs):
    pair = 2 * HDIM
    whole = [
        pl.BlockSpec((rows, 1), lambda i: (0, 0)),
        pl.BlockSpec((1, rows), lambda i: (0, 0)),
    ]
    return whole + [
        pl.BlockSpec((rows, pair), lambda i, j=j: (0, j * pairs + i)) for j in range(3)
    ]


def attend(projected, segment):
    rows = projected.shape[0]
    pairs = HEADS // 2
    windows = key_windows(rows)

    def body(*refs):
        attend_body(windows, *refs)

    return pl.pallas_call(
        body,
        grid=(pairs,),
        in_specs=pair_specs(rows, pairs),
        out_specs=pl.BlockSpec((rows, 2 * HDIM), lambda i: (0, i)),
        out_shape=jax.ShapeDtypeStruct((rows, HEADS * HDIM), jnp.bfloat16),
        name="attend",
    )(segment[:, None], segment[None, :], projected, projected, projected)


def attend_back(projected, grad_attn, segment):
    rows = projected.shape[0]
    pairs = HEADS // 2
    windows = key_windows(rows)

    def body(*refs):
        attend_back_body(windows, *refs)

    return pl.pallas_call(
        body,
        grid=(pairs,),
        in_specs=pair_specs(rows, pairs) + [pl.BlockSpec((rows, 2 * HDIM), lambda i: (0, i))],
        out_specs=pl.BlockSpec((rows, 3 * HEADS * HDIM), lambda i: (0, 0)),
        out_shape=jax.ShapeDtypeStruct((rows, 3 * HEADS * HDIM), jnp.bfloat16),
        scratch_shapes=[pltpu.VMEM((rows, 2 * HDIM), jnp.float32)] * 2,
        name="attend_back",
    )(segment[:, None], segment[None, :], projected, projected, projected, grad_attn)


def copies(pairs_of, sems):
    moves = [
        pltpu.make_async_copy(source, target, sems.at[i])
        for i, (source, target) in enumerate(pairs_of)
    ]
    for move in moves:
        move.start()
    for move in moves:
        move.wait()


def assemble(owns, parts, table, n_line, unit):
    n_places = sum(part.shape[0] for part in parts)
    n_own = len(owns)
    n_parts = len(parts)
    ends = []
    for own in owns:
        ends.append((ends[-1] if ends else 0) + own.shape[1])
    count = n_own * (1 + n_places * (n_line - 1))

    def body(table_ref, *refs):
        own_refs = refs[:n_own]
        part_refs = refs[n_own : n_own + n_parts]
        out_refs = refs[n_own + n_parts : 2 * n_own + n_parts]
        sems = refs[-1]
        todo = []
        for own_ref, out_ref, end in zip(own_refs, out_refs, ends):
            shard_rows = own_ref.shape[0]
            columns = pl.ds(end - own_ref.shape[1], own_ref.shape[1])
            first = pl.multiple_of(table_ref[n_places * n_line] * unit, unit)
            todo.append((own_ref, out_ref.at[pl.ds(first, shard_rows), :]))
            place = 0
            for part_ref in part_refs:
                for k in range(part_ref.shape[0]):
                    for step in range(1, n_line):
                        row = pl.multiple_of(table_ref[place * n_line + step] * unit, unit)
                        todo.append(
                            (
                                part_ref.at[k, step - 1, pl.ds(0, unit), columns],
                                out_ref.at[pl.ds(row, unit), :],
                            )
                        )
                    place += 1
        copies(todo, sems)

    anywhere = pl.BlockSpec(memory_space=pl.ANY)
    return pl.pallas_call(
        body,
        in_specs=[pl.BlockSpec(memory_space=pltpu.SMEM)] + [anywhere] * (n_own + n_parts),
        out_specs=[pl.BlockSpec(memory_space=pltpu.VMEM)] * n_own,
        out_shape=[
            jax.ShapeDtypeStruct((own.shape[0] * n_line, own.shape[1]), own.dtype) for own in owns
        ],
        scratch_shapes=[pltpu.SemaphoreType.DMA((count,))],
        name="assemble",
    )(table, *owns, *parts)


def column_order(block, table, unit):
    count = block.shape[1] // unit

    def body(table_ref, in_ref, out_ref):
        for i in range(count):
            column = pl.multiple_of(table_ref[i] * unit, unit)
            out_ref[:, i * unit : (i + 1) * unit] = in_ref[:, pl.ds(column, unit)]

    return pl.pallas_call(
        body,
        in_specs=[
            pl.BlockSpec(memory_space=pltpu.SMEM),
            pl.BlockSpec(memory_space=pltpu.VMEM),
        ],
        out_specs=pl.BlockSpec(memory_space=pltpu.VMEM),
        out_shape=jax.ShapeDtypeStruct(block.shape, block.dtype),
        name="column_order",
    )(table, block)


def finish(parts, owner, cuts):
    unit = parts[0].shape[1]
    n_places = sum(part.shape[0] for part in parts)

    def body(owner_ref, *refs):
        part_refs = refs[: len(parts)]
        out_refs = refs[len(parts) :]
        place = 0
        for part_ref in part_refs:
            for k in range(part_ref.shape[0]):
                row = pl.multiple_of(owner_ref[place] * unit, unit)
                at = 0
                for out_ref, cut in zip(out_refs, cuts):
                    out_ref[pl.ds(row, unit), :] = part_ref[k, :, at : at + cut].astype(jnp.float32)
                    at += cut
                place += 1

    return pl.pallas_call(
        body,
        in_specs=[pl.BlockSpec(memory_space=pltpu.SMEM)]
        + [pl.BlockSpec(memory_space=pltpu.VMEM)] * len(parts),
        out_specs=[pl.BlockSpec(memory_space=pltpu.VMEM)] * len(cuts),
        out_shape=[jax.ShapeDtypeStruct((n_places * unit, cut), jnp.float32) for cut in cuts],
        name="finish",
    )(owner, *parts)


def hop_bit(core, stage, bits):
    return 1 + stage if core == 0 else bits - stage


def hop_pairs(n_dp, stage):
    bits = n_dp.bit_length() - 2
    return [(i, i ^ (1 << hop_bit(i % 2, stage, bits))) for i in range(n_dp)]


def swap_core(block, n_dp):
    return lax.ppermute(block, "dp", [(i, i ^ 1) for i in range(n_dp)])


def ahead(block, n_line, step):
    return lax.ppermute(block, "fsdp", [(i, (i + step) % n_line) for i in range(n_line)])


def line_gather(unit, n_line):
    return jnp.stack([ahead(unit, n_line, step) for step in range(1, n_line)])


def spread(part, n_dp):
    parts = [part]
    for stage in range(n_dp.bit_length() - 2):
        parts = parts + [lax.ppermute(item, "dp", hop_pairs(n_dp, stage)) for item in parts]
    return parts + [swap_core(item, n_dp) for item in parts]


def add_up(terms):
    total = terms[0].astype(jnp.float32)
    for term in terms[1:]:
        total = total + term.astype(jnp.float32)
    return total


def reduce_steps(away, keep, n_dp, n_line):
    (away,) = yield [away]
    (got,) = yield [swap_core(away, n_dp)]
    terms = [keep, got]
    half = keep.shape[0] // 2
    for stage in range(n_dp.bit_length() - 2):
        (send,) = yield [add_up([term[half:] for term in terms]).astype(jnp.bfloat16)]
        (got,) = yield [lax.ppermute(send, "dp", hop_pairs(n_dp, stage))]
        terms = [term[:half] for term in terms] + [got]
        half //= 2
    terms = [term[0] for term in terms]
    sends = yield [
        add_up([term[step] for term in terms]).astype(jnp.bfloat16) for step in range(1, n_line)
    ]
    arrived = yield [ahead(send, n_line, step + 1) for step, send in enumerate(sends)]
    parts = [add_up([term[0] for term in terms] + arrived).astype(jnp.bfloat16)[None]]
    for stage in range(n_dp.bit_length() - 2):
        parts = yield parts
        parts = parts + (yield [lax.ppermute(item, "dp", hop_pairs(n_dp, stage)) for item in parts])
    parts = yield parts
    return parts + (yield [swap_core(item, n_dp) for item in parts])


class Reduction:
    def __init__(self, steps, close):
        self.steps = steps
        self.close = close
        self.parts = None
        self.held = None
        self.begin = next(steps)

    def take(self, got):
        try:
            return self.steps.send(got)
        except StopIteration as stop:
            self.parts = stop.value
            return []

    def result(self):
        if self.held is None:
            self.held = self.steps.send(self.begin)
        while self.parts is None:
            sends = self.take(self.held)
            if self.parts is None:
                self.held = self.steps.send(sends)
        return self.close(self.parts)


class Ready:
    def __init__(self, outs):
        self.outs = outs

    def result(self):
        return self.outs


def tick(value, running):
    running = [item for item in running if isinstance(item, Reduction) and item.parts is None]
    old = [item for item in running if item.held is not None]
    value, gots = lax.optimization_barrier((value, [item.held for item in old]))
    sends = [item.take(got) for item, got in zip(old, gots)]
    new = [item for item in running if item.held is None]
    sends = sends + [item.begin for item in new]
    value, sends = lax.optimization_barrier((value, sends))
    for item, send in zip(old + new, sends):
        if item.parts is None:
            item.held = item.steps.send(send)
    return value


def place_of(n_dp, me, flip):
    bits = n_dp.bit_length() - 2
    core = me % 2
    halves = []
    for other in range(2):
        place = jnp.arange(1 << bits, dtype=jnp.int32)
        owner = jnp.full((1 << bits,), me ^ other, jnp.int32)
        for stage in range(bits):
            at = bits - 1 - stage if flip else stage
            low = 1 << hop_bit(0, stage, bits)
            high = 1 << hop_bit(1, stage, bits)
            mask = jnp.where((core ^ other) == 0, low, high)
            owner = owner ^ (((place >> at) & 1) * mask)
        halves.append(owner)
    return jnp.concatenate(halves)


class Wide:
    def __init__(self, shard):
        self.shard = shard

    def gather(self, w_qkv, w_out, w_fc1, w_fc2, smalls):
        def full(matrix):
            return lax.all_gather(matrix, "fsdp", axis=0, tiled=True)

        table = lax.all_gather(smalls, "fsdp", axis=0)
        return (table, full(w_qkv), full(w_out), full(w_fc1), full(w_fc2))

    def rows(self, block):
        return block

    def wide_columns(self, block):
        return block

    def total(self, terms):
        bf16 = jnp.bfloat16
        outs = []
        for left, right in terms:
            grad = t_times(left, right).astype(bf16)
            own = lax.psum_scatter(grad, "fsdp", scatter_dimension=0, tiled=True)
            outs.append(lax.psum(own, "dp").astype(jnp.float32))
        return Ready(outs)

    def total_small(self, smalls):
        own = lax.psum_scatter(
            smalls.astype(jnp.bfloat16), "fsdp", scatter_dimension=0, tiled=False
        )
        return Ready(lax.psum(own, "dp").astype(jnp.float32))


class Staged:
    def __init__(self, n_dp, n_line, dp, line, width):
        self.n_dp = n_dp
        self.n_line = n_line
        self.dp = dp
        self.line = line
        self.unit = width // n_line // n_dp
        steps = jnp.arange(n_line, dtype=jnp.int32)
        owner = place_of(n_dp, dp, False)
        self.owner = owner
        self.unline = (line - steps) % n_line
        first = line * n_dp
        got = self.unline[None, :] * n_dp + owner[:, None]
        self.got_table = jnp.concatenate([got.reshape(-1), first[None]]).astype(jnp.int32)
        send_line = (line + steps) % n_line
        send = send_line[None, :] * n_dp + place_of(n_dp, dp, True)[:, None]
        self.send_table = send.reshape(-1).astype(jnp.int32)
        natural = jnp.arange(width, dtype=jnp.int32)
        arranged = (
            self.send_table[:, None] * self.unit + jnp.arange(self.unit, dtype=jnp.int32)[None, :]
        ).reshape(-1)
        self.order = (natural[:, None] == arranged[None, :]).astype(jnp.bfloat16)

    def pick(self, shard):
        size = shard.shape[0] // self.n_dp
        return lax.dynamic_slice_in_dim(shard, self.dp * size, size, 0)

    def gather(self, w_qkv, w_out, w_fc1, w_fc2, smalls):
        n_dp = self.n_dp
        n_line = self.n_line
        shard = smalls.shape[1]
        wide = w_qkv.shape[1] + w_out.shape[1]
        fold = wide // shard
        small_rows = -(-smalls.shape[0] // (16 * fold)) * 16
        padded = jnp.pad(smalls, ((0, small_rows * fold - smalls.shape[0]), (0, 0)))
        packed = jnp.concatenate(
            [padded[i * small_rows : (i + 1) * small_rows] for i in range(fold)], axis=1
        )
        unit_one = jnp.concatenate(
            [jnp.concatenate([self.pick(w_qkv), self.pick(w_out)], axis=1), packed]
        )
        unit_two, unit_three = (self.pick(w_fc1), self.pick(w_fc2))
        first = line_gather(unit_one, n_line)
        first, unit_two = lax.optimization_barrier((first, unit_two))
        second = line_gather(unit_two, n_line)
        second, unit_three = lax.optimization_barrier((second, unit_three))
        third = line_gather(unit_three, n_line)
        size = self.unit
        got_one = spread(first[None, :, :size], n_dp)
        got_two = spread(second[None], n_dp)
        got_three = spread(third[None], n_dp)
        full_qkv, full_out = assemble([w_qkv, w_out], got_one, self.got_table, n_line, size)
        (full_fc1,) = assemble([w_fc1], got_two, self.got_table, n_line, size)
        (full_fc2,) = assemble([w_fc2], got_three, self.got_table, n_line, third.shape[1])
        far = jnp.concatenate(
            [first[:, size:, i * shard : (i + 1) * shard] for i in range(fold)], axis=1
        )
        table = jnp.take(jnp.concatenate([padded[None], far]), self.unline, axis=0)
        return (table, full_qkv, full_out, full_fc1, full_fc2)

    def rows(self, block):
        return jnp.dot(block, self.order, preferred_element_type=jnp.float32).astype(jnp.bfloat16)

    def wide_columns(self, block):
        return column_order(block, self.send_table, block.shape[1] // (self.n_dp * self.n_line))

    def total(self, terms):
        n_dp = self.n_dp
        n_line = self.n_line
        sides = []
        for side in (1, 0):
            grads = []
            for left, right in terms:
                half = left.shape[1] // 2
                grad = t_times(left[:, side * half : (side + 1) * half], right).astype(jnp.bfloat16)
                grads.append(grad.reshape(n_dp // 2, n_line, -1, right.shape[1]))
            sides.append(jnp.concatenate(grads, axis=3) if len(grads) > 1 else grads[0])
        cuts = [right.shape[1] for left, right in terms]
        owner = self.owner.astype(jnp.int32)
        steps = reduce_steps(sides[0], sides[1], n_dp, n_line)
        return Reduction(steps, lambda parts: list(finish(parts, owner, cuts)))

    def total_small(self, smalls):
        n_dp = self.n_dp
        n_line = self.n_line
        n_small, shard = smalls.shape[1:]
        per_dp = -(-n_small // n_dp)
        units = jnp.pad(smalls, ((0, 0), (0, per_dp * n_dp - n_small), (0, 0)))
        units = units.reshape(n_line * n_dp, per_dp * shard).astype(jnp.bfloat16)
        size = -(-per_dp * shard // (16 * TILE)) * 16
        units = jnp.pad(units, ((0, 0), (0, size * TILE - per_dp * shard)))
        ids = jnp.arange(n_line * n_dp, dtype=jnp.int32)
        choose = (self.send_table[:, None] == ids[None, :]).astype(jnp.bfloat16)
        units = jnp.dot(choose, units, preferred_element_type=jnp.float32).astype(jnp.bfloat16)
        units = units.reshape(n_dp, n_line, size, TILE)
        owner = self.owner.astype(jnp.int32)

        def close(parts):
            (small,) = finish(parts, owner, [TILE])
            small = small.reshape(n_dp, size * TILE)[:, : per_dp * shard]
            return small.reshape(-1, shard)[:n_small]

        half = n_dp // 2
        return Reduction(reduce_steps(units[half:], units[:half], n_dp, n_line), close)


def per_device(
    patches,
    cotangent,
    ln1_gain,
    ln1_bias,
    w_qkv,
    w_out,
    ln2_gain,
    ln2_bias,
    w_fc1,
    fc1_bias,
    w_fc2,
    pos_table,
    pos_index,
    pos_weight,
):
    bf16 = jnp.bfloat16
    f32 = jnp.float32
    n_dp = lax.axis_size("dp")
    n_line = lax.axis_size("fsdp")
    dp = lax.axis_index("dp")
    line = lax.axis_index("fsdp")
    low_flag = dp < n_dp * 7 // 16
    rows = patches.shape[0]
    width = patches.shape[1]
    shard = width // n_line
    place, valid, segment = place_rows(rows, low_flag, pos_index, pos_weight)
    if n_line <= 4 and shard % (16 * n_dp) == 0:
        plan = Staged(n_dp, n_line, dp, line, width)
    else:
        plan = Wide(shard)
    n_bias = fc1_bias.size // shard
    smalls = jnp.concatenate(
        [
            jnp.stack([ln1_gain, ln1_bias, ln2_gain, ln2_bias]),
            fc1_bias.reshape(-1, shard),
            pos_table,
        ]
    )
    n_small = smalls.shape[0]
    table, full_qkv, full_out, full_fc1, full_fc2 = plan.gather(w_qkv, w_out, w_fc1, w_fc2, smalls)

    def across(block):
        return block.transpose(1, 0, 2).reshape(block.shape[1], width).astype(f32)

    gain_one, bias_one, gain_two, bias_two = across(table[:, :4])
    full_bias = table[:, 4 : 4 + n_bias].reshape(-1).astype(f32)
    full_table = across(table[:, 4 + n_bias : n_small])

    hidden_in = patches.astype(f32) + jnp.dot(place, full_table, precision=highest)
    normed_one = layer_norm(hidden_in, gain_one, bias_one).astype(bf16)
    projected = jnp.dot(normed_one, full_qkv, preferred_element_type=f32).astype(bf16)
    attn_rows = attend(projected, segment)
    hidden_mid = hidden_in + jnp.dot(attn_rows, full_out, preferred_element_type=f32)
    normed_two = layer_norm(hidden_mid, gain_two, bias_two).astype(bf16)
    pre_act = jnp.dot(normed_two, full_fc1, preferred_element_type=f32) + full_bias
    share = 0.5 * (1.0 + lax.erf(pre_act * 0.5**0.5))
    bell = jnp.exp(-0.5 * pre_act * pre_act) * (0.5 / jnp.pi) ** 0.5
    activated = (pre_act * share).astype(bf16)
    slope = (share + pre_act * bell).astype(bf16)
    branch_out = jnp.dot(activated, full_fc2, preferred_element_type=f32)
    block_out = jnp.where(valid[:, None], hidden_mid + branch_out, 0.0).astype(bf16)
    grad_out = jnp.where(valid[:, None], cotangent, jnp.zeros_like(cotangent))

    run_fc2 = plan.total([(plan.wide_columns(activated), grad_out)])
    grad_out = tick(grad_out, [run_fc2])
    grad_pre = (times_t(grad_out, full_fc2) * slope.astype(f32)).astype(bf16)
    grad_fc1_bias = jnp.sum(grad_pre.astype(f32), axis=0)
    run_fc1 = plan.total([(plan.rows(normed_two), grad_pre)])
    grad_pre = tick(grad_pre, [run_fc2, run_fc1])
    grad_norm_two = times_t(grad_pre, full_fc1)
    _, pull_two = jax.vjp(layer_norm, hidden_mid, gain_two, bias_two)
    back_mid, grad_gain_two, grad_bias_two = pull_two(grad_norm_two)
    grad_mid = grad_out.astype(f32) + back_mid
    grad_branch = tick(grad_mid.astype(bf16), [run_fc2, run_fc1])
    run_out = plan.total([(plan.rows(attn_rows), grad_branch)])
    grad_attn = times_t(grad_branch, full_out).astype(bf16)
    grad_attn = tick(grad_attn, [run_fc2, run_fc1, run_out])
    grad_proj = attend_back(projected, grad_attn, segment)
    run_qkv = plan.total([(plan.rows(normed_one), grad_proj)])
    grad_proj = tick(grad_proj, [run_fc2, run_fc1, run_out, run_qkv])
    grad_norm_one = times_t(grad_proj, full_qkv)
    _, pull_one = jax.vjp(layer_norm, hidden_in, gain_one, bias_one)
    back_in, grad_gain_one, grad_bias_one = pull_one(grad_norm_one)
    grad_in = tick(grad_mid + back_in, [run_fc2, run_fc1, run_out, run_qkv])
    grad_table = jnp.dot(place.T, grad_in, precision=highest)

    def split(block):
        return block.reshape(-1, n_line, shard).transpose(1, 0, 2)

    rows_small = jnp.concatenate(
        [
            split(jnp.stack([grad_gain_one, grad_bias_one, grad_gain_two, grad_bias_two])),
            grad_fc1_bias.reshape(n_line, -1, shard),
            split(grad_table),
        ],
        axis=1,
    )
    run_small = plan.total_small(rows_small)
    (sum_fc2,) = run_fc2.result()
    (sum_fc1,) = run_fc1.result()
    (sum_out,) = run_out.result()
    (sum_qkv,) = run_qkv.result()
    small = run_small.result()
    return (
        block_out,
        grad_in.astype(bf16),
        small[0],
        small[1],
        sum_qkv,
        sum_out,
        small[2],
        small[3],
        sum_fc1,
        small[4 : 4 + n_bias].reshape(-1),
        sum_fc2,
        small[4 + n_bias :],
    )


def solution(mesh):
    return jax.shard_map(
        per_device,
        mesh=mesh,
        in_specs=(
            P(("dp", "fsdp"), None),
            P(("dp", "fsdp"), None),
            P("fsdp"),
            P("fsdp"),
            P("fsdp", None),
            P("fsdp", None),
            P("fsdp"),
            P("fsdp"),
            P("fsdp", None),
            P("fsdp"),
            P("fsdp", None),
            P(None, "fsdp"),
            P(),
            P(),
        ),
        out_specs=(
            P(("dp", "fsdp"), None),
            P(("dp", "fsdp"), None),
            P("fsdp"),
            P("fsdp"),
            P("fsdp", None),
            P("fsdp", None),
            P("fsdp"),
            P("fsdp"),
            P("fsdp", None),
            P("fsdp"),
            P("fsdp", None),
            P(None, "fsdp"),
        ),
        check_vma=False,
    )
```

```python
import jax
import jax.numpy as jnp
from jax import lax
from jax.experimental import pallas as pl
from jax.experimental.pallas import tpu as pltpu
from jax.sharding import PartitionSpec as P

HEADS = 16
HDIM = 64
POS = 50
HIGH_LEN = 145
TILE = 128


highest = lax.Precision.HIGHEST


def layer_norm(hidden, gain, shift):
    centre = hidden - jnp.mean(hidden, axis=-1, keepdims=True)
    spread = jnp.mean(centre * centre, axis=-1, keepdims=True)
    return centre * lax.rsqrt(spread + 1e-06) * gain + shift


def place_rows(rows, low_flag, pos_index, pos_weight):
    offsets = jnp.arange(rows, dtype=jnp.int32)
    table_ids = jnp.arange(POS, dtype=jnp.int32)
    high_ids = jnp.arange(HIGH_LEN, dtype=jnp.int32)
    picks = (pos_index[:, :, None] == table_ids[None, None, :]).astype(jnp.float32)
    interp = jnp.sum(pos_weight[:, :, None] * picks, axis=1)
    low_valid = offsets < rows // POS * POS
    high_valid = offsets < rows // HIGH_LEN * HIGH_LEN
    low_place = (((offsets % POS)[:, None] == table_ids[None, :]) & low_valid[:, None]).astype(
        jnp.float32
    )
    high_pick = (((offsets % HIGH_LEN)[:, None] == high_ids[None, :]) & high_valid[:, None]).astype(
        jnp.float32
    )
    high_place = jnp.dot(high_pick, interp, precision=highest)
    place = jnp.where(low_flag, low_place, high_place)
    valid = jnp.where(low_flag, low_valid, high_valid)
    segment = jnp.where(
        low_flag,
        jnp.where(low_valid, offsets // POS, -1),
        jnp.where(high_valid, offsets // HIGH_LEN, -1),
    )
    return (place, valid, segment)


def key_windows(rows):
    out = []
    for start in range(0, rows, TILE):
        least, most = rows, 0
        for size in (POS, HIGH_LEN):
            used = rows // size * size
            for row in (start, start + TILE - 1):
                image = row // size
                begin = image * size if row < used else used
                end = begin + size if row < used else rows
                least, most = min(least, begin), max(most, end)
        out.append((start, least // TILE * TILE, -(-most // TILE) * TILE))
    return out


def times_t(left, right):
    return lax.dot_general(left, right, (((1,), (1,)), ((), ())), preferred_element_type=jnp.float32)


def t_times(left, right):
    return lax.dot_general(left, right, (((0,), (0,)), ((), ())), preferred_element_type=jnp.float32)


def halves(block, scale=None):
    lane = lax.broadcasted_iota(jnp.int32, block.shape, 1)
    if scale is not None:
        block = block * jnp.asarray(scale, block.dtype)
    zero = jnp.zeros_like(block)
    return (jnp.where(lane < HDIM, block, zero), jnp.where(lane < HDIM, zero, block))


def soft(query, keys, same):
    scores = jnp.where(same, times_t(query, keys), -1e30)
    expo = jnp.exp(scores - jnp.max(scores, axis=-1, keepdims=True))
    return expo * (1.0 / jnp.sum(expo, axis=-1, keepdims=True))


def attend_body(windows, col_ref, row_ref, q_ref, k_ref, v_ref, out_ref):
    values = halves(v_ref[...])
    for start, lo, hi in windows:
        rows = slice(start, start + TILE)
        same = col_ref[rows, :] == row_ref[:, lo:hi]
        keys = k_ref[lo:hi, :]
        total = None
        for query, value in zip(halves(q_ref[rows, :], HDIM ** (-0.5)), values):
            probs = soft(query, keys, same).astype(jnp.bfloat16)
            part = jnp.dot(probs, value[lo:hi], preferred_element_type=jnp.float32)
            total = part if total is None else total + part
        out_ref[rows, :] = total.astype(jnp.bfloat16)


def attend_back_body(windows, col_ref, row_ref, q_ref, k_ref, v_ref, g_ref, out_ref, dk_ref, dv_ref):
    width = q_ref.shape[1]
    full = out_ref.shape[1] // 3
    at = pl.program_id(0) * width
    dk_ref[...] = jnp.zeros_like(dk_ref)
    dv_ref[...] = jnp.zeros_like(dv_ref)
    scaled = halves(k_ref[...], HDIM ** (-0.5))
    for start, lo, hi in windows:
        rows = slice(start, start + TILE)
        same = col_ref[rows, :] == row_ref[:, lo:hi]
        keys = k_ref[lo:hi, :]
        values = v_ref[lo:hi, :]
        total = None
        queries = halves(q_ref[rows, :], HDIM ** (-0.5))
        grads = halves(g_ref[rows, :])
        for query, grad, key in zip(queries, grads, scaled):
            probs = soft(query, keys, same)
            grad_probs = times_t(grad, values)
            centre = jnp.sum(probs * grad_probs, axis=-1, keepdims=True)
            grad_scores = (probs * (grad_probs - centre)).astype(jnp.bfloat16)
            part = jnp.dot(grad_scores, key[lo:hi], preferred_element_type=jnp.float32)
            total = part if total is None else total + part
            dk_ref[lo:hi, :] += t_times(grad_scores, query)
            dv_ref[lo:hi, :] += t_times(probs.astype(jnp.bfloat16), grad)
        out_ref[rows, pl.ds(pl.multiple_of(at, width), width)] = total.astype(jnp.bfloat16)
    out_ref[:, pl.ds(pl.multiple_of(full + at, width), width)] = dk_ref[...].astype(jnp.bfloat16)
    out_ref[:, pl.ds(pl.multiple_of(2 * full + at, width), width)] = dv_ref[...].astype(jnp.bfloat16)


def pair_specs(rows, pairs, start=0):
    pair = 2 * HDIM
    whole = [
        pl.BlockSpec((rows, 1), lambda i: (0, 0)),
        pl.BlockSpec((1, rows), lambda i: (0, 0)),
    ]
    return whole + [
        pl.BlockSpec((rows, pair), lambda i, j=j: (0, j * pairs + start + i)) for j in range(3)
    ]


def attend(projected, segment):
    rows = projected.shape[0]
    pairs = HEADS // 2
    windows = key_windows(rows)

    def body(*refs):
        attend_body(windows, *refs)

    return pl.pallas_call(
        body,
        grid=(pairs,),
        in_specs=pair_specs(rows, pairs),
        out_specs=pl.BlockSpec((rows, 2 * HDIM), lambda i: (0, i)),
        out_shape=jax.ShapeDtypeStruct((rows, HEADS * HDIM), jnp.bfloat16),
        name="attend",
    )(segment[:, None], segment[None, :], projected, projected, projected)


def attend_back(projected, grad_attn, segment, start, count):
    rows = projected.shape[0]
    pairs = HEADS // 2
    windows = key_windows(rows)
    wide = 3 * count * 2 * HDIM

    def body(*refs):
        attend_back_body(windows, *refs)

    return pl.pallas_call(
        body,
        grid=(count,),
        in_specs=pair_specs(rows, pairs, start)
        + [pl.BlockSpec((rows, 2 * HDIM), lambda i: (0, start + i))],
        out_specs=pl.BlockSpec((rows, wide), lambda i: (0, 0)),
        out_shape=jax.ShapeDtypeStruct((rows, wide), jnp.bfloat16),
        scratch_shapes=[pltpu.VMEM((rows, 2 * HDIM), jnp.float32)] * 2,
        name="attend_back",
    )(segment[:, None], segment[None, :], projected, projected, projected, grad_attn)


def copies(pairs_of, sems):
    moves = [
        pltpu.make_async_copy(source, target, sems.at[i])
        for i, (source, target) in enumerate(pairs_of)
    ]
    for move in moves:
        move.start()
    for move in moves:
        move.wait()


def assemble(owns, parts, table, n_line, unit):
    n_places = sum(part.shape[0] for part in parts)
    n_own = len(owns)
    n_parts = len(parts)
    ends = []
    for own in owns:
        ends.append((ends[-1] if ends else 0) + own.shape[1])
    count = n_own * (1 + n_places * (n_line - 1))

    def body(table_ref, *refs):
        own_refs = refs[:n_own]
        part_refs = refs[n_own : n_own + n_parts]
        out_refs = refs[n_own + n_parts : 2 * n_own + n_parts]
        sems = refs[-1]
        todo = []
        for own_ref, out_ref, end in zip(own_refs, out_refs, ends):
            shard_rows = own_ref.shape[0]
            columns = pl.ds(end - own_ref.shape[1], own_ref.shape[1])
            first = pl.multiple_of(table_ref[n_places * n_line] * unit, unit)
            todo.append((own_ref, out_ref.at[pl.ds(first, shard_rows), :]))
            place = 0
            for part_ref in part_refs:
                for k in range(part_ref.shape[0]):
                    for step in range(1, n_line):
                        row = pl.multiple_of(table_ref[place * n_line + step] * unit, unit)
                        todo.append(
                            (
                                part_ref.at[k, step - 1, pl.ds(0, unit), columns],
                                out_ref.at[pl.ds(row, unit), :],
                            )
                        )
                    place += 1
        copies(todo, sems)

    anywhere = pl.BlockSpec(memory_space=pl.ANY)
    return pl.pallas_call(
        body,
        in_specs=[pl.BlockSpec(memory_space=pltpu.SMEM)] + [anywhere] * (n_own + n_parts),
        out_specs=[pl.BlockSpec(memory_space=pltpu.VMEM)] * n_own,
        out_shape=[
            jax.ShapeDtypeStruct((own.shape[0] * n_line, own.shape[1]), own.dtype) for own in owns
        ],
        scratch_shapes=[pltpu.SemaphoreType.DMA((count,))],
        name="assemble",
    )(table, *owns, *parts)


def column_order(block, table, unit):
    count = block.shape[1] // unit

    def body(table_ref, in_ref, out_ref):
        for i in range(count):
            column = pl.multiple_of(table_ref[i] * unit, unit)
            out_ref[:, i * unit : (i + 1) * unit] = in_ref[:, pl.ds(column, unit)]

    return pl.pallas_call(
        body,
        in_specs=[
            pl.BlockSpec(memory_space=pltpu.SMEM),
            pl.BlockSpec(memory_space=pltpu.VMEM),
        ],
        out_specs=pl.BlockSpec(memory_space=pltpu.VMEM),
        out_shape=jax.ShapeDtypeStruct(block.shape, block.dtype),
        name="column_order",
    )(table, block)


def finish(parts, owner, cuts):
    unit = parts[0].shape[1]
    n_places = sum(part.shape[0] for part in parts)

    def body(owner_ref, *refs):
        part_refs = refs[: len(parts)]
        out_refs = refs[len(parts) :]
        place = 0
        for part_ref in part_refs:
            for k in range(part_ref.shape[0]):
                row = pl.multiple_of(owner_ref[place] * unit, unit)
                at = 0
                for out_ref, cut in zip(out_refs, cuts):
                    out_ref[pl.ds(row, unit), :] = part_ref[k, :, at : at + cut].astype(jnp.float32)
                    at += cut
                place += 1

    return pl.pallas_call(
        body,
        in_specs=[pl.BlockSpec(memory_space=pltpu.SMEM)]
        + [pl.BlockSpec(memory_space=pltpu.VMEM)] * len(parts),
        out_specs=[pl.BlockSpec(memory_space=pltpu.VMEM)] * len(cuts),
        out_shape=[jax.ShapeDtypeStruct((n_places * unit, cut), jnp.float32) for cut in cuts],
        name="finish",
    )(owner, *parts)


def hop_bit(core, stage, bits):
    return 1 + stage if core == 0 else bits - stage


def hop_pairs(n_dp, stage):
    bits = n_dp.bit_length() - 2
    return [(i, i ^ (1 << hop_bit(i % 2, stage, bits))) for i in range(n_dp)]


def swap_core(block, n_dp):
    return lax.ppermute(block, "dp", [(i, i ^ 1) for i in range(n_dp)])


def ahead(block, n_line, step):
    return lax.ppermute(block, "fsdp", [(i, (i + step) % n_line) for i in range(n_line)])


def add_up(terms):
    total = terms[0].astype(jnp.float32)
    for term in terms[1:]:
        total = total + term.astype(jnp.float32)
    return total


def reduce_steps(away, keep, n_dp, n_line):
    (away,) = yield [away]
    (got,) = yield [swap_core(away, n_dp)]
    terms = [keep, got]
    half = keep.shape[0] // 2
    for stage in range(n_dp.bit_length() - 2):
        (send,) = yield [add_up([term[half:] for term in terms]).astype(jnp.bfloat16)]
        (got,) = yield [lax.ppermute(send, "dp", hop_pairs(n_dp, stage))]
        terms = [term[:half] for term in terms] + [got]
        half //= 2
    terms = [term[0] for term in terms]
    sends = yield [
        add_up([term[step] for term in terms]).astype(jnp.bfloat16) for step in range(1, n_line)
    ]
    arrived = yield [ahead(send, n_line, step + 1) for step, send in enumerate(sends)]
    parts = [add_up([term[0] for term in terms] + arrived).astype(jnp.bfloat16)[None]]
    for stage in range(n_dp.bit_length() - 2):
        (send,) = yield [jnp.concatenate(parts) if len(parts) > 1 else parts[0]]
        (got,) = yield [lax.ppermute(send, "dp", hop_pairs(n_dp, stage))]
        parts = parts + [got]
    (send,) = yield [jnp.concatenate(parts)]
    (got,) = yield [swap_core(send, n_dp)]
    return [send, got]


def small_steps(mine, n_dp, n_line):
    (mine,) = yield [mine]
    for bit in range(n_dp.bit_length() - 1):
        pairs = [(i, i ^ (1 << bit)) for i in range(n_dp)]
        (got,) = yield [lax.ppermute(mine, "dp", pairs)]
        (mine,) = yield [mine + got]
    line = lax.axis_index("fsdp")

    def part(step):
        return lax.dynamic_index_in_dim(mine, (line + step) % n_line, 0, keepdims=False)

    arrived = yield [ahead(part(step), n_line, step) for step in range(1, n_line)]
    total = part(0)
    for item in arrived:
        total = total + item
    return [total]


class Reduction:
    def __init__(self, steps, close):
        self.steps = steps
        self.close = close
        self.parts = None
        self.held = None
        self.begin = next(steps)

    def take(self, got):
        try:
            return self.steps.send(got)
        except StopIteration as stop:
            self.parts = stop.value
            return []

    def result(self):
        if self.held is None:
            self.held = self.steps.send(self.begin)
        while self.parts is None:
            sends = self.take(self.held)
            if self.parts is None:
                self.held = self.steps.send(sends)
        return self.close(self.parts)


class Ready:
    def __init__(self, outs):
        self.outs = outs

    def result(self):
        return self.outs


def tick(value, running):
    running = [item for item in running if isinstance(item, Reduction) and item.parts is None]
    old = [item for item in running if item.held is not None]
    value, gots = lax.optimization_barrier((value, [item.held for item in old]))
    sends = [item.take(got) for item, got in zip(old, gots)]
    new = [item for item in running if item.held is None]
    sends = sends + [item.begin for item in new]
    value, sends = lax.optimization_barrier((value, sends))
    for item, send in zip(old + new, sends):
        if item.parts is None:
            item.held = item.steps.send(send)
    return value


def place_of(n_dp, me, flip):
    bits = n_dp.bit_length() - 2
    core = me % 2
    halves = []
    for other in range(2):
        place = jnp.arange(1 << bits, dtype=jnp.int32)
        owner = jnp.full((1 << bits,), me ^ other, jnp.int32)
        for stage in range(bits):
            at = bits - 1 - stage if flip else stage
            low = 1 << hop_bit(0, stage, bits)
            high = 1 << hop_bit(1, stage, bits)
            mask = jnp.where((core ^ other) == 0, low, high)
            owner = owner ^ (((place >> at) & 1) * mask)
        halves.append(owner)
    return jnp.concatenate(halves)


class Wide:
    def __init__(self, shard):
        self.shard = shard

    def gather(self, w_qkv, w_out, w_fc1, w_fc2, smalls):
        def full(matrix):
            return lax.all_gather(matrix, "fsdp", axis=0, tiled=True)

        self.full = [full(w_qkv), full(w_out), full(w_fc1), full(w_fc2)]
        return lax.all_gather(smalls, "fsdp", axis=0)

    def first(self):
        return self.full[:2]

    def second(self):
        return self.full[2]

    def third(self):
        return self.full[3]

    def pass_one(self, gate):
        return gate

    pass_two = pass_three = pass_four = pass_one

    def rows(self, block):
        return block

    def wide_columns(self, block):
        return block

    def total(self, terms):
        bf16 = jnp.bfloat16
        outs = []
        for left, right in terms:
            grad = t_times(left, right).astype(bf16)
            own = lax.psum_scatter(grad, "fsdp", scatter_dimension=0, tiled=True)
            outs.append(lax.psum(own, "dp").astype(jnp.float32))
        return Ready(outs)

    def total_small(self, smalls):
        own = lax.psum_scatter(
            smalls.astype(jnp.bfloat16), "fsdp", scatter_dimension=0, tiled=False
        )
        return Ready(lax.psum(own, "dp").astype(jnp.float32))


class Gather:
    def __init__(self, unit, n_dp, n_line):
        self.n_dp = n_dp
        self.line = [ahead(unit, n_line, step) for step in range(1, n_line)]

    def hop(self, block, stage):
        return lax.ppermute(block, "dp", hop_pairs(self.n_dp, stage))

    def fan(self, gate, rows):
        self.line, gate = lax.optimization_barrier((self.line, gate))
        near = jnp.stack([item[:rows] for item in self.line])[None]
        near, gate = lax.optimization_barrier((near, gate))
        self.parts = [near, self.hop(near, 0), self.hop(near, 1)]
        self.cores = [swap_core(near, self.n_dp)]
        return gate

    def forward(self, gate):
        self.parts[1], gate = lax.optimization_barrier((self.parts[1], gate))
        self.parts.append(self.hop(self.parts[1], 1))
        self.cores.append(swap_core(self.parts[1], self.n_dp))
        return gate

    def close(self, gate):
        late, gate = lax.optimization_barrier((self.parts[2:], gate))
        self.cores += [swap_core(item, self.n_dp) for item in late]
        self.parts = self.parts[:2] + late
        return gate


class Staged:
    def __init__(self, n_dp, n_line, dp, line, width):
        self.n_dp = n_dp
        self.n_line = n_line
        self.dp = dp
        self.line = line
        self.unit = width // n_line // n_dp
        steps = jnp.arange(n_line, dtype=jnp.int32)
        owner = place_of(n_dp, dp, False)
        self.owner = owner
        self.unline = (line - steps) % n_line
        first = line * n_dp
        got = self.unline[None, :] * n_dp + owner[:, None]
        self.got_table = jnp.concatenate([got.reshape(-1), first[None]]).astype(jnp.int32)
        send_line = (line + steps) % n_line
        send = send_line[None, :] * n_dp + place_of(n_dp, dp, True)[:, None]
        self.send_table = send.reshape(-1).astype(jnp.int32)
        natural = jnp.arange(width, dtype=jnp.int32)
        arranged = (
            self.send_table[:, None] * self.unit + jnp.arange(self.unit, dtype=jnp.int32)[None, :]
        ).reshape(-1)
        self.order = (natural[:, None] == arranged[None, :]).astype(jnp.bfloat16)

    def pick(self, shard):
        size = shard.shape[0] // self.n_dp
        return lax.dynamic_slice_in_dim(shard, self.dp * size, size, 0)

    def gather(self, w_qkv, w_out, w_fc1, w_fc2, smalls):
        n_dp = self.n_dp
        n_line = self.n_line
        shard = smalls.shape[1]
        wide = w_qkv.shape[1] + w_out.shape[1]
        fold = wide // shard
        small_rows = -(-smalls.shape[0] // (16 * fold)) * 16
        padded = jnp.pad(smalls, ((0, small_rows * fold - smalls.shape[0]), (0, 0)))
        packed = jnp.concatenate(
            [padded[i * small_rows : (i + 1) * small_rows] for i in range(fold)], axis=1
        )
        unit_one = jnp.concatenate(
            [jnp.concatenate([self.pick(w_qkv), self.pick(w_out)], axis=1), packed]
        )
        unit_two, unit_three = (self.pick(w_fc1), self.pick(w_fc2))
        size = self.unit
        one = Gather(unit_one, n_dp, n_line)
        unit_two = one.fan(unit_two, size)
        far = jnp.stack([item[size:] for item in one.line])
        two = Gather(unit_two, n_dp, n_line)
        two.line = one.forward(two.line)
        two.line = one.close(two.line)
        table, unit_three = two.fan((self.got_table, unit_three), size)
        three = Gather(unit_three, n_dp, n_line)
        full_qkv, full_out = assemble([w_qkv, w_out], one.parts + one.cores, table, n_line, size)
        self.one = (full_qkv, full_out)
        self.two = (w_fc1, two)
        self.three = (w_fc2, three, unit_three.shape[0])
        far = jnp.concatenate([far[:, :, i * shard : (i + 1) * shard] for i in range(fold)], axis=1)
        return jnp.take(jnp.concatenate([padded[None], far]), self.unline, axis=0)

    def first(self):
        return self.one

    def pass_one(self, gate):
        return self.two[1].forward(gate)

    def pass_two(self, gate):
        return self.three[1].fan(self.two[1].close(gate), self.three[2])

    def pass_three(self, gate):
        return self.three[1].forward(gate)

    def pass_four(self, gate):
        return self.three[1].close(gate)

    def second(self):
        own, got = self.two
        return assemble([own], got.parts + got.cores, self.got_table, self.n_line, self.unit)[0]

    def third(self):
        own, got, unit = self.three
        return assemble([own], got.parts + got.cores, self.got_table, self.n_line, unit)[0]

    def rows(self, block):
        return jnp.dot(block, self.order, preferred_element_type=jnp.float32).astype(jnp.bfloat16)

    def wide_columns(self, block):
        return column_order(block, self.send_table, block.shape[1] // (self.n_dp * self.n_line))

    def total(self, terms):
        n_dp = self.n_dp
        n_line = self.n_line
        sides = []
        for side in (1, 0):
            grads = []
            for left, right in terms:
                half = left.shape[1] // 2
                grad = t_times(left[:, side * half : (side + 1) * half], right).astype(jnp.bfloat16)
                grads.append(grad.reshape(n_dp // 2, n_line, -1, right.shape[1]))
            sides.append(jnp.concatenate(grads, axis=3) if len(grads) > 1 else grads[0])
        cuts = [right.shape[1] for left, right in terms]
        owner = self.owner.astype(jnp.int32)
        steps = reduce_steps(sides[0], sides[1], n_dp, n_line)
        return Reduction(steps, lambda parts: list(finish(parts, owner, cuts)))

    def total_small(self, smalls):
        n_small = smalls.shape[1]
        padded = jnp.pad(smalls, ((0, 0), (0, -n_small % 8), (0, 0)))
        return Reduction(
            small_steps(padded, self.n_dp, self.n_line), lambda parts: parts[0][:n_small]
        )


def per_device(
    patches,
    cotangent,
    ln1_gain,
    ln1_bias,
    w_qkv,
    w_out,
    ln2_gain,
    ln2_bias,
    w_fc1,
    fc1_bias,
    w_fc2,
    pos_table,
    pos_index,
    pos_weight,
):
    bf16 = jnp.bfloat16
    f32 = jnp.float32
    n_dp = lax.axis_size("dp")
    n_line = lax.axis_size("fsdp")
    dp = lax.axis_index("dp")
    line = lax.axis_index("fsdp")
    low_flag = dp < n_dp * 7 // 16
    rows = patches.shape[0]
    width = patches.shape[1]
    shard = width // n_line
    place, valid, segment = place_rows(rows, low_flag, pos_index, pos_weight)
    if n_dp == 8 and n_line <= 4 and shard % (16 * n_dp) == 0:
        plan = Staged(n_dp, n_line, dp, line, width)
    else:
        plan = Wide(shard)
    n_bias = fc1_bias.size // shard
    smalls = jnp.concatenate(
        [
            jnp.stack([ln1_gain, ln1_bias, ln2_gain, ln2_bias]),
            fc1_bias.reshape(-1, shard),
            pos_table,
        ]
    )
    n_small = smalls.shape[0]
    table = plan.gather(w_qkv, w_out, w_fc1, w_fc2, smalls)
    full_qkv, full_out = plan.first()

    def across(block):
        return block.transpose(1, 0, 2).reshape(block.shape[1], width).astype(f32)

    gain_one, bias_one, gain_two, bias_two = across(table[:, :4])
    full_bias = table[:, 4 : 4 + n_bias].reshape(-1).astype(f32)
    full_table = across(table[:, 4 + n_bias : n_small])

    hidden_in = patches.astype(f32) + jnp.dot(place, full_table, precision=highest)
    normed_one = layer_norm(hidden_in, gain_one, bias_one).astype(bf16)
    projected = jnp.dot(normed_one, full_qkv, preferred_element_type=f32).astype(bf16)
    projected = plan.pass_one(projected)
    attn_rows = plan.pass_two(attend(projected, segment))
    hidden_mid = hidden_in + jnp.dot(attn_rows, full_out, preferred_element_type=f32)
    normed_two = layer_norm(hidden_mid, gain_two, bias_two).astype(bf16)
    normed_two = plan.pass_three(normed_two)
    full_fc1 = plan.second()
    pre_act = jnp.dot(normed_two, full_fc1, preferred_element_type=f32) + full_bias
    share = 0.5 * (1.0 + lax.erf(pre_act * 0.5**0.5))
    bell = jnp.exp(-0.5 * pre_act * pre_act) * (0.5 / jnp.pi) ** 0.5
    activated = (pre_act * share).astype(bf16)
    slope = (share + pre_act * bell).astype(bf16)
    activated = plan.pass_four(activated)
    grad_out = jnp.where(valid[:, None], cotangent, jnp.zeros_like(cotangent))
    run_fc2 = plan.total([(plan.wide_columns(activated), grad_out)])
    activated = tick(activated, [run_fc2])
    full_fc2, activated = tick((plan.third(), activated), [run_fc2])
    branch_out = jnp.dot(activated, full_fc2, preferred_element_type=f32)
    block_out = jnp.where(valid[:, None], hidden_mid + branch_out, 0.0).astype(bf16)

    grad_pre = (times_t(grad_out, full_fc2) * slope.astype(f32)).astype(bf16)
    grad_fc1_bias = jnp.sum(grad_pre.astype(f32), axis=0)
    run_fc1 = plan.total([(plan.rows(normed_two), grad_pre)])
    grad_pre = tick(grad_pre, [run_fc1])
    grad_norm_two = times_t(grad_pre, full_fc1)
    _, pull_two = jax.vjp(layer_norm, hidden_mid, gain_two, bias_two)
    back_mid, grad_gain_two, grad_bias_two = pull_two(grad_norm_two)
    grad_mid = grad_out.astype(f32) + back_mid
    grad_branch = tick(grad_mid.astype(bf16), [run_fc1])
    run_out = plan.total([(plan.rows(attn_rows), grad_branch)])
    grad_attn = times_t(grad_branch, full_out).astype(bf16)
    grad_attn = tick(grad_attn, [run_fc2, run_out])
    half = HEADS // 4
    back_a = attend_back(projected, grad_attn, segment, 0, half)
    back_a, grad_attn = tick((back_a, grad_attn), [run_fc2, run_fc1, run_out])
    back_b = attend_back(projected, grad_attn, segment, half, half)
    back_a, back_b = tick((back_a, back_b), [run_fc2, run_fc1, run_out])
    side = back_a.shape[1] // 3
    grad_proj = jnp.concatenate(
        [part[:, i * side : (i + 1) * side] for i in range(3) for part in (back_a, back_b)], axis=1
    )
    run_qkv = plan.total([(plan.rows(normed_one), grad_proj)])
    grad_proj = tick(grad_proj, [run_qkv])
    grad_norm_one = times_t(grad_proj, full_qkv)
    grad_norm_one = tick(grad_norm_one, [run_fc2, run_fc1, run_out, run_qkv])
    _, pull_one = jax.vjp(layer_norm, hidden_in, gain_one, bias_one)
    back_in, grad_gain_one, grad_bias_one = pull_one(grad_norm_one)
    grad_in = grad_mid + back_in
    grad_table = jnp.dot(place.T, grad_in, precision=highest)

    def split(block):
        return block.reshape(-1, n_line, shard).transpose(1, 0, 2)

    rows_small = jnp.concatenate(
        [
            split(jnp.stack([grad_gain_one, grad_bias_one, grad_gain_two, grad_bias_two])),
            grad_fc1_bias.reshape(n_line, -1, shard),
            split(grad_table),
        ],
        axis=1,
    )
    run_small = plan.total_small(rows_small)
    (sum_fc2,) = run_fc2.result()
    (sum_fc1,) = run_fc1.result()
    (sum_out,) = run_out.result()
    (sum_qkv,) = run_qkv.result()
    small = run_small.result()
    return (
        block_out,
        grad_in.astype(bf16),
        small[0],
        small[1],
        sum_qkv,
        sum_out,
        small[2],
        small[3],
        sum_fc1,
        small[4 : 4 + n_bias].reshape(-1),
        sum_fc2,
        small[4 + n_bias :],
    )


def solution(mesh):
    return jax.shard_map(
        per_device,
        mesh=mesh,
        in_specs=(
            P(("dp", "fsdp"), None),
            P(("dp", "fsdp"), None),
            P("fsdp"),
            P("fsdp"),
            P("fsdp", None),
            P("fsdp", None),
            P("fsdp"),
            P("fsdp"),
            P("fsdp", None),
            P("fsdp"),
            P("fsdp", None),
            P(None, "fsdp"),
            P(),
            P(),
        ),
        out_specs=(
            P(("dp", "fsdp"), None),
            P(("dp", "fsdp"), None),
            P("fsdp"),
            P("fsdp"),
            P("fsdp", None),
            P("fsdp", None),
            P("fsdp"),
            P("fsdp"),
            P("fsdp", None),
            P("fsdp"),
            P("fsdp", None),
            P(None, "fsdp"),
        ),
        check_vma=False,
    )
```

```python
import jax
import jax.numpy as jnp
from jax import lax
from jax.experimental import pallas as pl
from jax.experimental.pallas import tpu as pltpu
from jax.sharding import PartitionSpec as P

HEADS = 16
HDIM = 64
POS = 50
HIGH_LEN = 145
TILE = 128


highest = lax.Precision.HIGHEST


def layer_norm(hidden, gain, shift):
    centre = hidden - jnp.mean(hidden, axis=-1, keepdims=True)
    spread = jnp.mean(centre * centre, axis=-1, keepdims=True)
    return centre * lax.rsqrt(spread + 1e-06) * gain + shift


def place_rows(rows, low_flag, pos_index, pos_weight):
    offsets = jnp.arange(rows, dtype=jnp.int32)
    table_ids = jnp.arange(POS, dtype=jnp.int32)
    high_ids = jnp.arange(HIGH_LEN, dtype=jnp.int32)
    picks = (pos_index[:, :, None] == table_ids[None, None, :]).astype(jnp.float32)
    interp = jnp.sum(pos_weight[:, :, None] * picks, axis=1)
    low_valid = offsets < rows // POS * POS
    high_valid = offsets < rows // HIGH_LEN * HIGH_LEN
    low_place = (((offsets % POS)[:, None] == table_ids[None, :]) & low_valid[:, None]).astype(
        jnp.float32
    )
    high_pick = (((offsets % HIGH_LEN)[:, None] == high_ids[None, :]) & high_valid[:, None]).astype(
        jnp.float32
    )
    high_place = jnp.dot(high_pick, interp, precision=highest)
    place = jnp.where(low_flag, low_place, high_place)
    valid = jnp.where(low_flag, low_valid, high_valid)
    segment = jnp.where(
        low_flag,
        jnp.where(low_valid, offsets // POS, -1),
        jnp.where(high_valid, offsets // HIGH_LEN, -1),
    )
    return (place, valid, segment)


def key_windows(rows):
    out = []
    for start in range(0, rows, TILE):
        least, most = rows, 0
        for size in (POS, HIGH_LEN):
            used = rows // size * size
            for row in (start, start + TILE - 1):
                image = row // size
                begin = image * size if row < used else used
                end = begin + size if row < used else rows
                least, most = min(least, begin), max(most, end)
        out.append((start, least // TILE * TILE, -(-most // TILE) * TILE))
    return out


def times_t(left, right):
    return lax.dot_general(left, right, (((1,), (1,)), ((), ())), preferred_element_type=jnp.float32)


def t_times(left, right):
    return lax.dot_general(left, right, (((0,), (0,)), ((), ())), preferred_element_type=jnp.float32)


def halves(block, scale=None):
    lane = lax.broadcasted_iota(jnp.int32, block.shape, 1)
    if scale is not None:
        block = block * jnp.asarray(scale, block.dtype)
    zero = jnp.zeros_like(block)
    return (jnp.where(lane < HDIM, block, zero), jnp.where(lane < HDIM, zero, block))


def soft(query, keys, same):
    scores = jnp.where(same, times_t(query, keys), -1e30)
    expo = jnp.exp(scores - jnp.max(scores, axis=-1, keepdims=True))
    return expo * (1.0 / jnp.sum(expo, axis=-1, keepdims=True))


def attend_body(windows, col_ref, row_ref, q_ref, k_ref, v_ref, out_ref):
    values = halves(v_ref[...])
    for start, lo, hi in windows:
        rows = slice(start, start + TILE)
        same = col_ref[rows, :] == row_ref[:, lo:hi]
        keys = k_ref[lo:hi, :]
        total = None
        for query, value in zip(halves(q_ref[rows, :], HDIM ** (-0.5)), values):
            probs = soft(query, keys, same).astype(jnp.bfloat16)
            part = jnp.dot(probs, value[lo:hi], preferred_element_type=jnp.float32)
            total = part if total is None else total + part
        out_ref[rows, :] = total.astype(jnp.bfloat16)


def attend_back_body(windows, col_ref, row_ref, q_ref, k_ref, v_ref, g_ref, out_ref, dk_ref, dv_ref):
    width = q_ref.shape[1]
    full = out_ref.shape[1] // 3
    at = pl.program_id(0) * width
    dk_ref[...] = jnp.zeros_like(dk_ref)
    dv_ref[...] = jnp.zeros_like(dv_ref)
    scaled = halves(k_ref[...], HDIM ** (-0.5))
    for start, lo, hi in windows:
        rows = slice(start, start + TILE)
        same = col_ref[rows, :] == row_ref[:, lo:hi]
        keys = k_ref[lo:hi, :]
        values = v_ref[lo:hi, :]
        total = None
        queries = halves(q_ref[rows, :], HDIM ** (-0.5))
        grads = halves(g_ref[rows, :])
        for query, grad, key in zip(queries, grads, scaled):
            probs = soft(query, keys, same)
            grad_probs = times_t(grad, values)
            centre = jnp.sum(probs * grad_probs, axis=-1, keepdims=True)
            grad_scores = (probs * (grad_probs - centre)).astype(jnp.bfloat16)
            part = jnp.dot(grad_scores, key[lo:hi], preferred_element_type=jnp.float32)
            total = part if total is None else total + part
            dk_ref[lo:hi, :] += t_times(grad_scores, query)
            dv_ref[lo:hi, :] += t_times(probs.astype(jnp.bfloat16), grad)
        out_ref[rows, pl.ds(pl.multiple_of(at, width), width)] = total.astype(jnp.bfloat16)
    out_ref[:, pl.ds(pl.multiple_of(full + at, width), width)] = dk_ref[...].astype(jnp.bfloat16)
    out_ref[:, pl.ds(pl.multiple_of(2 * full + at, width), width)] = dv_ref[...].astype(jnp.bfloat16)


def pair_specs(rows, pairs, start=0):
    pair = 2 * HDIM
    whole = [
        pl.BlockSpec((rows, 1), lambda i: (0, 0)),
        pl.BlockSpec((1, rows), lambda i: (0, 0)),
    ]
    return whole + [
        pl.BlockSpec((rows, pair), lambda i, j=j: (0, j * pairs + start + i)) for j in range(3)
    ]


def attend(projected, segment):
    rows = projected.shape[0]
    pairs = HEADS // 2
    windows = key_windows(rows)

    def body(*refs):
        attend_body(windows, *refs)

    return pl.pallas_call(
        body,
        grid=(pairs,),
        in_specs=pair_specs(rows, pairs),
        out_specs=pl.BlockSpec((rows, 2 * HDIM), lambda i: (0, i)),
        out_shape=jax.ShapeDtypeStruct((rows, HEADS * HDIM), jnp.bfloat16),
        name="attend",
    )(segment[:, None], segment[None, :], projected, projected, projected)


def attend_back(projected, grad_attn, segment, start, count):
    rows = projected.shape[0]
    pairs = HEADS // 2
    windows = key_windows(rows)
    wide = 3 * count * 2 * HDIM

    def body(*refs):
        attend_back_body(windows, *refs)

    return pl.pallas_call(
        body,
        grid=(count,),
        in_specs=pair_specs(rows, pairs, start)
        + [pl.BlockSpec((rows, 2 * HDIM), lambda i: (0, start + i))],
        out_specs=pl.BlockSpec((rows, wide), lambda i: (0, 0)),
        out_shape=jax.ShapeDtypeStruct((rows, wide), jnp.bfloat16),
        scratch_shapes=[pltpu.VMEM((rows, 2 * HDIM), jnp.float32)] * 2,
        name="attend_back",
    )(segment[:, None], segment[None, :], projected, projected, projected, grad_attn)


def copies(pairs_of, sems):
    moves = [
        pltpu.make_async_copy(source, target, sems.at[i])
        for i, (source, target) in enumerate(pairs_of)
    ]
    for move in moves:
        move.start()
    for move in moves:
        move.wait()


def assemble(owns, parts, table, n_line, unit):
    n_places = sum(part.shape[0] for part in parts)
    n_own = len(owns)
    n_parts = len(parts)
    ends = []
    for own in owns:
        ends.append((ends[-1] if ends else 0) + own.shape[1])
    count = n_own * (1 + n_places * (n_line - 1))

    def body(table_ref, *refs):
        own_refs = refs[:n_own]
        part_refs = refs[n_own : n_own + n_parts]
        out_refs = refs[n_own + n_parts : 2 * n_own + n_parts]
        sems = refs[-1]
        todo = []
        for own_ref, out_ref, end in zip(own_refs, out_refs, ends):
            shard_rows = own_ref.shape[0]
            columns = pl.ds(end - own_ref.shape[1], own_ref.shape[1])
            first = pl.multiple_of(table_ref[n_places * n_line] * unit, unit)
            todo.append((own_ref, out_ref.at[pl.ds(first, shard_rows), :]))
            place = 0
            for part_ref in part_refs:
                for k in range(part_ref.shape[0]):
                    for step in range(1, n_line):
                        row = pl.multiple_of(table_ref[place * n_line + step] * unit, unit)
                        todo.append(
                            (
                                part_ref.at[k, step - 1, pl.ds(0, unit), columns],
                                out_ref.at[pl.ds(row, unit), :],
                            )
                        )
                    place += 1
        copies(todo, sems)

    anywhere = pl.BlockSpec(memory_space=pl.ANY)
    return pl.pallas_call(
        body,
        in_specs=[pl.BlockSpec(memory_space=pltpu.SMEM)] + [anywhere] * (n_own + n_parts),
        out_specs=[pl.BlockSpec(memory_space=pltpu.VMEM)] * n_own,
        out_shape=[
            jax.ShapeDtypeStruct((own.shape[0] * n_line, own.shape[1]), own.dtype) for own in owns
        ],
        scratch_shapes=[pltpu.SemaphoreType.DMA((count,))],
        name="assemble",
    )(table, *owns, *parts)


def column_order(block, table, unit):
    count = block.shape[1] // unit

    def body(table_ref, in_ref, out_ref):
        for i in range(count):
            column = pl.multiple_of(table_ref[i] * unit, unit)
            out_ref[:, i * unit : (i + 1) * unit] = in_ref[:, pl.ds(column, unit)]

    return pl.pallas_call(
        body,
        in_specs=[
            pl.BlockSpec(memory_space=pltpu.SMEM),
            pl.BlockSpec(memory_space=pltpu.VMEM),
        ],
        out_specs=pl.BlockSpec(memory_space=pltpu.VMEM),
        out_shape=jax.ShapeDtypeStruct(block.shape, block.dtype),
        name="column_order",
    )(table, block)


def finish(parts, owner, cuts):
    unit = parts[0].shape[1]
    n_places = sum(part.shape[0] for part in parts)

    def body(owner_ref, *refs):
        part_refs = refs[: len(parts)]
        out_refs = refs[len(parts) :]
        place = 0
        for part_ref in part_refs:
            for k in range(part_ref.shape[0]):
                row = pl.multiple_of(owner_ref[place] * unit, unit)
                at = 0
                for out_ref, cut in zip(out_refs, cuts):
                    out_ref[pl.ds(row, unit), :] = part_ref[k, :, at : at + cut].astype(jnp.float32)
                    at += cut
                place += 1

    return pl.pallas_call(
        body,
        in_specs=[pl.BlockSpec(memory_space=pltpu.SMEM)]
        + [pl.BlockSpec(memory_space=pltpu.VMEM)] * len(parts),
        out_specs=[pl.BlockSpec(memory_space=pltpu.VMEM)] * len(cuts),
        out_shape=[jax.ShapeDtypeStruct((n_places * unit, cut), jnp.float32) for cut in cuts],
        name="finish",
    )(owner, *parts)


def hop_bit(core, stage, bits):
    return 1 + stage if core == 0 else bits - stage


def hop_pairs(n_dp, stage):
    bits = n_dp.bit_length() - 2
    return [(i, i ^ (1 << hop_bit(i % 2, stage, bits))) for i in range(n_dp)]


def swap_core(block, n_dp):
    return lax.ppermute(block, "dp", [(i, i ^ 1) for i in range(n_dp)])


def ahead(block, n_line, step):
    return lax.ppermute(block, "fsdp", [(i, (i + step) % n_line) for i in range(n_line)])


def add_up(terms):
    total = terms[0].astype(jnp.float32)
    for term in terms[1:]:
        total = total + term.astype(jnp.float32)
    return total


def reduce_steps(grad, n_dp, n_line):
    half = n_dp // 2
    (away,) = yield [grad(half, n_dp).astype(jnp.bfloat16)]
    (got,) = yield [swap_core(away, n_dp)]
    terms = [got]
    half //= 2
    for stage in range(n_dp.bit_length() - 2):
        total = add_up([grad(half, 2 * half)] + [term[half:] for term in terms])
        (send,) = yield [total.astype(jnp.bfloat16)]
        (got,) = yield [lax.ppermute(send, "dp", hop_pairs(n_dp, stage))]
        terms = [term[:half] for term in terms] + [got]
        half //= 2
    total = add_up([grad(0, 1)[0]] + [term[0] for term in terms]).astype(jnp.bfloat16)
    sends = yield [total[step] for step in range(n_line)]
    arrived = yield [ahead(sends[step], n_line, step) for step in range(1, n_line)]
    parts = [add_up([sends[0]] + arrived).astype(jnp.bfloat16)[None]]
    for stage in range(n_dp.bit_length() - 2):
        (send,) = yield [jnp.concatenate(parts) if len(parts) > 1 else parts[0]]
        (got,) = yield [lax.ppermute(send, "dp", hop_pairs(n_dp, stage))]
        parts = parts + [got]
    (send,) = yield [jnp.concatenate(parts)]
    (got,) = yield [swap_core(send, n_dp)]
    return [send, got]


def small_steps(mine, n_dp, n_line):
    (mine,) = yield [mine]
    for bit in range(n_dp.bit_length() - 1):
        pairs = [(i, i ^ (1 << bit)) for i in range(n_dp)]
        (got,) = yield [lax.ppermute(mine, "dp", pairs)]
        (mine,) = yield [mine + got]
    line = lax.axis_index("fsdp")

    def part(step):
        return lax.dynamic_index_in_dim(mine, (line + step) % n_line, 0, keepdims=False)

    arrived = yield [ahead(part(step), n_line, step) for step in range(1, n_line)]
    total = part(0)
    for item in arrived:
        total = total + item
    return [total]


class Reduction:
    def __init__(self, steps, close):
        self.steps = steps
        self.close = close
        self.parts = None
        self.held = None
        self.begin = next(steps)

    def take(self, got):
        try:
            return self.steps.send(got)
        except StopIteration as stop:
            self.parts = stop.value
            return []

    def result(self):
        if self.held is None:
            self.held = self.steps.send(self.begin)
        while self.parts is None:
            sends = self.take(self.held)
            if self.parts is None:
                self.held = self.steps.send(sends)
        return self.close(self.parts)


class Ready:
    def __init__(self, outs):
        self.outs = outs

    def result(self):
        return self.outs


def tick(value, running):
    running = [item for item in running if isinstance(item, Reduction) and item.parts is None]
    old = [item for item in running if item.held is not None]
    value, gots = lax.optimization_barrier((value, [item.held for item in old]))
    sends = [item.take(got) for item, got in zip(old, gots)]
    new = [item for item in running if item.held is None]
    sends = sends + [item.begin for item in new]
    value, sends = lax.optimization_barrier((value, sends))
    for item, send in zip(old + new, sends):
        if item.parts is None:
            item.held = item.steps.send(send)
    return value


def place_of(n_dp, me, flip):
    bits = n_dp.bit_length() - 2
    core = me % 2
    halves = []
    for other in range(2):
        place = jnp.arange(1 << bits, dtype=jnp.int32)
        owner = jnp.full((1 << bits,), me ^ other, jnp.int32)
        for stage in range(bits):
            at = bits - 1 - stage if flip else stage
            low = 1 << hop_bit(0, stage, bits)
            high = 1 << hop_bit(1, stage, bits)
            mask = jnp.where((core ^ other) == 0, low, high)
            owner = owner ^ (((place >> at) & 1) * mask)
        halves.append(owner)
    return jnp.concatenate(halves)


class Wide:
    def __init__(self, shard):
        self.shard = shard

    def gather(self, w_qkv, w_out, w_fc1, w_fc2, smalls):
        def full(matrix):
            return lax.all_gather(matrix, "fsdp", axis=0, tiled=True)

        self.full = [full(w_qkv), full(w_out), full(w_fc1), full(w_fc2)]
        return lax.all_gather(smalls, "fsdp", axis=0)

    def first(self):
        return self.full[0]

    def second(self):
        return self.full[1:3]

    def third(self):
        return self.full[3]

    def pass_one(self, gate):
        return gate

    pass_two = pass_three = pass_four = pass_one

    def rows(self, block):
        return block

    def wide_columns(self, block):
        return block

    def total(self, left, right):
        grad = t_times(left, right).astype(jnp.bfloat16)
        own = lax.psum_scatter(grad, "fsdp", scatter_dimension=0, tiled=True)
        return Ready(lax.psum(own, "dp").astype(jnp.float32))

    def total_small(self, smalls):
        own = lax.psum_scatter(
            smalls.astype(jnp.bfloat16), "fsdp", scatter_dimension=0, tiled=False
        )
        return Ready(lax.psum(own, "dp").astype(jnp.float32))


class Gather:
    def __init__(self, unit, n_dp, n_line):
        self.n_dp = n_dp
        self.line = [ahead(unit, n_line, step) for step in range(1, n_line)]

    def hop(self, block, stage):
        return lax.ppermute(block, "dp", hop_pairs(self.n_dp, stage))

    def fan(self, gate, columns):
        self.line, gate = lax.optimization_barrier((self.line, gate))
        near = jnp.stack([item[:, :columns] for item in self.line])[None]
        near, gate = lax.optimization_barrier((near, gate))
        self.parts = [near, self.hop(near, 0), self.hop(near, 1)]
        self.cores = [swap_core(near, self.n_dp)]
        return gate

    def forward(self, gate):
        self.parts[1], gate = lax.optimization_barrier((self.parts[1], gate))
        self.parts.append(self.hop(self.parts[1], 1))
        self.cores.append(swap_core(self.parts[1], self.n_dp))
        return gate

    def close(self, gate):
        late, gate = lax.optimization_barrier((self.parts[2:], gate))
        self.cores += [swap_core(item, self.n_dp) for item in late]
        self.parts = self.parts[:2] + late
        return gate


class Staged:
    def __init__(self, n_dp, n_line, dp, line, width):
        self.n_dp = n_dp
        self.n_line = n_line
        self.dp = dp
        self.line = line
        self.unit = width // n_line // n_dp
        steps = jnp.arange(n_line, dtype=jnp.int32)
        owner = place_of(n_dp, dp, False)
        self.owner = owner
        self.unline = (line - steps) % n_line
        first = line * n_dp
        got = self.unline[None, :] * n_dp + owner[:, None]
        self.got_table = jnp.concatenate([got.reshape(-1), first[None]]).astype(jnp.int32)
        send_line = (line + steps) % n_line
        send = send_line[None, :] * n_dp + place_of(n_dp, dp, True)[:, None]
        self.send_table = send.reshape(-1).astype(jnp.int32)
        natural = jnp.arange(width, dtype=jnp.int32)
        arranged = (
            self.send_table[:, None] * self.unit + jnp.arange(self.unit, dtype=jnp.int32)[None, :]
        ).reshape(-1)
        self.order = (natural[:, None] == arranged[None, :]).astype(jnp.bfloat16)

    def pick(self, shard):
        size = shard.shape[0] // self.n_dp
        return lax.dynamic_slice_in_dim(shard, self.dp * size, size, 0)

    def gather(self, w_qkv, w_out, w_fc1, w_fc2, smalls):
        n_dp = self.n_dp
        n_line = self.n_line
        shard = smalls.shape[1]
        size = self.unit
        wide = w_qkv.shape[1]
        fold = -(-smalls.shape[0] // size)
        padded = jnp.pad(smalls, ((0, size * fold - smalls.shape[0]), (0, 0)))
        packed = [padded[i * size : (i + 1) * size] for i in range(fold)]
        unit_one = jnp.concatenate([self.pick(w_qkv)] + packed, axis=1)
        unit_two = jnp.concatenate([self.pick(w_out), self.pick(w_fc1)], axis=1)
        unit_three = self.pick(w_fc2)
        one = Gather(unit_one, n_dp, n_line)
        unit_two = one.fan(unit_two, wide)
        far = jnp.stack([item[:, wide:] for item in one.line])
        two = Gather(unit_two, n_dp, n_line)
        two.line = one.forward(two.line)
        two.line = one.close(two.line)
        table, unit_three = two.fan((self.got_table, unit_three), unit_two.shape[1])
        three = Gather(unit_three, n_dp, n_line)
        (full_qkv,) = assemble([w_qkv], one.parts + one.cores, table, n_line, size)
        self.one = full_qkv
        self.two = ([w_out, w_fc1], two)
        self.three = (w_fc2, three, unit_three.shape)
        far = jnp.concatenate([far[:, :, i * shard : (i + 1) * shard] for i in range(fold)], axis=1)
        return jnp.take(jnp.concatenate([padded[None], far]), self.unline, axis=0)

    def first(self):
        return self.one

    def pass_one(self, gate):
        return self.two[1].forward(gate)

    def pass_two(self, gate):
        return self.three[1].fan(self.two[1].close(gate), self.three[2][1])

    def pass_three(self, gate):
        return self.three[1].forward(gate)

    def pass_four(self, gate):
        return self.three[1].close(gate)

    def second(self):
        owns, got = self.two
        return assemble(owns, got.parts + got.cores, self.got_table, self.n_line, self.unit)

    def third(self):
        own, got, unit = self.three
        return assemble([own], got.parts + got.cores, self.got_table, self.n_line, unit[0])[0]

    def rows(self, block):
        return jnp.dot(block, self.order, preferred_element_type=jnp.float32).astype(jnp.bfloat16)

    def wide_columns(self, block):
        return column_order(block, self.send_table, block.shape[1] // (self.n_dp * self.n_line))

    def total(self, left, right):
        n_dp = self.n_dp
        per = left.shape[1] // n_dp
        owner = self.owner.astype(jnp.int32)

        def grad(first, last):
            out = t_times(left[:, first * per : last * per], right)
            return out.reshape(last - first, self.n_line, -1, right.shape[1])

        steps = reduce_steps(grad, n_dp, self.n_line)
        return Reduction(steps, lambda parts: finish(parts, owner, [right.shape[1]])[0])

    def total_small(self, smalls):
        n_small = smalls.shape[1]
        padded = jnp.pad(smalls, ((0, 0), (0, -n_small % 8), (0, 0)))
        return Reduction(
            small_steps(padded, self.n_dp, self.n_line), lambda parts: parts[0][:n_small]
        )


def per_device(
    patches,
    cotangent,
    ln1_gain,
    ln1_bias,
    w_qkv,
    w_out,
    ln2_gain,
    ln2_bias,
    w_fc1,
    fc1_bias,
    w_fc2,
    pos_table,
    pos_index,
    pos_weight,
):
    bf16 = jnp.bfloat16
    f32 = jnp.float32
    n_dp = lax.axis_size("dp")
    n_line = lax.axis_size("fsdp")
    dp = lax.axis_index("dp")
    line = lax.axis_index("fsdp")
    low_flag = dp < n_dp * 7 // 16
    rows = patches.shape[0]
    width = patches.shape[1]
    shard = width // n_line
    place, valid, segment = place_rows(rows, low_flag, pos_index, pos_weight)
    if n_dp == 8 and n_line <= 4 and shard % (16 * n_dp) == 0:
        plan = Staged(n_dp, n_line, dp, line, width)
    else:
        plan = Wide(shard)
    n_bias = fc1_bias.size // shard
    smalls = jnp.concatenate(
        [
            jnp.stack([ln1_gain, ln1_bias, ln2_gain, ln2_bias]),
            fc1_bias.reshape(-1, shard),
            pos_table,
        ]
    )
    n_small = smalls.shape[0]
    table = plan.gather(w_qkv, w_out, w_fc1, w_fc2, smalls)
    full_qkv = plan.first()

    def across(block):
        return block.transpose(1, 0, 2).reshape(block.shape[1], width).astype(f32)

    gain_one, bias_one, gain_two, bias_two = across(table[:, :4])
    full_bias = table[:, 4 : 4 + n_bias].reshape(-1).astype(f32)
    full_table = across(table[:, 4 + n_bias : n_small])

    hidden_in = patches.astype(f32) + jnp.dot(place, full_table, precision=highest)
    normed_one = layer_norm(hidden_in, gain_one, bias_one).astype(bf16)
    projected = jnp.dot(normed_one, full_qkv, preferred_element_type=f32).astype(bf16)
    projected = plan.pass_one(projected)
    attn_rows = plan.pass_two(attend(projected, segment))
    full_out, full_fc1 = plan.second()
    hidden_mid = hidden_in + jnp.dot(attn_rows, full_out, preferred_element_type=f32)
    normed_two = layer_norm(hidden_mid, gain_two, bias_two).astype(bf16)
    pre_act = jnp.dot(normed_two, full_fc1, preferred_element_type=f32) + full_bias
    share = 0.5 * (1.0 + lax.erf(pre_act * 0.5**0.5))
    bell = jnp.exp(-0.5 * pre_act * pre_act) * (0.5 / jnp.pi) ** 0.5
    activated = (pre_act * share).astype(bf16)
    slope = (share + pre_act * bell).astype(bf16)
    activated, slope = plan.pass_three((activated, slope))
    grad_out = jnp.where(valid[:, None], cotangent, jnp.zeros_like(cotangent))
    run_fc2 = plan.total(plan.wide_columns(activated), grad_out)
    activated, slope = tick((activated, slope), [run_fc2])
    activated, slope = plan.pass_four((activated, slope))
    full_fc2 = tick(plan.third(), [run_fc2])
    branch_out = jnp.dot(activated, full_fc2, preferred_element_type=f32)
    block_out = jnp.where(valid[:, None], hidden_mid + branch_out, 0.0).astype(bf16)

    grad_pre = (times_t(grad_out, full_fc2) * slope.astype(f32)).astype(bf16)
    grad_fc1_bias = jnp.sum(grad_pre.astype(f32), axis=0)
    run_fc1 = plan.total(plan.rows(normed_two), grad_pre)
    grad_pre = tick(grad_pre, [run_fc1])
    grad_norm_two = times_t(grad_pre, full_fc1)
    grad_norm_two = tick(grad_norm_two, [run_fc1, run_fc2])
    _, pull_two = jax.vjp(layer_norm, hidden_mid, gain_two, bias_two)
    back_mid, grad_gain_two, grad_bias_two = pull_two(grad_norm_two)
    grad_mid = grad_out.astype(f32) + back_mid
    grad_branch = grad_mid.astype(bf16)
    run_out = plan.total(plan.rows(attn_rows), grad_branch)
    grad_branch = tick(grad_branch, [run_out])
    grad_attn = times_t(grad_branch, full_out).astype(bf16)
    grad_attn = tick(grad_attn, [run_out])
    half = HEADS // 4
    back_a = attend_back(projected, grad_attn, segment, 0, half)
    back_a, grad_attn = tick((back_a, grad_attn), [run_fc2, run_fc1, run_out])
    back_b = attend_back(projected, grad_attn, segment, half, half)
    side = back_a.shape[1] // 3
    grad_proj = jnp.concatenate(
        [part[:, i * side : (i + 1) * side] for i in range(3) for part in (back_a, back_b)], axis=1
    )
    run_qkv = plan.total(plan.rows(normed_one), grad_proj)
    grad_proj = tick(grad_proj, [run_qkv])
    grad_norm_one = tick(times_t(grad_proj, full_qkv), [run_qkv])
    grad_norm_one = tick(grad_norm_one, [run_fc2, run_fc1, run_out])
    _, pull_one = jax.vjp(layer_norm, hidden_in, gain_one, bias_one)
    back_in, grad_gain_one, grad_bias_one = pull_one(grad_norm_one)
    grad_in = grad_mid + back_in
    grad_table = jnp.dot(place.T, grad_in, precision=highest)
    grad_table, block_out = tick((grad_table, block_out), [run_qkv, run_fc1, run_fc2, run_out])

    def split(block):
        return block.reshape(-1, n_line, shard).transpose(1, 0, 2)

    rows_small = jnp.concatenate(
        [
            split(jnp.stack([grad_gain_one, grad_bias_one, grad_gain_two, grad_bias_two])),
            grad_fc1_bias.reshape(n_line, -1, shard),
            split(grad_table),
        ],
        axis=1,
    )
    run_small = plan.total_small(rows_small)
    sum_fc2 = run_fc2.result()
    sum_fc1 = run_fc1.result()
    sum_out = run_out.result()
    sum_qkv = run_qkv.result()
    small = run_small.result()
    return (
        block_out,
        grad_in.astype(bf16),
        small[0],
        small[1],
        sum_qkv,
        sum_out,
        small[2],
        small[3],
        sum_fc1,
        small[4 : 4 + n_bias].reshape(-1),
        sum_fc2,
        small[4 + n_bias :],
    )


def solution(mesh):
    return jax.shard_map(
        per_device,
        mesh=mesh,
        in_specs=(
            P(("dp", "fsdp"), None),
            P(("dp", "fsdp"), None),
            P("fsdp"),
            P("fsdp"),
            P("fsdp", None),
            P("fsdp", None),
            P("fsdp"),
            P("fsdp"),
            P("fsdp", None),
            P("fsdp"),
            P("fsdp", None),
            P(None, "fsdp"),
            P(),
            P(),
        ),
        out_specs=(
            P(("dp", "fsdp"), None),
            P(("dp", "fsdp"), None),
            P("fsdp"),
            P("fsdp"),
            P("fsdp", None),
            P("fsdp", None),
            P("fsdp"),
            P("fsdp"),
            P("fsdp", None),
            P("fsdp"),
            P("fsdp", None),
            P(None, "fsdp"),
        ),
        check_vma=False,
    )
```

```python
import jax
import jax.numpy as jnp
from jax import lax
from jax.experimental import pallas as pl
from jax.experimental.pallas import tpu as pltpu
from jax.sharding import PartitionSpec as P

HEADS = 16
HDIM = 64
POS = 50
HIGH_LEN = 145
TILE = 128


highest = lax.Precision.HIGHEST


def layer_norm(hidden, gain, shift):
    centre = hidden - jnp.mean(hidden, axis=-1, keepdims=True)
    spread = jnp.mean(centre * centre, axis=-1, keepdims=True)
    return centre * lax.rsqrt(spread + 1e-06) * gain + shift


def place_rows(rows, low_flag, pos_index, pos_weight):
    offsets = jnp.arange(rows, dtype=jnp.int32)
    table_ids = jnp.arange(POS, dtype=jnp.int32)
    high_ids = jnp.arange(HIGH_LEN, dtype=jnp.int32)
    picks = (pos_index[:, :, None] == table_ids[None, None, :]).astype(jnp.float32)
    interp = jnp.sum(pos_weight[:, :, None] * picks, axis=1)
    low_valid = offsets < rows // POS * POS
    high_valid = offsets < rows // HIGH_LEN * HIGH_LEN
    low_place = (((offsets % POS)[:, None] == table_ids[None, :]) & low_valid[:, None]).astype(
        jnp.float32
    )
    high_pick = (((offsets % HIGH_LEN)[:, None] == high_ids[None, :]) & high_valid[:, None]).astype(
        jnp.float32
    )
    high_place = jnp.dot(high_pick, interp, precision=highest)
    place = jnp.where(low_flag, low_place, high_place)
    valid = jnp.where(low_flag, low_valid, high_valid)
    segment = jnp.where(
        low_flag,
        jnp.where(low_valid, offsets // POS, -1),
        jnp.where(high_valid, offsets // HIGH_LEN, -1),
    )
    return (place, valid, segment)


def key_windows(rows):
    out = []
    for start in range(0, rows, TILE):
        least, most = rows, 0
        for size in (POS, HIGH_LEN):
            used = rows // size * size
            for row in (start, start + TILE - 1):
                image = row // size
                begin = image * size if row < used else used
                end = begin + size if row < used else rows
                least, most = min(least, begin), max(most, end)
        out.append((start, least // TILE * TILE, -(-most // TILE) * TILE))
    return out


def times_t(left, right):
    return lax.dot_general(left, right, (((1,), (1,)), ((), ())), preferred_element_type=jnp.float32)


def t_times(left, right):
    return lax.dot_general(left, right, (((0,), (0,)), ((), ())), preferred_element_type=jnp.float32)


def halves(block, scale=None):
    lane = lax.broadcasted_iota(jnp.int32, block.shape, 1)
    if scale is not None:
        block = block * jnp.asarray(scale, block.dtype)
    zero = jnp.zeros_like(block)
    return (jnp.where(lane < HDIM, block, zero), jnp.where(lane < HDIM, zero, block))


def soft(query, keys, same):
    scores = jnp.where(same, times_t(query, keys), -1e30)
    expo = jnp.exp(scores - jnp.max(scores, axis=-1, keepdims=True))
    return expo * (1.0 / jnp.sum(expo, axis=-1, keepdims=True))


def attend_body(windows, col_ref, row_ref, q_ref, k_ref, v_ref, out_ref):
    values = halves(v_ref[...])
    for start, lo, hi in windows:
        rows = slice(start, start + TILE)
        same = col_ref[rows, :] == row_ref[:, lo:hi]
        keys = k_ref[lo:hi, :]
        total = None
        for query, value in zip(halves(q_ref[rows, :], HDIM ** (-0.5)), values):
            probs = soft(query, keys, same).astype(jnp.bfloat16)
            part = jnp.dot(probs, value[lo:hi], preferred_element_type=jnp.float32)
            total = part if total is None else total + part
        out_ref[rows, :] = total.astype(jnp.bfloat16)


def attend_back_body(windows, col_ref, row_ref, q_ref, k_ref, v_ref, g_ref, out_ref, dk_ref, dv_ref):
    width = q_ref.shape[1]
    full = out_ref.shape[1] // 3
    at = pl.program_id(0) * width
    dk_ref[...] = jnp.zeros_like(dk_ref)
    dv_ref[...] = jnp.zeros_like(dv_ref)
    scaled = halves(k_ref[...], HDIM ** (-0.5))
    for start, lo, hi in windows:
        rows = slice(start, start + TILE)
        same = col_ref[rows, :] == row_ref[:, lo:hi]
        keys = k_ref[lo:hi, :]
        values = v_ref[lo:hi, :]
        total = None
        queries = halves(q_ref[rows, :], HDIM ** (-0.5))
        grads = halves(g_ref[rows, :])
        for query, grad, key in zip(queries, grads, scaled):
            probs = soft(query, keys, same)
            grad_probs = times_t(grad, values)
            centre = jnp.sum(probs * grad_probs, axis=-1, keepdims=True)
            grad_scores = (probs * (grad_probs - centre)).astype(jnp.bfloat16)
            part = jnp.dot(grad_scores, key[lo:hi], preferred_element_type=jnp.float32)
            total = part if total is None else total + part
            dk_ref[lo:hi, :] += t_times(grad_scores, query)
            dv_ref[lo:hi, :] += t_times(probs.astype(jnp.bfloat16), grad)
        out_ref[rows, pl.ds(pl.multiple_of(at, width), width)] = total.astype(jnp.bfloat16)
    out_ref[:, pl.ds(pl.multiple_of(full + at, width), width)] = dk_ref[...].astype(jnp.bfloat16)
    out_ref[:, pl.ds(pl.multiple_of(2 * full + at, width), width)] = dv_ref[...].astype(jnp.bfloat16)


def pair_specs(rows, pairs, start=0):
    pair = 2 * HDIM
    whole = [
        pl.BlockSpec((rows, 1), lambda i: (0, 0)),
        pl.BlockSpec((1, rows), lambda i: (0, 0)),
    ]
    return whole + [
        pl.BlockSpec((rows, pair), lambda i, j=j: (0, j * pairs + start + i)) for j in range(3)
    ]


def attend(projected, segment, start, count):
    rows = projected.shape[0]
    pairs = HEADS // 2
    windows = key_windows(rows)

    def body(*refs):
        attend_body(windows, *refs)

    return pl.pallas_call(
        body,
        grid=(count,),
        in_specs=pair_specs(rows, pairs, start),
        out_specs=pl.BlockSpec((rows, 2 * HDIM), lambda i: (0, i)),
        out_shape=jax.ShapeDtypeStruct((rows, 2 * HDIM * count), jnp.bfloat16),
        name="attend",
    )(segment[:, None], segment[None, :], projected, projected, projected)


def attend_back(projected, grad_attn, segment, start, count):
    rows = projected.shape[0]
    pairs = HEADS // 2
    windows = key_windows(rows)
    wide = 3 * count * 2 * HDIM

    def body(*refs):
        attend_back_body(windows, *refs)

    return pl.pallas_call(
        body,
        grid=(count,),
        in_specs=pair_specs(rows, pairs, start)
        + [pl.BlockSpec((rows, 2 * HDIM), lambda i: (0, start + i))],
        out_specs=pl.BlockSpec((rows, wide), lambda i: (0, 0)),
        out_shape=jax.ShapeDtypeStruct((rows, wide), jnp.bfloat16),
        scratch_shapes=[pltpu.VMEM((rows, 2 * HDIM), jnp.float32)] * 2,
        name="attend_back",
    )(segment[:, None], segment[None, :], projected, projected, projected, grad_attn)


def copies(pairs_of, sems):
    moves = [
        pltpu.make_async_copy(source, target, sems.at[i])
        for i, (source, target) in enumerate(pairs_of)
    ]
    for move in moves:
        move.start()
    for move in moves:
        move.wait()


def assemble(owns, parts, table, n_line, unit):
    n_places = sum(part.shape[0] for part in parts)
    n_own = len(owns)
    n_parts = len(parts)
    ends = []
    for own in owns:
        ends.append((ends[-1] if ends else 0) + own.shape[1])
    count = n_own * (1 + n_places * (n_line - 1))

    def body(table_ref, *refs):
        own_refs = refs[:n_own]
        part_refs = refs[n_own : n_own + n_parts]
        out_refs = refs[n_own + n_parts : 2 * n_own + n_parts]
        sems = refs[-1]
        todo = []
        for own_ref, out_ref, end in zip(own_refs, out_refs, ends):
            shard_rows = own_ref.shape[0]
            columns = pl.ds(end - own_ref.shape[1], own_ref.shape[1])
            first = pl.multiple_of(table_ref[n_places * n_line] * unit, unit)
            todo.append((own_ref, out_ref.at[pl.ds(first, shard_rows), :]))
            place = 0
            for part_ref in part_refs:
                for k in range(part_ref.shape[0]):
                    for step in range(1, n_line):
                        row = pl.multiple_of(table_ref[place * n_line + step] * unit, unit)
                        todo.append(
                            (
                                part_ref.at[k, step - 1, pl.ds(0, unit), columns],
                                out_ref.at[pl.ds(row, unit), :],
                            )
                        )
                    place += 1
        copies(todo, sems)

    anywhere = pl.BlockSpec(memory_space=pl.ANY)
    return pl.pallas_call(
        body,
        in_specs=[pl.BlockSpec(memory_space=pltpu.SMEM)] + [anywhere] * (n_own + n_parts),
        out_specs=[pl.BlockSpec(memory_space=pltpu.VMEM)] * n_own,
        out_shape=[
            jax.ShapeDtypeStruct((own.shape[0] * n_line, own.shape[1]), own.dtype) for own in owns
        ],
        scratch_shapes=[pltpu.SemaphoreType.DMA((count,))],
        name="assemble",
    )(table, *owns, *parts)


def column_order(block, table, unit):
    count = block.shape[1] // unit

    def body(table_ref, in_ref, out_ref):
        for i in range(count):
            column = pl.multiple_of(table_ref[i] * unit, unit)
            out_ref[:, i * unit : (i + 1) * unit] = in_ref[:, pl.ds(column, unit)]

    return pl.pallas_call(
        body,
        in_specs=[
            pl.BlockSpec(memory_space=pltpu.SMEM),
            pl.BlockSpec(memory_space=pltpu.VMEM),
        ],
        out_specs=pl.BlockSpec(memory_space=pltpu.VMEM),
        out_shape=jax.ShapeDtypeStruct(block.shape, block.dtype),
        name="column_order",
    )(table, block)


def finish(parts, owner, cuts):
    unit = parts[0].shape[1]
    n_places = sum(part.shape[0] for part in parts)

    def body(owner_ref, *refs):
        part_refs = refs[: len(parts)]
        out_refs = refs[len(parts) :]
        place = 0
        for part_ref in part_refs:
            for k in range(part_ref.shape[0]):
                row = pl.multiple_of(owner_ref[place] * unit, unit)
                at = 0
                for out_ref, cut in zip(out_refs, cuts):
                    out_ref[pl.ds(row, unit), :] = part_ref[k, :, at : at + cut].astype(jnp.float32)
                    at += cut
                place += 1

    return pl.pallas_call(
        body,
        in_specs=[pl.BlockSpec(memory_space=pltpu.SMEM)]
        + [pl.BlockSpec(memory_space=pltpu.VMEM)] * len(parts),
        out_specs=[pl.BlockSpec(memory_space=pltpu.VMEM)] * len(cuts),
        out_shape=[jax.ShapeDtypeStruct((n_places * unit, cut), jnp.float32) for cut in cuts],
        name="finish",
    )(owner, *parts)


def hop_bit(core, stage, bits):
    return 1 + stage if core == 0 else bits - stage


def hop_pairs(n_dp, stage):
    bits = n_dp.bit_length() - 2
    return [(i, i ^ (1 << hop_bit(i % 2, stage, bits))) for i in range(n_dp)]


def swap_core(block, n_dp):
    return lax.ppermute(block, "dp", [(i, i ^ 1) for i in range(n_dp)])


def ahead(block, n_line, step):
    return lax.ppermute(block, "fsdp", [(i, (i + step) % n_line) for i in range(n_line)])


def plane_hops(block, n_dp):
    across = (1 << n_dp.bit_length() - 1) - 2
    both = [(i, i ^ across) for i in range(n_dp)]
    hops = [hop_pairs(n_dp, stage) for stage in range(n_dp.bit_length() - 2)] + [both]
    return [lax.ppermute(block, "dp", pairs) for pairs in hops]


def add_up(terms):
    total = terms[0].astype(jnp.float32)
    for term in terms[1:]:
        total = total + term.astype(jnp.float32)
    return total


def reduce_steps(grad, n_dp, n_line):
    half = n_dp // 2
    (away,) = yield [grad(half, n_dp).astype(jnp.bfloat16)]
    (got,) = yield [swap_core(away, n_dp)]
    terms = [got]
    half //= 2
    for stage in range(n_dp.bit_length() - 2):
        total = add_up([grad(half, 2 * half)] + [term[half:] for term in terms])
        (send,) = yield [total.astype(jnp.bfloat16)]
        (got,) = yield [lax.ppermute(send, "dp", hop_pairs(n_dp, stage))]
        terms = [term[:half] for term in terms] + [got]
        half //= 2
    total = add_up([grad(0, 1)[0]] + [term[0] for term in terms]).astype(jnp.bfloat16)
    sends = yield [total[step] for step in range(n_line)]
    arrived = yield [ahead(sends[step], n_line, step) for step in range(1, n_line)]
    (near,) = yield [add_up([sends[0]] + arrived).astype(jnp.bfloat16)[None]]
    got = yield plane_hops(near, n_dp)
    (send,) = yield [jnp.concatenate([near] + got)]
    (got,) = yield [swap_core(send, n_dp)]
    return [send, got]


def small_steps(mine, n_dp, n_line):
    (mine,) = yield [mine]
    for bit in range(n_dp.bit_length() - 1):
        pairs = [(i, i ^ (1 << bit)) for i in range(n_dp)]
        (got,) = yield [lax.ppermute(mine, "dp", pairs)]
        (mine,) = yield [mine + got]
    line = lax.axis_index("fsdp")

    def part(step):
        return lax.dynamic_index_in_dim(mine, (line + step) % n_line, 0, keepdims=False)

    arrived = yield [ahead(part(step), n_line, step) for step in range(1, n_line)]
    total = part(0)
    for item in arrived:
        total = total + item
    return [total]


class Reduction:
    def __init__(self, steps, close):
        self.steps = steps
        self.close = close
        self.parts = None
        self.held = None
        self.begin = next(steps)

    def take(self, got):
        try:
            return self.steps.send(got)
        except StopIteration as stop:
            self.parts = stop.value
            return []

    def result(self):
        if self.held is None:
            self.held = self.steps.send(self.begin)
        while self.parts is None:
            sends = self.take(self.held)
            if self.parts is None:
                self.held = self.steps.send(sends)
        return self.close(self.parts)


class Ready:
    def __init__(self, outs):
        self.outs = outs

    def result(self):
        return self.outs


def tick(value, running):
    running = [item for item in running if isinstance(item, Reduction) and item.parts is None]
    old = [item for item in running if item.held is not None]
    value, gots = lax.optimization_barrier((value, [item.held for item in old]))
    sends = [item.take(got) for item, got in zip(old, gots)]
    new = [item for item in running if item.held is None]
    sends = sends + [item.begin for item in new]
    value, sends = lax.optimization_barrier((value, sends))
    for item, send in zip(old + new, sends):
        if item.parts is None:
            item.held = item.steps.send(send)
    return value


def place_of(n_dp, me, flip):
    bits = n_dp.bit_length() - 2
    core = me % 2
    halves = []
    for other in range(2):
        place = jnp.arange(1 << bits, dtype=jnp.int32)
        owner = jnp.full((1 << bits,), me ^ other, jnp.int32)
        for stage in range(bits):
            at = bits - 1 - stage if flip else stage
            low = 1 << hop_bit(0, stage, bits)
            high = 1 << hop_bit(1, stage, bits)
            mask = jnp.where((core ^ other) == 0, low, high)
            owner = owner ^ (((place >> at) & 1) * mask)
        halves.append(owner)
    return jnp.concatenate(halves)


class Wide:
    def __init__(self, shard):
        self.shard = shard

    def gather(self, w_qkv, w_out, w_fc1, w_fc2, smalls):
        def full(matrix):
            return lax.all_gather(matrix, "fsdp", axis=0, tiled=True)

        self.full = [full(w_qkv), full(w_out), full(w_fc1), full(w_fc2)]
        return lax.all_gather(smalls, "fsdp", axis=0)

    def first(self):
        return self.full[0]

    def second(self):
        return self.full[1:3]

    def third(self):
        return self.full[3]

    def pass_one(self, gate):
        return gate

    pass_two = pass_three = pass_one

    def rows(self, block):
        return block

    def wide_columns(self, block):
        return block

    def total(self, left, right):
        grad = t_times(left, right).astype(jnp.bfloat16)
        own = lax.psum_scatter(grad, "fsdp", scatter_dimension=0, tiled=True)
        return Ready(lax.psum(own, "dp").astype(jnp.float32))

    def total_small(self, smalls):
        own = lax.psum_scatter(
            smalls.astype(jnp.bfloat16), "fsdp", scatter_dimension=0, tiled=False
        )
        return Ready(lax.psum(own, "dp").astype(jnp.float32))


class Gather:
    def __init__(self, unit, n_dp, n_line):
        self.n_dp = n_dp
        self.line = [ahead(unit, n_line, step) for step in range(1, n_line)]

    def hop(self, block, stage):
        return lax.ppermute(block, "dp", hop_pairs(self.n_dp, stage))

    def settle(self, gate):
        self.line, gate = lax.optimization_barrier((self.line, gate))
        return gate

    def near(self, gate, columns):
        self.line, gate = lax.optimization_barrier((self.line, gate))
        near = jnp.stack([item[:, :columns] for item in self.line])[None]
        near, gate = lax.optimization_barrier((near, gate))
        self.cores = [swap_core(near, self.n_dp)]
        return (near, gate)

    def fan(self, gate, columns):
        near, gate = self.near(gate, columns)
        self.parts = [near, self.hop(near, 0), self.hop(near, 1)]
        return gate

    def fan_wide(self, gate, columns):
        near, gate = self.near(gate, columns)
        self.parts = [near] + plane_hops(near, self.n_dp)
        return gate

    def close_wide(self, gate):
        late, gate = lax.optimization_barrier((self.parts[1:], gate))
        self.cores += [swap_core(item, self.n_dp) for item in late]
        self.parts = self.parts[:1] + late
        return gate

    def forward(self, gate):
        self.parts[1], gate = lax.optimization_barrier((self.parts[1], gate))
        self.parts.append(self.hop(self.parts[1], 1))
        self.cores.append(swap_core(self.parts[1], self.n_dp))
        return gate

    def close(self, gate):
        late, gate = lax.optimization_barrier((self.parts[2:], gate))
        self.cores += [swap_core(item, self.n_dp) for item in late]
        self.parts = self.parts[:2] + late
        return gate


class Staged:
    def __init__(self, n_dp, n_line, dp, line, width):
        self.n_dp = n_dp
        self.n_line = n_line
        self.dp = dp
        self.line = line
        self.unit = width // n_line // n_dp
        steps = jnp.arange(n_line, dtype=jnp.int32)
        owner = place_of(n_dp, dp, False)
        self.owner = owner
        self.unline = (line - steps) % n_line
        first = line * n_dp
        got = self.unline[None, :] * n_dp + owner[:, None]
        self.got_table = jnp.concatenate([got.reshape(-1), first[None]]).astype(jnp.int32)
        send_line = (line + steps) % n_line
        send = send_line[None, :] * n_dp + place_of(n_dp, dp, True)[:, None]
        self.send_table = send.reshape(-1).astype(jnp.int32)
        natural = jnp.arange(width, dtype=jnp.int32)
        arranged = (
            self.send_table[:, None] * self.unit + jnp.arange(self.unit, dtype=jnp.int32)[None, :]
        ).reshape(-1)
        self.order = (natural[:, None] == arranged[None, :]).astype(jnp.bfloat16)

    def pick(self, shard):
        size = shard.shape[0] // self.n_dp
        return lax.dynamic_slice_in_dim(shard, self.dp * size, size, 0)

    def gather(self, w_qkv, w_out, w_fc1, w_fc2, smalls):
        n_dp = self.n_dp
        n_line = self.n_line
        shard = smalls.shape[1]
        size = self.unit
        wide = w_qkv.shape[1]
        fold = -(-smalls.shape[0] // size)
        padded = jnp.pad(smalls, ((0, size * fold - smalls.shape[0]), (0, 0)))
        packed = [padded[i * size : (i + 1) * size] for i in range(fold)]
        unit_one = jnp.concatenate([self.pick(w_qkv)] + packed, axis=1)
        unit_two = jnp.concatenate([self.pick(w_out), self.pick(w_fc1)], axis=1)
        unit_three = self.pick(w_fc2)
        one = Gather(unit_one, n_dp, n_line)
        unit_two = one.fan(unit_two, wide)
        far = jnp.stack([item[:, wide:] for item in one.line])
        two = Gather(unit_two, n_dp, n_line)
        two.line = one.forward(two.line)
        two.line = one.close(two.line)
        table, unit_three = two.fan_wide((self.got_table, unit_three), unit_two.shape[1])
        three = Gather(unit_three, n_dp, n_line)
        (full_qkv,) = assemble([w_qkv], one.parts + one.cores, table, n_line, size)
        self.one = full_qkv
        self.two = ([w_out, w_fc1], two)
        self.three = (w_fc2, three, unit_three.shape)
        far = jnp.concatenate([far[:, :, i * shard : (i + 1) * shard] for i in range(fold)], axis=1)
        return jnp.take(jnp.concatenate([padded[None], far]), self.unline, axis=0)

    def first(self):
        return self.one

    def pass_one(self, gate):
        return self.three[1].settle(gate)

    def pass_two(self, gate):
        return self.three[1].fan_wide(self.two[1].close_wide(gate), self.three[2][1])

    def pass_three(self, gate):
        return self.three[1].close_wide(gate)

    def second(self):
        owns, got = self.two
        return assemble(owns, got.parts + got.cores, self.got_table, self.n_line, self.unit)

    def third(self):
        own, got, unit = self.three
        return assemble([own], got.parts + got.cores, self.got_table, self.n_line, unit[0])[0]

    def rows(self, block):
        return jnp.dot(block, self.order, preferred_element_type=jnp.float32).astype(jnp.bfloat16)

    def wide_columns(self, block):
        return column_order(block, self.send_table, block.shape[1] // (self.n_dp * self.n_line))

    def total(self, left, right):
        n_dp = self.n_dp
        per = left.shape[1] // n_dp
        owner = self.owner.astype(jnp.int32)

        def grad(first, last):
            out = t_times(left[:, first * per : last * per], right)
            return out.reshape(last - first, self.n_line, -1, right.shape[1])

        steps = reduce_steps(grad, n_dp, self.n_line)
        return Reduction(steps, lambda parts: finish(parts, owner, [right.shape[1]])[0])

    def total_small(self, smalls):
        n_small = smalls.shape[1]
        padded = jnp.pad(smalls, ((0, 0), (0, -n_small % 8), (0, 0)))
        return Reduction(
            small_steps(padded, self.n_dp, self.n_line), lambda parts: parts[0][:n_small]
        )


def per_device(
    patches,
    cotangent,
    ln1_gain,
    ln1_bias,
    w_qkv,
    w_out,
    ln2_gain,
    ln2_bias,
    w_fc1,
    fc1_bias,
    w_fc2,
    pos_table,
    pos_index,
    pos_weight,
):
    bf16 = jnp.bfloat16
    f32 = jnp.float32
    n_dp = lax.axis_size("dp")
    n_line = lax.axis_size("fsdp")
    dp = lax.axis_index("dp")
    line = lax.axis_index("fsdp")
    low_flag = dp < n_dp * 7 // 16
    rows = patches.shape[0]
    width = patches.shape[1]
    shard = width // n_line
    place, valid, segment = place_rows(rows, low_flag, pos_index, pos_weight)
    if n_dp == 8 and n_line <= 4 and shard % (16 * n_dp) == 0:
        plan = Staged(n_dp, n_line, dp, line, width)
    else:
        plan = Wide(shard)
    n_bias = fc1_bias.size // shard
    smalls = jnp.concatenate(
        [
            jnp.stack([ln1_gain, ln1_bias, ln2_gain, ln2_bias]),
            fc1_bias.reshape(-1, shard),
            pos_table,
        ]
    )
    n_small = smalls.shape[0]
    table = plan.gather(w_qkv, w_out, w_fc1, w_fc2, smalls)
    full_qkv = plan.first()

    def across(block):
        return block.transpose(1, 0, 2).reshape(block.shape[1], width).astype(f32)

    gain_one, bias_one, gain_two, bias_two = across(table[:, :4])
    full_bias = table[:, 4 : 4 + n_bias].reshape(-1).astype(f32)
    full_table = across(table[:, 4 + n_bias : n_small])

    hidden_in = patches.astype(f32) + jnp.dot(place, full_table, precision=highest)
    normed_one = layer_norm(hidden_in, gain_one, bias_one).astype(bf16)
    projected = jnp.dot(normed_one, full_qkv, preferred_element_type=f32).astype(bf16)
    half = HEADS // 4
    rows_a = attend(projected, segment, 0, half)
    rows_a, projected = plan.pass_one((rows_a, projected))
    rows_b = attend(projected, segment, half, half)
    attn_rows = plan.pass_two(jnp.concatenate([rows_a, rows_b], axis=1))
    full_out, full_fc1 = plan.second()
    hidden_mid = hidden_in + jnp.dot(attn_rows, full_out, preferred_element_type=f32)
    normed_two = layer_norm(hidden_mid, gain_two, bias_two).astype(bf16)
    pre_act = jnp.dot(normed_two, full_fc1, preferred_element_type=f32) + full_bias
    share = 0.5 * (1.0 + lax.erf(pre_act * 0.5**0.5))
    bell = jnp.exp(-0.5 * pre_act * pre_act) * (0.5 / jnp.pi) ** 0.5
    activated = (pre_act * share).astype(bf16)
    slope = (share + pre_act * bell).astype(bf16)
    grad_out = jnp.where(valid[:, None], cotangent, jnp.zeros_like(cotangent))
    run_fc2 = plan.total(plan.wide_columns(activated), grad_out)
    activated, slope = tick((activated, slope), [run_fc2])
    activated, slope = plan.pass_three((activated, slope))
    full_fc2 = tick(plan.third(), [run_fc2])

    grad_pre = (times_t(grad_out, full_fc2) * slope.astype(f32)).astype(bf16)
    grad_fc1_bias = jnp.sum(grad_pre.astype(f32), axis=0)
    run_fc1 = plan.total(plan.rows(normed_two), grad_pre)
    grad_pre = tick(grad_pre, [run_fc1])
    grad_norm_two = times_t(grad_pre, full_fc1)
    _, pull_two = jax.vjp(layer_norm, hidden_mid, gain_two, bias_two)
    back_mid, grad_gain_two, grad_bias_two = pull_two(grad_norm_two)
    grad_mid = grad_out.astype(f32) + back_mid
    grad_branch = tick(grad_mid.astype(bf16), [run_fc1])
    run_out = plan.total(plan.rows(attn_rows), grad_branch)
    grad_attn = times_t(grad_branch, full_out).astype(bf16)
    grad_attn = tick(grad_attn, [run_out, run_fc2])
    fourth = HEADS // 8
    backs = []
    for group in ([run_out], [run_fc2], [run_fc1, run_out], [run_fc2, run_out]):
        back = attend_back(projected, grad_attn, segment, len(backs) * fourth, fourth)
        back, grad_attn = tick((back, grad_attn), group)
        backs.append(back)
    side = backs[0].shape[1] // 3
    grad_proj = jnp.concatenate(
        [part[:, i * side : (i + 1) * side] for i in range(3) for part in backs], axis=1
    )
    run_qkv = plan.total(plan.rows(normed_one), grad_proj)
    grad_proj = tick(grad_proj, [run_qkv])
    grad_norm_one = tick(times_t(grad_proj, full_qkv), [run_qkv])
    grad_norm_one, activated = tick((grad_norm_one, activated), [run_fc1, run_fc2])
    _, pull_one = jax.vjp(layer_norm, hidden_in, gain_one, bias_one)
    back_in, grad_gain_one, grad_bias_one = pull_one(grad_norm_one)
    grad_in = grad_mid + back_in
    grad_table = jnp.dot(place.T, grad_in, precision=highest)
    branch_out = jnp.dot(activated, full_fc2, preferred_element_type=f32)
    block_out = jnp.where(valid[:, None], hidden_mid + branch_out, 0.0).astype(bf16)
    grad_table, block_out = tick((grad_table, block_out), [run_qkv, run_fc1])

    def split(block):
        return block.reshape(-1, n_line, shard).transpose(1, 0, 2)

    rows_small = jnp.concatenate(
        [
            split(jnp.stack([grad_gain_one, grad_bias_one, grad_gain_two, grad_bias_two])),
            grad_fc1_bias.reshape(n_line, -1, shard),
            split(grad_table),
        ],
        axis=1,
    )
    run_small = plan.total_small(rows_small)
    sum_fc2 = run_fc2.result()
    sum_fc1 = run_fc1.result()
    sum_out = run_out.result()
    sum_qkv = run_qkv.result()
    small = run_small.result()
    return (
        block_out,
        grad_in.astype(bf16),
        small[0],
        small[1],
        sum_qkv,
        sum_out,
        small[2],
        small[3],
        sum_fc1,
        small[4 : 4 + n_bias].reshape(-1),
        sum_fc2,
        small[4 + n_bias :],
    )


def solution(mesh):
    return jax.shard_map(
        per_device,
        mesh=mesh,
        in_specs=(
            P(("dp", "fsdp"), None),
            P(("dp", "fsdp"), None),
            P("fsdp"),
            P("fsdp"),
            P("fsdp", None),
            P("fsdp", None),
            P("fsdp"),
            P("fsdp"),
            P("fsdp", None),
            P("fsdp"),
            P("fsdp", None),
            P(None, "fsdp"),
            P(),
            P(),
        ),
        out_specs=(
            P(("dp", "fsdp"), None),
            P(("dp", "fsdp"), None),
            P("fsdp"),
            P("fsdp"),
            P("fsdp", None),
            P("fsdp", None),
            P("fsdp"),
            P("fsdp"),
            P("fsdp", None),
            P("fsdp"),
            P("fsdp", None),
            P(None, "fsdp"),
        ),
        check_vma=False,
    )
```

```python
import jax
import jax.numpy as jnp
from jax import lax
from jax.experimental import pallas as pl
from jax.experimental.pallas import tpu as pltpu
from jax.sharding import PartitionSpec as P

HEADS = 16
HDIM = 64
POS = 50
HIGH_LEN = 145
TILE = 128


highest = lax.Precision.HIGHEST


def layer_norm(hidden, gain, shift):
    centre = hidden - jnp.mean(hidden, axis=-1, keepdims=True)
    spread = jnp.mean(centre * centre, axis=-1, keepdims=True)
    return centre * lax.rsqrt(spread + 1e-06) * gain + shift


def place_rows(rows, low_flag, pos_index, pos_weight):
    offsets = jnp.arange(rows, dtype=jnp.int32)
    table_ids = jnp.arange(POS, dtype=jnp.int32)
    high_ids = jnp.arange(HIGH_LEN, dtype=jnp.int32)
    picks = (pos_index[:, :, None] == table_ids[None, None, :]).astype(jnp.float32)
    interp = jnp.sum(pos_weight[:, :, None] * picks, axis=1)
    low_valid = offsets < rows // POS * POS
    high_valid = offsets < rows // HIGH_LEN * HIGH_LEN
    low_place = (((offsets % POS)[:, None] == table_ids[None, :]) & low_valid[:, None]).astype(
        jnp.float32
    )
    high_pick = (((offsets % HIGH_LEN)[:, None] == high_ids[None, :]) & high_valid[:, None]).astype(
        jnp.float32
    )
    high_place = jnp.dot(high_pick, interp, precision=highest)
    place = jnp.where(low_flag, low_place, high_place)
    valid = jnp.where(low_flag, low_valid, high_valid)
    segment = jnp.where(
        low_flag,
        jnp.where(low_valid, offsets // POS, -1),
        jnp.where(high_valid, offsets // HIGH_LEN, -1),
    )
    return (place, valid, segment)


def key_windows(rows):
    out = []
    for start in range(0, rows, TILE):
        least, most = rows, 0
        for size in (POS, HIGH_LEN):
            used = rows // size * size
            for row in (start, start + TILE - 1):
                image = row // size
                begin = image * size if row < used else used
                end = begin + size if row < used else rows
                least, most = min(least, begin), max(most, end)
        out.append((start, least // TILE * TILE, -(-most // TILE) * TILE))
    return out


def times_t(left, right):
    return lax.dot_general(left, right, (((1,), (1,)), ((), ())), preferred_element_type=jnp.float32)


def t_times(left, right):
    return lax.dot_general(left, right, (((0,), (0,)), ((), ())), preferred_element_type=jnp.float32)


def halves(block, scale=None):
    lane = lax.broadcasted_iota(jnp.int32, block.shape, 1)
    if scale is not None:
        block = block * jnp.asarray(scale, block.dtype)
    zero = jnp.zeros_like(block)
    return (jnp.where(lane < HDIM, block, zero), jnp.where(lane < HDIM, zero, block))


def soft(query, keys, same):
    scores = jnp.where(same, times_t(query, keys), -1e30)
    expo = jnp.exp(scores - jnp.max(scores, axis=-1, keepdims=True))
    return expo * (1.0 / jnp.sum(expo, axis=-1, keepdims=True))


def attend_body(windows, col_ref, row_ref, q_ref, k_ref, v_ref, out_ref):
    values = halves(v_ref[...])
    for start, lo, hi in windows:
        rows = slice(start, start + TILE)
        same = col_ref[rows, :] == row_ref[:, lo:hi]
        keys = k_ref[lo:hi, :]
        total = None
        for query, value in zip(halves(q_ref[rows, :], HDIM ** (-0.5)), values):
            probs = soft(query, keys, same).astype(jnp.bfloat16)
            part = jnp.dot(probs, value[lo:hi], preferred_element_type=jnp.float32)
            total = part if total is None else total + part
        out_ref[rows, :] = total.astype(jnp.bfloat16)


def attend_back_body(windows, col_ref, row_ref, q_ref, k_ref, v_ref, g_ref, out_ref, dk_ref, dv_ref):
    width = q_ref.shape[1]
    full = out_ref.shape[1] // 3
    at = pl.program_id(0) * width
    dk_ref[...] = jnp.zeros_like(dk_ref)
    dv_ref[...] = jnp.zeros_like(dv_ref)
    scaled = halves(k_ref[...], HDIM ** (-0.5))
    for start, lo, hi in windows:
        rows = slice(start, start + TILE)
        same = col_ref[rows, :] == row_ref[:, lo:hi]
        keys = k_ref[lo:hi, :]
        values = v_ref[lo:hi, :]
        total = None
        queries = halves(q_ref[rows, :], HDIM ** (-0.5))
        grads = halves(g_ref[rows, :])
        for query, grad, key in zip(queries, grads, scaled):
            probs = soft(query, keys, same)
            grad_probs = times_t(grad, values)
            centre = jnp.sum(probs * grad_probs, axis=-1, keepdims=True)
            grad_scores = (probs * (grad_probs - centre)).astype(jnp.bfloat16)
            part = jnp.dot(grad_scores, key[lo:hi], preferred_element_type=jnp.float32)
            total = part if total is None else total + part
            dk_ref[lo:hi, :] += t_times(grad_scores, query)
            dv_ref[lo:hi, :] += t_times(probs.astype(jnp.bfloat16), grad)
        out_ref[rows, pl.ds(pl.multiple_of(at, width), width)] = total.astype(jnp.bfloat16)
    out_ref[:, pl.ds(pl.multiple_of(full + at, width), width)] = dk_ref[...].astype(jnp.bfloat16)
    out_ref[:, pl.ds(pl.multiple_of(2 * full + at, width), width)] = dv_ref[...].astype(jnp.bfloat16)


def pair_specs(rows, pairs, start=0):
    pair = 2 * HDIM
    whole = [
        pl.BlockSpec((rows, 1), lambda i: (0, 0)),
        pl.BlockSpec((1, rows), lambda i: (0, 0)),
    ]
    return whole + [
        pl.BlockSpec((rows, pair), lambda i, j=j: (0, j * pairs + start + i)) for j in range(3)
    ]


def attend(projected, segment, start, count):
    rows = projected.shape[0]
    pairs = HEADS // 2
    windows = key_windows(rows)

    def body(*refs):
        attend_body(windows, *refs)

    return pl.pallas_call(
        body,
        grid=(count,),
        in_specs=pair_specs(rows, pairs, start),
        out_specs=pl.BlockSpec((rows, 2 * HDIM), lambda i: (0, i)),
        out_shape=jax.ShapeDtypeStruct((rows, 2 * HDIM * count), jnp.bfloat16),
        name="attend",
    )(segment[:, None], segment[None, :], projected, projected, projected)


def attend_back(projected, grad_attn, segment, start, count):
    rows = projected.shape[0]
    pairs = HEADS // 2
    windows = key_windows(rows)
    wide = 3 * count * 2 * HDIM

    def body(*refs):
        attend_back_body(windows, *refs)

    return pl.pallas_call(
        body,
        grid=(count,),
        in_specs=pair_specs(rows, pairs, start)
        + [pl.BlockSpec((rows, 2 * HDIM), lambda i: (0, start + i))],
        out_specs=pl.BlockSpec((rows, wide), lambda i: (0, 0)),
        out_shape=jax.ShapeDtypeStruct((rows, wide), jnp.bfloat16),
        scratch_shapes=[pltpu.VMEM((rows, 2 * HDIM), jnp.float32)] * 2,
        name="attend_back",
    )(segment[:, None], segment[None, :], projected, projected, projected, grad_attn)


def copies(pairs_of, sems):
    moves = [
        pltpu.make_async_copy(source, target, sems.at[i])
        for i, (source, target) in enumerate(pairs_of)
    ]
    for move in moves:
        move.start()
    for move in moves:
        move.wait()


def assemble(owns, parts, table, n_line, unit):
    n_places = sum(part.shape[0] for part in parts)
    n_own = len(owns)
    n_parts = len(parts)
    ends = []
    for own in owns:
        ends.append((ends[-1] if ends else 0) + own.shape[1])
    count = n_own * (1 + n_places * (n_line - 1))

    def body(table_ref, *refs):
        own_refs = refs[:n_own]
        part_refs = refs[n_own : n_own + n_parts]
        out_refs = refs[n_own + n_parts : 2 * n_own + n_parts]
        sems = refs[-1]
        todo = []
        for own_ref, out_ref, end in zip(own_refs, out_refs, ends):
            shard_rows = own_ref.shape[0]
            columns = pl.ds(end - own_ref.shape[1], own_ref.shape[1])
            first = pl.multiple_of(table_ref[n_places * n_line] * unit, unit)
            todo.append((own_ref, out_ref.at[pl.ds(first, shard_rows), :]))
            place = 0
            for part_ref in part_refs:
                for k in range(part_ref.shape[0]):
                    for step in range(1, n_line):
                        row = pl.multiple_of(table_ref[place * n_line + step] * unit, unit)
                        todo.append(
                            (
                                part_ref.at[k, step - 1, pl.ds(0, unit), columns],
                                out_ref.at[pl.ds(row, unit), :],
                            )
                        )
                    place += 1
        copies(todo, sems)

    anywhere = pl.BlockSpec(memory_space=pl.ANY)
    return pl.pallas_call(
        body,
        in_specs=[pl.BlockSpec(memory_space=pltpu.SMEM)] + [anywhere] * (n_own + n_parts),
        out_specs=[pl.BlockSpec(memory_space=pltpu.VMEM)] * n_own,
        out_shape=[
            jax.ShapeDtypeStruct((own.shape[0] * n_line, own.shape[1]), own.dtype) for own in owns
        ],
        scratch_shapes=[pltpu.SemaphoreType.DMA((count,))],
        name="assemble",
    )(table, *owns, *parts)


def column_order(block, table, unit):
    count = block.shape[1] // unit

    def body(table_ref, in_ref, out_ref):
        for i in range(count):
            column = pl.multiple_of(table_ref[i] * unit, unit)
            out_ref[:, i * unit : (i + 1) * unit] = in_ref[:, pl.ds(column, unit)]

    return pl.pallas_call(
        body,
        in_specs=[
            pl.BlockSpec(memory_space=pltpu.SMEM),
            pl.BlockSpec(memory_space=pltpu.VMEM),
        ],
        out_specs=pl.BlockSpec(memory_space=pltpu.VMEM),
        out_shape=jax.ShapeDtypeStruct(block.shape, block.dtype),
        name="column_order",
    )(table, block)


def finish(parts, owner, cuts):
    unit = parts[0].shape[1]
    n_places = sum(part.shape[0] for part in parts)

    def body(owner_ref, *refs):
        part_refs = refs[: len(parts)]
        out_refs = refs[len(parts) :]
        place = 0
        for part_ref in part_refs:
            for k in range(part_ref.shape[0]):
                row = pl.multiple_of(owner_ref[place] * unit, unit)
                at = 0
                for out_ref, cut in zip(out_refs, cuts):
                    out_ref[pl.ds(row, unit), :] = part_ref[k, :, at : at + cut].astype(jnp.float32)
                    at += cut
                place += 1

    return pl.pallas_call(
        body,
        in_specs=[pl.BlockSpec(memory_space=pltpu.SMEM)]
        + [pl.BlockSpec(memory_space=pltpu.VMEM)] * len(parts),
        out_specs=[pl.BlockSpec(memory_space=pltpu.VMEM)] * len(cuts),
        out_shape=[jax.ShapeDtypeStruct((n_places * unit, cut), jnp.float32) for cut in cuts],
        name="finish",
    )(owner, *parts)


def hop_bit(core, stage, bits):
    return 1 + stage if core == 0 else bits - stage


def hop_pairs(n_dp, stage):
    bits = n_dp.bit_length() - 2
    return [(i, i ^ (1 << hop_bit(i % 2, stage, bits))) for i in range(n_dp)]


def swap_core(block, n_dp):
    return lax.ppermute(block, "dp", [(i, i ^ 1) for i in range(n_dp)])


def ahead(block, n_line, step):
    return lax.ppermute(block, "fsdp", [(i, (i + step) % n_line) for i in range(n_line)])


def plane_hops(block, n_dp):
    across = (1 << n_dp.bit_length() - 1) - 2
    both = [(i, i ^ across) for i in range(n_dp)]
    hops = [hop_pairs(n_dp, stage) for stage in range(n_dp.bit_length() - 2)] + [both]
    return [lax.ppermute(block, "dp", pairs) for pairs in hops]


def add_up(terms):
    total = terms[0].astype(jnp.float32)
    for term in terms[1:]:
        total = total + term.astype(jnp.float32)
    return total


def reduce_steps(grad, n_dp, n_line):
    half = n_dp // 2
    (away,) = yield [grad(half, n_dp).astype(jnp.bfloat16)]
    (got,) = yield [swap_core(away, n_dp)]
    terms = [got]
    half //= 2
    for stage in range(n_dp.bit_length() - 2):
        total = add_up([grad(half, 2 * half)] + [term[half:] for term in terms])
        (send,) = yield [total.astype(jnp.bfloat16)]
        (got,) = yield [lax.ppermute(send, "dp", hop_pairs(n_dp, stage))]
        terms = [term[:half] for term in terms] + [got]
        half //= 2
    total = add_up([grad(0, 1)[0]] + [term[0] for term in terms]).astype(jnp.bfloat16)
    sends = yield [total[step] for step in range(n_line)]
    arrived = yield [ahead(sends[step], n_line, step) for step in range(1, n_line)]
    (near,) = yield [add_up([sends[0]] + arrived).astype(jnp.bfloat16)[None]]
    got = yield plane_hops(near, n_dp)
    (send,) = yield [jnp.concatenate([near] + got)]
    (got,) = yield [swap_core(send, n_dp)]
    return [send, got]


def small_steps(mine, n_dp, n_line):
    (mine,) = yield [mine]
    for bit in range(n_dp.bit_length() - 1):
        pairs = [(i, i ^ (1 << bit)) for i in range(n_dp)]
        (got,) = yield [lax.ppermute(mine, "dp", pairs)]
        (mine,) = yield [mine + got]
    line = lax.axis_index("fsdp")

    def part(step):
        return lax.dynamic_index_in_dim(mine, (line + step) % n_line, 0, keepdims=False)

    arrived = yield [ahead(part(step), n_line, step) for step in range(1, n_line)]
    total = part(0)
    for item in arrived:
        total = total + item
    return [total]


class Reduction:
    def __init__(self, steps, close):
        self.steps = steps
        self.close = close
        self.parts = None
        self.held = None
        self.begin = next(steps)

    def take(self, got):
        try:
            return self.steps.send(got)
        except StopIteration as stop:
            self.parts = stop.value
            return []

    def result(self):
        if self.held is None:
            self.held = self.steps.send(self.begin)
        while self.parts is None:
            sends = self.take(self.held)
            if self.parts is None:
                self.held = self.steps.send(sends)
        return self.close(self.parts)


class Ready:
    def __init__(self, outs):
        self.outs = outs

    def result(self):
        return self.outs


def tick(value, running):
    running = [item for item in running if isinstance(item, Reduction) and item.parts is None]
    old = [item for item in running if item.held is not None]
    value, gots = lax.optimization_barrier((value, [item.held for item in old]))
    sends = [item.take(got) for item, got in zip(old, gots)]
    new = [item for item in running if item.held is None]
    sends = sends + [item.begin for item in new]
    value, sends = lax.optimization_barrier((value, sends))
    for item, send in zip(old + new, sends):
        if item.parts is None:
            item.held = item.steps.send(send)
    return value


def place_of(n_dp, me, flip):
    bits = n_dp.bit_length() - 2
    core = me % 2
    halves = []
    for other in range(2):
        place = jnp.arange(1 << bits, dtype=jnp.int32)
        owner = jnp.full((1 << bits,), me ^ other, jnp.int32)
        for stage in range(bits):
            at = bits - 1 - stage if flip else stage
            low = 1 << hop_bit(0, stage, bits)
            high = 1 << hop_bit(1, stage, bits)
            mask = jnp.where((core ^ other) == 0, low, high)
            owner = owner ^ (((place >> at) & 1) * mask)
        halves.append(owner)
    return jnp.concatenate(halves)


class Wide:
    def __init__(self, shard):
        self.shard = shard

    def gather(self, w_qkv, w_out, w_fc1, w_fc2, smalls):
        def full(matrix):
            return lax.all_gather(matrix, "fsdp", axis=0, tiled=True)

        self.full = [full(w_qkv), full(w_out), full(w_fc1), full(w_fc2)]
        return lax.all_gather(smalls, "fsdp", axis=0)

    def first(self):
        return self.full[0]

    def second(self):
        return self.full[1:3]

    def third(self):
        return self.full[3]

    def pass_one(self, gate):
        return gate

    pass_two = pass_three = pass_four = pass_five = pass_one

    def rows(self, block):
        return block

    def wide_columns(self, block):
        return block

    def total(self, left, right):
        grad = t_times(left, right).astype(jnp.bfloat16)
        own = lax.psum_scatter(grad, "fsdp", scatter_dimension=0, tiled=True)
        return Ready(lax.psum(own, "dp").astype(jnp.float32))

    def total_small(self, smalls):
        own = lax.psum_scatter(
            smalls.astype(jnp.bfloat16), "fsdp", scatter_dimension=0, tiled=False
        )
        return Ready(lax.psum(own, "dp").astype(jnp.float32))


class Gather:
    def __init__(self, unit, n_dp, n_line):
        self.n_dp = n_dp
        self.line = [ahead(unit, n_line, step) for step in range(1, n_line)]

    def hop(self, block, stage):
        return lax.ppermute(block, "dp", hop_pairs(self.n_dp, stage))

    def near(self, gate, columns):
        self.line, gate = lax.optimization_barrier((self.line, gate))
        near = jnp.stack([item[:, :columns] for item in self.line])[None]
        near, gate = lax.optimization_barrier((near, gate))
        self.cores = [swap_core(near, self.n_dp)]
        return (near, gate)

    def fan(self, gate, columns):
        near, gate = self.near(gate, columns)
        self.parts = [near, self.hop(near, 0), self.hop(near, 1)]
        return gate

    def fan_wide(self, gate, columns):
        near, gate = self.near(gate, columns)
        self.parts = [near] + plane_hops(near, self.n_dp)
        return gate

    def close_wide(self, gate):
        late, gate = lax.optimization_barrier((self.parts[1:], gate))
        self.cores += [swap_core(item, self.n_dp) for item in late]
        self.parts = self.parts[:1] + late
        return gate

    def forward(self, gate):
        self.parts[1], gate = lax.optimization_barrier((self.parts[1], gate))
        self.parts.append(self.hop(self.parts[1], 1))
        self.cores.append(swap_core(self.parts[1], self.n_dp))
        return gate

    def close(self, gate):
        late, gate = lax.optimization_barrier((self.parts[2:], gate))
        self.cores += [swap_core(item, self.n_dp) for item in late]
        self.parts = self.parts[:2] + late
        return gate


class Staged:
    def __init__(self, n_dp, n_line, dp, line, width):
        self.n_dp = n_dp
        self.n_line = n_line
        self.dp = dp
        self.line = line
        self.unit = width // n_line // n_dp
        steps = jnp.arange(n_line, dtype=jnp.int32)
        owner = place_of(n_dp, dp, False)
        self.owner = owner
        self.unline = (line - steps) % n_line
        first = line * n_dp
        got = self.unline[None, :] * n_dp + owner[:, None]
        self.got_table = jnp.concatenate([got.reshape(-1), first[None]]).astype(jnp.int32)
        send_line = (line + steps) % n_line
        send = send_line[None, :] * n_dp + place_of(n_dp, dp, True)[:, None]
        self.send_table = send.reshape(-1).astype(jnp.int32)
        natural = jnp.arange(width, dtype=jnp.int32)
        arranged = (
            self.send_table[:, None] * self.unit + jnp.arange(self.unit, dtype=jnp.int32)[None, :]
        ).reshape(-1)
        self.order = (natural[:, None] == arranged[None, :]).astype(jnp.bfloat16)

    def pick(self, shard):
        size = shard.shape[0] // self.n_dp
        return lax.dynamic_slice_in_dim(shard, self.dp * size, size, 0)

    def gather(self, w_qkv, w_out, w_fc1, w_fc2, smalls):
        n_dp = self.n_dp
        n_line = self.n_line
        shard = smalls.shape[1]
        size = self.unit
        wide = w_qkv.shape[1]
        fold = -(-smalls.shape[0] // size)
        padded = jnp.pad(smalls, ((0, size * fold - smalls.shape[0]), (0, 0)))
        packed = [padded[i * size : (i + 1) * size] for i in range(fold)]
        unit_one = jnp.concatenate([self.pick(w_qkv)] + packed, axis=1)
        unit_two = jnp.concatenate([self.pick(w_out), self.pick(w_fc1)], axis=1)
        unit_three = self.pick(w_fc2)
        one = Gather(unit_one, n_dp, n_line)
        unit_two = one.fan(unit_two, wide)
        far = jnp.stack([item[:, wide:] for item in one.line])
        two = Gather(unit_two, n_dp, n_line)
        two.line = one.forward(two.line)
        two.line = one.close(two.line)
        table = two.fan_wide(self.got_table, unit_two.shape[1])
        (full_qkv,) = assemble([w_qkv], one.parts + one.cores, table, n_line, size)
        self.one = full_qkv
        self.two = ([w_out, w_fc1], two)
        self.w_fc2 = w_fc2
        self.unit_three = unit_three
        far = jnp.concatenate([far[:, :, i * shard : (i + 1) * shard] for i in range(fold)], axis=1)
        return jnp.take(jnp.concatenate([padded[None], far]), self.unline, axis=0)

    def first(self):
        return self.one

    def pass_one(self, gate):
        unit, gate = lax.optimization_barrier((self.unit_three, gate))
        self.three = Gather(unit, self.n_dp, self.n_line)
        return gate

    def pass_two(self, gate):
        return self.two[1].close_wide(gate)

    def pass_three(self, gate):
        return self.three.fan(gate, self.unit_three.shape[1])

    def pass_four(self, gate):
        return self.three.forward(gate)

    def pass_five(self, gate):
        return self.three.close(gate)

    def second(self):
        owns, got = self.two
        return assemble(owns, got.parts + got.cores, self.got_table, self.n_line, self.unit)

    def third(self):
        got = self.three
        return assemble(
            [self.w_fc2], got.parts + got.cores, self.got_table, self.n_line, self.unit_three.shape[0]
        )[0]

    def rows(self, block):
        return jnp.dot(block, self.order, preferred_element_type=jnp.float32).astype(jnp.bfloat16)

    def wide_columns(self, block):
        return column_order(block, self.send_table, block.shape[1] // (self.n_dp * self.n_line))

    def total(self, left, right):
        n_dp = self.n_dp
        per = left.shape[1] // n_dp
        owner = self.owner.astype(jnp.int32)

        def grad(first, last):
            out = t_times(left[:, first * per : last * per], right)
            return out.reshape(last - first, self.n_line, -1, right.shape[1])

        steps = reduce_steps(grad, n_dp, self.n_line)
        return Reduction(steps, lambda parts: finish(parts, owner, [right.shape[1]])[0])

    def total_small(self, smalls):
        n_small = smalls.shape[1]
        padded = jnp.pad(smalls, ((0, 0), (0, -n_small % 8), (0, 0)))
        return Reduction(
            small_steps(padded, self.n_dp, self.n_line), lambda parts: parts[0][:n_small]
        )


def per_device(
    patches,
    cotangent,
    ln1_gain,
    ln1_bias,
    w_qkv,
    w_out,
    ln2_gain,
    ln2_bias,
    w_fc1,
    fc1_bias,
    w_fc2,
    pos_table,
    pos_index,
    pos_weight,
):
    bf16 = jnp.bfloat16
    f32 = jnp.float32
    n_dp = lax.axis_size("dp")
    n_line = lax.axis_size("fsdp")
    dp = lax.axis_index("dp")
    line = lax.axis_index("fsdp")
    low_flag = dp < n_dp * 7 // 16
    rows = patches.shape[0]
    width = patches.shape[1]
    shard = width // n_line
    place, valid, segment = place_rows(rows, low_flag, pos_index, pos_weight)
    if n_dp == 8 and n_line <= 4 and shard % (16 * n_dp) == 0:
        plan = Staged(n_dp, n_line, dp, line, width)
    else:
        plan = Wide(shard)
    n_bias = fc1_bias.size // shard
    smalls = jnp.concatenate(
        [
            jnp.stack([ln1_gain, ln1_bias, ln2_gain, ln2_bias]),
            fc1_bias.reshape(-1, shard),
            pos_table,
        ]
    )
    n_small = smalls.shape[0]
    table = plan.gather(w_qkv, w_out, w_fc1, w_fc2, smalls)
    full_qkv = plan.first()

    def across(block):
        return block.transpose(1, 0, 2).reshape(block.shape[1], width).astype(f32)

    gain_one, bias_one, gain_two, bias_two = across(table[:, :4])
    full_bias = table[:, 4 : 4 + n_bias].reshape(-1).astype(f32)
    full_table = across(table[:, 4 + n_bias : n_small])

    hidden_in = patches.astype(f32) + jnp.dot(place, full_table, precision=highest)
    normed_one = layer_norm(hidden_in, gain_one, bias_one).astype(bf16)
    projected = jnp.dot(normed_one, full_qkv, preferred_element_type=f32).astype(bf16)
    half = HEADS // 4
    projected = plan.pass_one(projected)
    attn_rows = plan.pass_two(attend(projected, segment, 0, 2 * half))
    full_out, full_fc1 = plan.second()
    attn_rows, full_out = plan.pass_three((attn_rows, full_out))
    hidden_mid = hidden_in + jnp.dot(attn_rows, full_out, preferred_element_type=f32)
    normed_two = layer_norm(hidden_mid, gain_two, bias_two).astype(bf16)
    normed_two = plan.pass_four(normed_two)
    pre_act = jnp.dot(normed_two, full_fc1, preferred_element_type=f32) + full_bias
    share = 0.5 * (1.0 + lax.erf(pre_act * 0.5**0.5))
    bell = jnp.exp(-0.5 * pre_act * pre_act) * (0.5 / jnp.pi) ** 0.5
    activated = (pre_act * share).astype(bf16)
    slope = (share + pre_act * bell).astype(bf16)
    activated, slope = plan.pass_five((activated, slope))
    grad_out = jnp.where(valid[:, None], cotangent, jnp.zeros_like(cotangent))
    run_fc2 = plan.total(plan.wide_columns(activated), grad_out)
    activated, slope = tick((activated, slope), [run_fc2])
    full_fc2 = tick(plan.third(), [run_fc2])

    grad_pre = (times_t(grad_out, full_fc2) * slope.astype(f32)).astype(bf16)
    grad_fc1_bias = jnp.sum(grad_pre.astype(f32), axis=0)
    run_fc1 = plan.total(plan.rows(normed_two), grad_pre)
    grad_pre = tick(grad_pre, [run_fc1])
    grad_norm_two = times_t(grad_pre, full_fc1)
    _, pull_two = jax.vjp(layer_norm, hidden_mid, gain_two, bias_two)
    back_mid, grad_gain_two, grad_bias_two = pull_two(grad_norm_two)
    grad_mid = grad_out.astype(f32) + back_mid
    grad_branch = tick(grad_mid.astype(bf16), [run_fc1])
    run_out = plan.total(plan.rows(attn_rows), grad_branch)
    grad_attn = times_t(grad_branch, full_out).astype(bf16)
    grad_attn = tick(grad_attn, [run_out, run_fc2])
    fourth = HEADS // 8
    backs = []
    every = [run_fc2, run_fc1, run_out]
    for group in ([run_out], [], every, every):
        back = attend_back(projected, grad_attn, segment, len(backs) * fourth, fourth)
        back, grad_attn = tick((back, grad_attn), group)
        backs.append(back)
    side = backs[0].shape[1] // 3
    grad_proj = jnp.concatenate(
        [part[:, i * side : (i + 1) * side] for i in range(3) for part in backs], axis=1
    )
    run_qkv = plan.total(plan.rows(normed_one), grad_proj)
    grad_proj = tick(grad_proj, [run_qkv])
    grad_norm_one = tick(times_t(grad_proj, full_qkv), [run_qkv])
    _, pull_one = jax.vjp(layer_norm, hidden_in, gain_one, bias_one)
    back_in, grad_gain_one, grad_bias_one = pull_one(grad_norm_one)
    grad_in = grad_mid + back_in
    grad_table = jnp.dot(place.T, grad_in, precision=highest)
    grad_table, activated = tick((grad_table, activated), [run_qkv] + every)
    branch_out = jnp.dot(activated, full_fc2, preferred_element_type=f32)
    block_out = jnp.where(valid[:, None], hidden_mid + branch_out, 0.0).astype(bf16)
    block_out = tick(block_out, [run_qkv] + every)

    def split(block):
        return block.reshape(-1, n_line, shard).transpose(1, 0, 2)

    rows_small = jnp.concatenate(
        [
            split(jnp.stack([grad_gain_one, grad_bias_one, grad_gain_two, grad_bias_two])),
            grad_fc1_bias.reshape(n_line, -1, shard),
            split(grad_table),
        ],
        axis=1,
    )
    run_small = plan.total_small(rows_small)
    sum_fc2 = run_fc2.result()
    sum_fc1 = run_fc1.result()
    sum_out = run_out.result()
    sum_qkv = run_qkv.result()
    small = run_small.result()
    return (
        block_out,
        grad_in.astype(bf16),
        small[0],
        small[1],
        sum_qkv,
        sum_out,
        small[2],
        small[3],
        sum_fc1,
        small[4 : 4 + n_bias].reshape(-1),
        sum_fc2,
        small[4 + n_bias :],
    )


def solution(mesh):
    return jax.shard_map(
        per_device,
        mesh=mesh,
        in_specs=(
            P(("dp", "fsdp"), None),
            P(("dp", "fsdp"), None),
            P("fsdp"),
            P("fsdp"),
            P("fsdp", None),
            P("fsdp", None),
            P("fsdp"),
            P("fsdp"),
            P("fsdp", None),
            P("fsdp"),
            P("fsdp", None),
            P(None, "fsdp"),
            P(),
            P(),
        ),
        out_specs=(
            P(("dp", "fsdp"), None),
            P(("dp", "fsdp"), None),
            P("fsdp"),
            P("fsdp"),
            P("fsdp", None),
            P("fsdp", None),
            P("fsdp"),
            P("fsdp"),
            P("fsdp", None),
            P("fsdp"),
            P("fsdp", None),
            P(None, "fsdp"),
        ),
        check_vma=False,
    )
```

```python
import jax
import jax.numpy as jnp
from jax import lax
from jax.experimental import pallas as pl
from jax.experimental.pallas import tpu as pltpu
from jax.sharding import PartitionSpec as P

HEADS = 16
HDIM = 64
POS = 50
HIGH_LEN = 145
TILE = 128


highest = lax.Precision.HIGHEST


def layer_norm(hidden, gain, shift):
    centre = hidden - jnp.mean(hidden, axis=-1, keepdims=True)
    spread = jnp.mean(centre * centre, axis=-1, keepdims=True)
    return centre * lax.rsqrt(spread + 1e-06) * gain + shift


def place_rows(rows, low_flag, pos_index, pos_weight):
    offsets = jnp.arange(rows, dtype=jnp.int32)
    table_ids = jnp.arange(POS, dtype=jnp.int32)
    high_ids = jnp.arange(HIGH_LEN, dtype=jnp.int32)
    picks = (pos_index[:, :, None] == table_ids[None, None, :]).astype(jnp.float32)
    interp = jnp.sum(pos_weight[:, :, None] * picks, axis=1)
    low_valid = offsets < rows // POS * POS
    high_valid = offsets < rows // HIGH_LEN * HIGH_LEN
    low_place = (((offsets % POS)[:, None] == table_ids[None, :]) & low_valid[:, None]).astype(
        jnp.float32
    )
    high_pick = (((offsets % HIGH_LEN)[:, None] == high_ids[None, :]) & high_valid[:, None]).astype(
        jnp.float32
    )
    high_place = jnp.dot(high_pick, interp, precision=highest)
    place = jnp.where(low_flag, low_place, high_place)
    valid = jnp.where(low_flag, low_valid, high_valid)
    segment = jnp.where(
        low_flag,
        jnp.where(low_valid, offsets // POS, -1),
        jnp.where(high_valid, offsets // HIGH_LEN, -1),
    )
    return (place, valid, segment)


def key_windows(rows):
    out = []
    for start in range(0, rows, TILE):
        least, most = rows, 0
        for size in (POS, HIGH_LEN):
            used = rows // size * size
            for row in (start, start + TILE - 1):
                image = row // size
                begin = image * size if row < used else used
                end = begin + size if row < used else rows
                least, most = min(least, begin), max(most, end)
        out.append((start, least // TILE * TILE, -(-most // TILE) * TILE))
    return out


def times_t(left, right):
    return lax.dot_general(left, right, (((1,), (1,)), ((), ())), preferred_element_type=jnp.float32)


def t_times(left, right):
    return lax.dot_general(left, right, (((0,), (0,)), ((), ())), preferred_element_type=jnp.float32)


def halves(block, scale=None):
    lane = lax.broadcasted_iota(jnp.int32, block.shape, 1)
    if scale is not None:
        block = block * jnp.asarray(scale, block.dtype)
    zero = jnp.zeros_like(block)
    return (jnp.where(lane < HDIM, block, zero), jnp.where(lane < HDIM, zero, block))


def soft(query, keys, same):
    scores = jnp.where(same, times_t(query, keys), -1e30)
    expo = jnp.exp(scores - jnp.max(scores, axis=-1, keepdims=True))
    return expo * (1.0 / jnp.sum(expo, axis=-1, keepdims=True))


def attend_body(windows, col_ref, row_ref, q_ref, k_ref, v_ref, out_ref):
    values = halves(v_ref[...])
    for start, lo, hi in windows:
        rows = slice(start, start + TILE)
        same = col_ref[rows, :] == row_ref[:, lo:hi]
        keys = k_ref[lo:hi, :]
        total = None
        for query, value in zip(halves(q_ref[rows, :], HDIM ** (-0.5)), values):
            probs = soft(query, keys, same).astype(jnp.bfloat16)
            part = jnp.dot(probs, value[lo:hi], preferred_element_type=jnp.float32)
            total = part if total is None else total + part
        out_ref[rows, :] = total.astype(jnp.bfloat16)


def attend_back_body(windows, col_ref, row_ref, q_ref, k_ref, v_ref, g_ref, out_ref, dk_ref, dv_ref):
    width = q_ref.shape[1]
    full = out_ref.shape[1] // 3
    at = pl.program_id(0) * width
    dk_ref[...] = jnp.zeros_like(dk_ref)
    dv_ref[...] = jnp.zeros_like(dv_ref)
    scaled = halves(k_ref[...], HDIM ** (-0.5))
    for start, lo, hi in windows:
        rows = slice(start, start + TILE)
        same = col_ref[rows, :] == row_ref[:, lo:hi]
        keys = k_ref[lo:hi, :]
        values = v_ref[lo:hi, :]
        total = None
        queries = halves(q_ref[rows, :], HDIM ** (-0.5))
        grads = halves(g_ref[rows, :])
        for query, grad, key in zip(queries, grads, scaled):
            probs = soft(query, keys, same)
            grad_probs = times_t(grad, values)
            centre = jnp.sum(probs * grad_probs, axis=-1, keepdims=True)
            grad_scores = (probs * (grad_probs - centre)).astype(jnp.bfloat16)
            part = jnp.dot(grad_scores, key[lo:hi], preferred_element_type=jnp.float32)
            total = part if total is None else total + part
            dk_ref[lo:hi, :] += t_times(grad_scores, query)
            dv_ref[lo:hi, :] += t_times(probs.astype(jnp.bfloat16), grad)
        out_ref[rows, pl.ds(pl.multiple_of(at, width), width)] = total.astype(jnp.bfloat16)
    out_ref[:, pl.ds(pl.multiple_of(full + at, width), width)] = dk_ref[...].astype(jnp.bfloat16)
    out_ref[:, pl.ds(pl.multiple_of(2 * full + at, width), width)] = dv_ref[...].astype(jnp.bfloat16)


def pair_specs(rows, pairs, start=0):
    pair = 2 * HDIM
    whole = [
        pl.BlockSpec((rows, 1), lambda i: (0, 0)),
        pl.BlockSpec((1, rows), lambda i: (0, 0)),
    ]
    return whole + [
        pl.BlockSpec((rows, pair), lambda i, j=j: (0, j * pairs + start + i)) for j in range(3)
    ]


def attend(projected, segment):
    rows = projected.shape[0]
    pairs = HEADS // 2
    windows = key_windows(rows)

    def body(*refs):
        attend_body(windows, *refs)

    return pl.pallas_call(
        body,
        grid=(pairs,),
        in_specs=pair_specs(rows, pairs),
        out_specs=pl.BlockSpec((rows, 2 * HDIM), lambda i: (0, i)),
        out_shape=jax.ShapeDtypeStruct((rows, HEADS * HDIM), jnp.bfloat16),
        name="attend",
    )(segment[:, None], segment[None, :], projected, projected, projected)


def attend_back(projected, grad_attn, segment, start, count):
    rows = projected.shape[0]
    pairs = HEADS // 2
    windows = key_windows(rows)
    wide = 3 * count * 2 * HDIM

    def body(*refs):
        attend_back_body(windows, *refs)

    return pl.pallas_call(
        body,
        grid=(count,),
        in_specs=pair_specs(rows, pairs, start)
        + [pl.BlockSpec((rows, 2 * HDIM), lambda i: (0, start + i))],
        out_specs=pl.BlockSpec((rows, wide), lambda i: (0, 0)),
        out_shape=jax.ShapeDtypeStruct((rows, wide), jnp.bfloat16),
        scratch_shapes=[pltpu.VMEM((rows, 2 * HDIM), jnp.float32)] * 2,
        name="attend_back",
    )(segment[:, None], segment[None, :], projected, projected, projected, grad_attn)


def copies(pairs_of, sems):
    moves = [
        pltpu.make_async_copy(source, target, sems.at[i])
        for i, (source, target) in enumerate(pairs_of)
    ]
    for move in moves:
        move.start()
    for move in moves:
        move.wait()


def assemble(owns, parts, table, n_line, unit):
    n_places = sum(part.shape[0] for part in parts)
    n_own = len(owns)
    n_parts = len(parts)
    ends = []
    for own in owns:
        ends.append((ends[-1] if ends else 0) + own.shape[1])
    count = n_own * (1 + n_places * (n_line - 1))

    def body(table_ref, *refs):
        own_refs = refs[:n_own]
        part_refs = refs[n_own : n_own + n_parts]
        out_refs = refs[n_own + n_parts : 2 * n_own + n_parts]
        sems = refs[-1]
        todo = []
        for own_ref, out_ref, end in zip(own_refs, out_refs, ends):
            shard_rows = own_ref.shape[0]
            columns = pl.ds(end - own_ref.shape[1], own_ref.shape[1])
            first = pl.multiple_of(table_ref[n_places * n_line] * unit, unit)
            todo.append((own_ref, out_ref.at[pl.ds(first, shard_rows), :]))
            place = 0
            for part_ref in part_refs:
                for k in range(part_ref.shape[0]):
                    for step in range(1, n_line):
                        row = pl.multiple_of(table_ref[place * n_line + step] * unit, unit)
                        todo.append(
                            (
                                part_ref.at[k, step - 1, pl.ds(0, unit), columns],
                                out_ref.at[pl.ds(row, unit), :],
                            )
                        )
                    place += 1
        copies(todo, sems)

    anywhere = pl.BlockSpec(memory_space=pl.ANY)
    return pl.pallas_call(
        body,
        in_specs=[pl.BlockSpec(memory_space=pltpu.SMEM)] + [anywhere] * (n_own + n_parts),
        out_specs=[pl.BlockSpec(memory_space=pltpu.VMEM)] * n_own,
        out_shape=[
            jax.ShapeDtypeStruct((own.shape[0] * n_line, own.shape[1]), own.dtype) for own in owns
        ],
        scratch_shapes=[pltpu.SemaphoreType.DMA((count,))],
        name="assemble",
    )(table, *owns, *parts)


def column_order(block, table, unit):
    count = block.shape[1] // unit

    def body(table_ref, in_ref, out_ref):
        for i in range(count):
            column = pl.multiple_of(table_ref[i] * unit, unit)
            out_ref[:, i * unit : (i + 1) * unit] = in_ref[:, pl.ds(column, unit)]

    return pl.pallas_call(
        body,
        in_specs=[
            pl.BlockSpec(memory_space=pltpu.SMEM),
            pl.BlockSpec(memory_space=pltpu.VMEM),
        ],
        out_specs=pl.BlockSpec(memory_space=pltpu.VMEM),
        out_shape=jax.ShapeDtypeStruct(block.shape, block.dtype),
        name="column_order",
    )(table, block)


def finish(parts, owner, cuts):
    unit = parts[0].shape[1]
    n_places = sum(part.shape[0] for part in parts)

    def body(owner_ref, *refs):
        part_refs = refs[: len(parts)]
        out_refs = refs[len(parts) :]
        place = 0
        for part_ref in part_refs:
            for k in range(part_ref.shape[0]):
                row = pl.multiple_of(owner_ref[place] * unit, unit)
                at = 0
                for out_ref, cut in zip(out_refs, cuts):
                    out_ref[pl.ds(row, unit), :] = part_ref[k, :, at : at + cut].astype(jnp.float32)
                    at += cut
                place += 1

    return pl.pallas_call(
        body,
        in_specs=[pl.BlockSpec(memory_space=pltpu.SMEM)]
        + [pl.BlockSpec(memory_space=pltpu.VMEM)] * len(parts),
        out_specs=[pl.BlockSpec(memory_space=pltpu.VMEM)] * len(cuts),
        out_shape=[jax.ShapeDtypeStruct((n_places * unit, cut), jnp.float32) for cut in cuts],
        name="finish",
    )(owner, *parts)


def hop_bit(core, stage, bits):
    return 1 + stage if core == 0 else bits - stage


def hop_pairs(n_dp, stage):
    bits = n_dp.bit_length() - 2
    return [(i, i ^ (1 << hop_bit(i % 2, stage, bits))) for i in range(n_dp)]


def swap_core(block, n_dp):
    return lax.ppermute(block, "dp", [(i, i ^ 1) for i in range(n_dp)])


def ahead(block, n_line, step):
    return lax.ppermute(block, "fsdp", [(i, (i + step) % n_line) for i in range(n_line)])


def plane_hops(block, n_dp):
    across = (1 << n_dp.bit_length() - 1) - 2
    both = [(i, i ^ across) for i in range(n_dp)]
    hops = [hop_pairs(n_dp, stage) for stage in range(n_dp.bit_length() - 2)] + [both]
    return [lax.ppermute(block, "dp", pairs) for pairs in hops]


def add_up(terms):
    total = terms[0].astype(jnp.float32)
    for term in terms[1:]:
        total = total + term.astype(jnp.float32)
    return total


def reduce_steps(away, keep, n_dp, n_line):
    (away,) = yield [away]
    (got,) = yield [swap_core(away, n_dp)]
    terms = [keep, got]
    half = keep.shape[0] // 2
    for stage in range(n_dp.bit_length() - 2):
        (send,) = yield [add_up([term[half:] for term in terms]).astype(jnp.bfloat16)]
        (got,) = yield [lax.ppermute(send, "dp", hop_pairs(n_dp, stage))]
        terms = [term[:half] for term in terms] + [got]
        half //= 2
    terms = [term[0] for term in terms]
    sends = yield [
        add_up([term[step] for term in terms]).astype(jnp.bfloat16) for step in range(1, n_line)
    ]
    arrived = yield [ahead(send, n_line, step + 1) for step, send in enumerate(sends)]
    total = add_up([term[0] for term in terms] + arrived)
    (near,) = yield [total.astype(jnp.bfloat16)[None]]
    got = yield plane_hops(near, n_dp)
    (send,) = yield [jnp.concatenate([near] + got)]
    (got,) = yield [swap_core(send, n_dp)]
    return [send, got]


def small_steps(mine, n_dp, n_line):
    (mine,) = yield [mine]
    for bit in range(n_dp.bit_length() - 1):
        pairs = [(i, i ^ (1 << bit)) for i in range(n_dp)]
        (got,) = yield [lax.ppermute(mine, "dp", pairs)]
        (mine,) = yield [mine + got]
    line = lax.axis_index("fsdp")

    def part(step):
        return lax.dynamic_index_in_dim(mine, (line + step) % n_line, 0, keepdims=False)

    arrived = yield [ahead(part(step), n_line, step) for step in range(1, n_line)]
    total = part(0)
    for item in arrived:
        total = total + item
    return [total]


class Reduction:
    def __init__(self, steps, close):
        self.steps = steps
        self.close = close
        self.parts = None
        self.held = None
        self.begin = next(steps)

    def take(self, got):
        try:
            return self.steps.send(got)
        except StopIteration as stop:
            self.parts = stop.value
            return []

    def result(self):
        if self.held is None:
            self.held = self.steps.send(self.begin)
        while self.parts is None:
            sends = self.take(self.held)
            if self.parts is None:
                self.held = self.steps.send(sends)
        return self.close(self.parts)


class Ready:
    def __init__(self, outs):
        self.outs = outs

    def result(self):
        return self.outs


def tick(value, running):
    running = [item for item in running if isinstance(item, Reduction) and item.parts is None]
    old = [item for item in running if item.held is not None]
    value, gots = lax.optimization_barrier((value, [item.held for item in old]))
    sends = [item.take(got) for item, got in zip(old, gots)]
    new = [item for item in running if item.held is None]
    sends = sends + [item.begin for item in new]
    value, sends = lax.optimization_barrier((value, sends))
    for item, send in zip(old + new, sends):
        if item.parts is None:
            item.held = item.steps.send(send)
    return value


def place_of(n_dp, me, flip):
    bits = n_dp.bit_length() - 2
    core = me % 2
    halves = []
    for other in range(2):
        place = jnp.arange(1 << bits, dtype=jnp.int32)
        owner = jnp.full((1 << bits,), me ^ other, jnp.int32)
        for stage in range(bits):
            at = bits - 1 - stage if flip else stage
            low = 1 << hop_bit(0, stage, bits)
            high = 1 << hop_bit(1, stage, bits)
            mask = jnp.where((core ^ other) == 0, low, high)
            owner = owner ^ (((place >> at) & 1) * mask)
        halves.append(owner)
    return jnp.concatenate(halves)


class Wide:
    def __init__(self, shard):
        self.shard = shard

    def gather(self, w_qkv, w_out, w_fc1, w_fc2, smalls):
        def full(matrix):
            return lax.all_gather(matrix, "fsdp", axis=0, tiled=True)

        self.full = [full(w_qkv), full(w_out), full(w_fc1), full(w_fc2)]
        return lax.all_gather(smalls, "fsdp", axis=0)

    def first(self):
        return self.full[:2]

    def second(self):
        return self.full[2]

    def third(self):
        return self.full[3]

    def pass_one(self, gate):
        return gate

    pass_two = pass_three = pass_four = pass_one

    def rows(self, block):
        return block

    def wide_columns(self, block):
        return block

    def total(self, terms):
        bf16 = jnp.bfloat16
        outs = []
        for left, right in terms:
            grad = t_times(left, right).astype(bf16)
            own = lax.psum_scatter(grad, "fsdp", scatter_dimension=0, tiled=True)
            outs.append(lax.psum(own, "dp").astype(jnp.float32))
        return Ready(outs)

    def total_small(self, smalls):
        own = lax.psum_scatter(
            smalls.astype(jnp.bfloat16), "fsdp", scatter_dimension=0, tiled=False
        )
        return Ready(lax.psum(own, "dp").astype(jnp.float32))


class Gather:
    def __init__(self, unit, n_dp, n_line):
        self.n_dp = n_dp
        self.line = [ahead(unit, n_line, step) for step in range(1, n_line)]

    def hop(self, block, stage):
        return lax.ppermute(block, "dp", hop_pairs(self.n_dp, stage))

    def fan(self, gate, columns):
        self.line, gate = lax.optimization_barrier((self.line, gate))
        near = jnp.stack([item[:, :columns] for item in self.line])[None]
        near, gate = lax.optimization_barrier((near, gate))
        self.parts = [near, self.hop(near, 0), self.hop(near, 1)]
        self.cores = [swap_core(near, self.n_dp)]
        return gate

    def forward(self, gate):
        self.parts[1], gate = lax.optimization_barrier((self.parts[1], gate))
        self.parts.append(self.hop(self.parts[1], 1))
        self.cores.append(swap_core(self.parts[1], self.n_dp))
        return gate

    def close(self, gate):
        late, gate = lax.optimization_barrier((self.parts[2:], gate))
        self.cores += [swap_core(item, self.n_dp) for item in late]
        self.parts = self.parts[:2] + late
        return gate


class Staged:
    def __init__(self, n_dp, n_line, dp, line, width):
        self.n_dp = n_dp
        self.n_line = n_line
        self.dp = dp
        self.line = line
        self.unit = width // n_line // n_dp
        steps = jnp.arange(n_line, dtype=jnp.int32)
        owner = place_of(n_dp, dp, False)
        self.owner = owner
        self.unline = (line - steps) % n_line
        first = line * n_dp
        got = self.unline[None, :] * n_dp + owner[:, None]
        self.got_table = jnp.concatenate([got.reshape(-1), first[None]]).astype(jnp.int32)
        send_line = (line + steps) % n_line
        send = send_line[None, :] * n_dp + place_of(n_dp, dp, True)[:, None]
        self.send_table = send.reshape(-1).astype(jnp.int32)
        natural = jnp.arange(width, dtype=jnp.int32)
        arranged = (
            self.send_table[:, None] * self.unit + jnp.arange(self.unit, dtype=jnp.int32)[None, :]
        ).reshape(-1)
        self.order = (natural[:, None] == arranged[None, :]).astype(jnp.bfloat16)

    def pick(self, shard):
        size = shard.shape[0] // self.n_dp
        return lax.dynamic_slice_in_dim(shard, self.dp * size, size, 0)

    def gather(self, w_qkv, w_out, w_fc1, w_fc2, smalls):
        n_dp = self.n_dp
        n_line = self.n_line
        shard = smalls.shape[1]
        size = self.unit
        wide = w_qkv.shape[1] + w_out.shape[1]
        fold = -(-smalls.shape[0] // size)
        padded = jnp.pad(smalls, ((0, size * fold - smalls.shape[0]), (0, 0)))
        packed = [padded[i * size : (i + 1) * size] for i in range(fold)]
        unit_one = jnp.concatenate([self.pick(w_qkv), self.pick(w_out)] + packed, axis=1)
        unit_two, unit_three = (self.pick(w_fc1), self.pick(w_fc2))
        one = Gather(unit_one, n_dp, n_line)
        unit_two = one.fan(unit_two, wide)
        far = jnp.stack([item[:, wide:] for item in one.line])
        two = Gather(unit_two, n_dp, n_line)
        two.line = one.forward(two.line)
        two.line = one.close(two.line)
        table, unit_three = two.fan((self.got_table, unit_three), unit_two.shape[1])
        three = Gather(unit_three, n_dp, n_line)
        full_qkv, full_out = assemble([w_qkv, w_out], one.parts + one.cores, table, n_line, size)
        self.one = (full_qkv, full_out)
        self.two = (w_fc1, two)
        self.three = (w_fc2, three, unit_three.shape)
        far = jnp.concatenate([far[:, :, i * shard : (i + 1) * shard] for i in range(fold)], axis=1)
        return jnp.take(jnp.concatenate([padded[None], far]), self.unline, axis=0)

    def first(self):
        return self.one

    def pass_one(self, gate):
        return self.two[1].forward(gate)

    def pass_two(self, gate):
        return self.three[1].fan(self.two[1].close(gate), self.three[2][1])

    def pass_three(self, gate):
        return self.three[1].forward(gate)

    def pass_four(self, gate):
        return self.three[1].close(gate)

    def second(self):
        own, got = self.two
        return assemble([own], got.parts + got.cores, self.got_table, self.n_line, self.unit)[0]

    def third(self):
        own, got, unit = self.three
        return assemble([own], got.parts + got.cores, self.got_table, self.n_line, unit[0])[0]

    def rows(self, block):
        return jnp.dot(block, self.order, preferred_element_type=jnp.float32).astype(jnp.bfloat16)

    def wide_columns(self, block):
        return column_order(block, self.send_table, block.shape[1] // (self.n_dp * self.n_line))

    def total(self, terms):
        n_dp = self.n_dp
        n_line = self.n_line
        sides = []
        for side in (1, 0):
            grads = []
            for left, right in terms:
                half = left.shape[1] // 2
                grad = t_times(left[:, side * half : (side + 1) * half], right).astype(jnp.bfloat16)
                grads.append(grad.reshape(n_dp // 2, n_line, -1, right.shape[1]))
            sides.append(jnp.concatenate(grads, axis=3) if len(grads) > 1 else grads[0])
        cuts = [right.shape[1] for left, right in terms]
        owner = self.owner.astype(jnp.int32)
        steps = reduce_steps(sides[0], sides[1], n_dp, n_line)
        return Reduction(steps, lambda parts: list(finish(parts, owner, cuts)))

    def total_small(self, smalls):
        n_small = smalls.shape[1]
        padded = jnp.pad(smalls, ((0, 0), (0, -n_small % 8), (0, 0)))
        return Reduction(
            small_steps(padded, self.n_dp, self.n_line), lambda parts: parts[0][:n_small]
        )


def per_device(
    patches,
    cotangent,
    ln1_gain,
    ln1_bias,
    w_qkv,
    w_out,
    ln2_gain,
    ln2_bias,
    w_fc1,
    fc1_bias,
    w_fc2,
    pos_table,
    pos_index,
    pos_weight,
):
    bf16 = jnp.bfloat16
    f32 = jnp.float32
    n_dp = lax.axis_size("dp")
    n_line = lax.axis_size("fsdp")
    dp = lax.axis_index("dp")
    line = lax.axis_index("fsdp")
    low_flag = dp < n_dp * 7 // 16
    rows = patches.shape[0]
    width = patches.shape[1]
    shard = width // n_line
    place, valid, segment = place_rows(rows, low_flag, pos_index, pos_weight)
    if n_dp == 8 and n_line <= 4 and shard % (16 * n_dp) == 0:
        plan = Staged(n_dp, n_line, dp, line, width)
    else:
        plan = Wide(shard)
    n_bias = fc1_bias.size // shard
    smalls = jnp.concatenate(
        [
            jnp.stack([ln1_gain, ln1_bias, ln2_gain, ln2_bias]),
            fc1_bias.reshape(-1, shard),
            pos_table,
        ]
    )
    n_small = smalls.shape[0]
    table = plan.gather(w_qkv, w_out, w_fc1, w_fc2, smalls)
    full_qkv, full_out = plan.first()

    def across(block):
        return block.transpose(1, 0, 2).reshape(block.shape[1], width).astype(f32)

    gain_one, bias_one, gain_two, bias_two = across(table[:, :4])
    full_bias = table[:, 4 : 4 + n_bias].reshape(-1).astype(f32)
    full_table = across(table[:, 4 + n_bias : n_small])

    hidden_in = patches.astype(f32) + jnp.dot(place, full_table, precision=highest)
    normed_one = layer_norm(hidden_in, gain_one, bias_one).astype(bf16)
    projected = jnp.dot(normed_one, full_qkv, preferred_element_type=f32).astype(bf16)
    projected = plan.pass_one(projected)
    attn_rows = plan.pass_two(attend(projected, segment))
    hidden_mid = hidden_in + jnp.dot(attn_rows, full_out, preferred_element_type=f32)
    normed_two = layer_norm(hidden_mid, gain_two, bias_two).astype(bf16)
    normed_two = plan.pass_three(normed_two)
    full_fc1 = plan.second()
    pre_act = jnp.dot(normed_two, full_fc1, preferred_element_type=f32) + full_bias
    share = 0.5 * (1.0 + lax.erf(pre_act * 0.5**0.5))
    bell = jnp.exp(-0.5 * pre_act * pre_act) * (0.5 / jnp.pi) ** 0.5
    activated = (pre_act * share).astype(bf16)
    slope = (share + pre_act * bell).astype(bf16)
    activated = plan.pass_four(activated)
    grad_out = jnp.where(valid[:, None], cotangent, jnp.zeros_like(cotangent))
    run_fc2 = plan.total([(plan.wide_columns(activated), grad_out)])
    activated = tick(activated, [run_fc2])
    full_fc2, activated = tick((plan.third(), activated), [run_fc2])

    grad_pre = (times_t(grad_out, full_fc2) * slope.astype(f32)).astype(bf16)
    grad_fc1_bias = jnp.sum(grad_pre.astype(f32), axis=0)
    run_fc1 = plan.total([(plan.rows(normed_two), grad_pre)])
    grad_pre = tick(grad_pre, [run_fc1])
    grad_norm_two = times_t(grad_pre, full_fc1)
    _, pull_two = jax.vjp(layer_norm, hidden_mid, gain_two, bias_two)
    back_mid, grad_gain_two, grad_bias_two = pull_two(grad_norm_two)
    grad_mid = grad_out.astype(f32) + back_mid
    grad_branch = tick(grad_mid.astype(bf16), [run_fc1])
    run_out = plan.total([(plan.rows(attn_rows), grad_branch)])
    grad_attn = times_t(grad_branch, full_out).astype(bf16)
    grad_attn = tick(grad_attn, [run_fc2, run_out])
    half = HEADS // 4
    back_a = attend_back(projected, grad_attn, segment, 0, half)
    back_a, grad_attn = tick((back_a, grad_attn), [run_fc2, run_fc1, run_out])
    back_b = attend_back(projected, grad_attn, segment, half, half)
    back_a, back_b = tick((back_a, back_b), [run_fc2, run_fc1, run_out])
    side = back_a.shape[1] // 3
    grad_proj = jnp.concatenate(
        [part[:, i * side : (i + 1) * side] for i in range(3) for part in (back_a, back_b)], axis=1
    )
    run_qkv = plan.total([(plan.rows(normed_one), grad_proj)])
    grad_proj = tick(grad_proj, [run_qkv])
    grad_norm_one = tick(times_t(grad_proj, full_qkv), [run_qkv])
    _, pull_one = jax.vjp(layer_norm, hidden_in, gain_one, bias_one)
    back_in, grad_gain_one, grad_bias_one = pull_one(grad_norm_one)
    grad_in = grad_mid + back_in
    grad_table = jnp.dot(place.T, grad_in, precision=highest)
    grad_table, activated = tick((grad_table, activated), [run_qkv])
    branch_out = jnp.dot(activated, full_fc2, preferred_element_type=f32)
    block_out = jnp.where(valid[:, None], hidden_mid + branch_out, 0.0).astype(bf16)
    block_out = tick(block_out, [run_qkv, run_fc2, run_fc1, run_out])

    def split(block):
        return block.reshape(-1, n_line, shard).transpose(1, 0, 2)

    rows_small = jnp.concatenate(
        [
            split(jnp.stack([grad_gain_one, grad_bias_one, grad_gain_two, grad_bias_two])),
            grad_fc1_bias.reshape(n_line, -1, shard),
            split(grad_table),
        ],
        axis=1,
    )
    run_small = plan.total_small(rows_small)
    (sum_fc2,) = run_fc2.result()
    (sum_fc1,) = run_fc1.result()
    (sum_out,) = run_out.result()
    (sum_qkv,) = run_qkv.result()
    small = run_small.result()
    return (
        block_out,
        grad_in.astype(bf16),
        small[0],
        small[1],
        sum_qkv,
        sum_out,
        small[2],
        small[3],
        sum_fc1,
        small[4 : 4 + n_bias].reshape(-1),
        sum_fc2,
        small[4 + n_bias :],
    )


def solution(mesh):
    return jax.shard_map(
        per_device,
        mesh=mesh,
        in_specs=(
            P(("dp", "fsdp"), None),
            P(("dp", "fsdp"), None),
            P("fsdp"),
            P("fsdp"),
            P("fsdp", None),
            P("fsdp", None),
            P("fsdp"),
            P("fsdp"),
            P("fsdp", None),
            P("fsdp"),
            P("fsdp", None),
            P(None, "fsdp"),
            P(),
            P(),
        ),
        out_specs=(
            P(("dp", "fsdp"), None),
            P(("dp", "fsdp"), None),
            P("fsdp"),
            P("fsdp"),
            P("fsdp", None),
            P("fsdp", None),
            P("fsdp"),
            P("fsdp"),
            P("fsdp", None),
            P("fsdp"),
            P("fsdp", None),
            P(None, "fsdp"),
        ),
        check_vma=False,
    )
```

```python
import jax
import jax.numpy as jnp
from jax import lax
from jax.experimental import pallas as pl
from jax.experimental.pallas import tpu as pltpu
from jax.sharding import PartitionSpec as P

HEADS = 16
HDIM = 64
POS = 50
HIGH_LEN = 145
TILE = 128


highest = lax.Precision.HIGHEST


def layer_norm(hidden, gain, shift):
    centre = hidden - jnp.mean(hidden, axis=-1, keepdims=True)
    spread = jnp.mean(centre * centre, axis=-1, keepdims=True)
    return centre * lax.rsqrt(spread + 1e-06) * gain + shift


def place_rows(rows, low_flag, pos_index, pos_weight):
    offsets = jnp.arange(rows, dtype=jnp.int32)
    table_ids = jnp.arange(POS, dtype=jnp.int32)
    high_ids = jnp.arange(HIGH_LEN, dtype=jnp.int32)
    picks = (pos_index[:, :, None] == table_ids[None, None, :]).astype(jnp.float32)
    interp = jnp.sum(pos_weight[:, :, None] * picks, axis=1)
    low_valid = offsets < rows // POS * POS
    high_valid = offsets < rows // HIGH_LEN * HIGH_LEN
    low_place = (((offsets % POS)[:, None] == table_ids[None, :]) & low_valid[:, None]).astype(
        jnp.float32
    )
    high_pick = (((offsets % HIGH_LEN)[:, None] == high_ids[None, :]) & high_valid[:, None]).astype(
        jnp.float32
    )
    high_place = jnp.dot(high_pick, interp, precision=highest)
    place = jnp.where(low_flag, low_place, high_place)
    valid = jnp.where(low_flag, low_valid, high_valid)
    segment = jnp.where(
        low_flag,
        jnp.where(low_valid, offsets // POS, -1),
        jnp.where(high_valid, offsets // HIGH_LEN, -1),
    )
    return (place, valid, segment)


def key_windows(rows):
    out = []
    for start in range(0, rows, TILE):
        least, most = rows, 0
        for size in (POS, HIGH_LEN):
            used = rows // size * size
            for row in (start, start + TILE - 1):
                image = row // size
                begin = image * size if row < used else used
                end = begin + size if row < used else rows
                least, most = min(least, begin), max(most, end)
        out.append((start, least // TILE * TILE, -(-most // TILE) * TILE))
    return out


def times_t(left, right):
    return lax.dot_general(left, right, (((1,), (1,)), ((), ())), preferred_element_type=jnp.float32)


def t_times(left, right):
    return lax.dot_general(left, right, (((0,), (0,)), ((), ())), preferred_element_type=jnp.float32)


def halves(block, scale=None):
    lane = lax.broadcasted_iota(jnp.int32, block.shape, 1)
    if scale is not None:
        block = block * jnp.asarray(scale, block.dtype)
    zero = jnp.zeros_like(block)
    return (jnp.where(lane < HDIM, block, zero), jnp.where(lane < HDIM, zero, block))


def soft(query, keys, same):
    scores = jnp.where(same, times_t(query, keys), -1e30)
    expo = jnp.exp(scores - jnp.max(scores, axis=-1, keepdims=True))
    return expo * (1.0 / jnp.sum(expo, axis=-1, keepdims=True))


def attend_body(windows, col_ref, row_ref, q_ref, k_ref, v_ref, out_ref):
    values = halves(v_ref[...])
    for start, lo, hi in windows:
        rows = slice(start, start + TILE)
        same = col_ref[rows, :] == row_ref[:, lo:hi]
        keys = k_ref[lo:hi, :]
        total = None
        for query, value in zip(halves(q_ref[rows, :], HDIM ** (-0.5)), values):
            probs = soft(query, keys, same).astype(jnp.bfloat16)
            part = jnp.dot(probs, value[lo:hi], preferred_element_type=jnp.float32)
            total = part if total is None else total + part
        out_ref[rows, :] = total.astype(jnp.bfloat16)


def attend_back_body(windows, col_ref, row_ref, q_ref, k_ref, v_ref, g_ref, out_ref, dk_ref, dv_ref):
    width = q_ref.shape[1]
    full = out_ref.shape[1] // 3
    at = pl.program_id(0) * width
    dk_ref[...] = jnp.zeros_like(dk_ref)
    dv_ref[...] = jnp.zeros_like(dv_ref)
    scaled = halves(k_ref[...], HDIM ** (-0.5))
    for start, lo, hi in windows:
        rows = slice(start, start + TILE)
        same = col_ref[rows, :] == row_ref[:, lo:hi]
        keys = k_ref[lo:hi, :]
        values = v_ref[lo:hi, :]
        total = None
        queries = halves(q_ref[rows, :], HDIM ** (-0.5))
        grads = halves(g_ref[rows, :])
        for query, grad, key in zip(queries, grads, scaled):
            probs = soft(query, keys, same)
            grad_probs = times_t(grad, values)
            centre = jnp.sum(probs * grad_probs, axis=-1, keepdims=True)
            grad_scores = (probs * (grad_probs - centre)).astype(jnp.bfloat16)
            part = jnp.dot(grad_scores, key[lo:hi], preferred_element_type=jnp.float32)
            total = part if total is None else total + part
            dk_ref[lo:hi, :] += t_times(grad_scores, query)
            dv_ref[lo:hi, :] += t_times(probs.astype(jnp.bfloat16), grad)
        out_ref[rows, pl.ds(pl.multiple_of(at, width), width)] = total.astype(jnp.bfloat16)
    out_ref[:, pl.ds(pl.multiple_of(full + at, width), width)] = dk_ref[...].astype(jnp.bfloat16)
    out_ref[:, pl.ds(pl.multiple_of(2 * full + at, width), width)] = dv_ref[...].astype(jnp.bfloat16)


def pair_specs(rows, pairs, start=0):
    pair = 2 * HDIM
    whole = [
        pl.BlockSpec((rows, 1), lambda i: (0, 0)),
        pl.BlockSpec((1, rows), lambda i: (0, 0)),
    ]
    return whole + [
        pl.BlockSpec((rows, pair), lambda i, j=j: (0, j * pairs + start + i)) for j in range(3)
    ]


def attend(projected, segment):
    rows = projected.shape[0]
    pairs = HEADS // 2
    windows = key_windows(rows)

    def body(*refs):
        attend_body(windows, *refs)

    return pl.pallas_call(
        body,
        grid=(pairs,),
        in_specs=pair_specs(rows, pairs),
        out_specs=pl.BlockSpec((rows, 2 * HDIM), lambda i: (0, i)),
        out_shape=jax.ShapeDtypeStruct((rows, HEADS * HDIM), jnp.bfloat16),
        name="attend",
    )(segment[:, None], segment[None, :], projected, projected, projected)


def attend_back(projected, grad_attn, segment, start, count):
    rows = projected.shape[0]
    pairs = HEADS // 2
    windows = key_windows(rows)
    wide = 3 * count * 2 * HDIM

    def body(*refs):
        attend_back_body(windows, *refs)

    return pl.pallas_call(
        body,
        grid=(count,),
        in_specs=pair_specs(rows, pairs, start)
        + [pl.BlockSpec((rows, 2 * HDIM), lambda i: (0, start + i))],
        out_specs=pl.BlockSpec((rows, wide), lambda i: (0, 0)),
        out_shape=jax.ShapeDtypeStruct((rows, wide), jnp.bfloat16),
        scratch_shapes=[pltpu.VMEM((rows, 2 * HDIM), jnp.float32)] * 2,
        name="attend_back",
    )(segment[:, None], segment[None, :], projected, projected, projected, grad_attn)


def copies(pairs_of, sems):
    moves = [
        pltpu.make_async_copy(source, target, sems.at[i])
        for i, (source, target) in enumerate(pairs_of)
    ]
    for move in moves:
        move.start()
    for move in moves:
        move.wait()


def assemble(owns, parts, table, n_line, unit):
    n_places = sum(part.shape[0] for part in parts)
    n_own = len(owns)
    n_parts = len(parts)
    ends = []
    for own in owns:
        ends.append((ends[-1] if ends else 0) + own.shape[1])
    count = n_own * (1 + n_places * (n_line - 1))

    def body(table_ref, *refs):
        own_refs = refs[:n_own]
        part_refs = refs[n_own : n_own + n_parts]
        out_refs = refs[n_own + n_parts : 2 * n_own + n_parts]
        sems = refs[-1]
        todo = []
        for own_ref, out_ref, end in zip(own_refs, out_refs, ends):
            shard_rows = own_ref.shape[0]
            columns = pl.ds(end - own_ref.shape[1], own_ref.shape[1])
            first = pl.multiple_of(table_ref[n_places * n_line] * unit, unit)
            todo.append((own_ref, out_ref.at[pl.ds(first, shard_rows), :]))
            place = 0
            for part_ref in part_refs:
                for k in range(part_ref.shape[0]):
                    for step in range(1, n_line):
                        row = pl.multiple_of(table_ref[place * n_line + step] * unit, unit)
                        todo.append(
                            (
                                part_ref.at[k, step - 1, pl.ds(0, unit), columns],
                                out_ref.at[pl.ds(row, unit), :],
                            )
                        )
                    place += 1
        copies(todo, sems)

    anywhere = pl.BlockSpec(memory_space=pl.ANY)
    return pl.pallas_call(
        body,
        in_specs=[pl.BlockSpec(memory_space=pltpu.SMEM)] + [anywhere] * (n_own + n_parts),
        out_specs=[pl.BlockSpec(memory_space=pltpu.VMEM)] * n_own,
        out_shape=[
            jax.ShapeDtypeStruct((own.shape[0] * n_line, own.shape[1]), own.dtype) for own in owns
        ],
        scratch_shapes=[pltpu.SemaphoreType.DMA((count,))],
        name="assemble",
    )(table, *owns, *parts)


def column_order(block, table, unit):
    count = block.shape[1] // unit

    def body(table_ref, in_ref, out_ref):
        for i in range(count):
            column = pl.multiple_of(table_ref[i] * unit, unit)
            out_ref[:, i * unit : (i + 1) * unit] = in_ref[:, pl.ds(column, unit)]

    return pl.pallas_call(
        body,
        in_specs=[
            pl.BlockSpec(memory_space=pltpu.SMEM),
            pl.BlockSpec(memory_space=pltpu.VMEM),
        ],
        out_specs=pl.BlockSpec(memory_space=pltpu.VMEM),
        out_shape=jax.ShapeDtypeStruct(block.shape, block.dtype),
        name="column_order",
    )(table, block)


def finish(parts, owner, cuts):
    unit = parts[0].shape[1]
    n_places = sum(part.shape[0] for part in parts)

    def body(owner_ref, *refs):
        part_refs = refs[: len(parts)]
        out_refs = refs[len(parts) :]
        place = 0
        for part_ref in part_refs:
            for k in range(part_ref.shape[0]):
                row = pl.multiple_of(owner_ref[place] * unit, unit)
                at = 0
                for out_ref, cut in zip(out_refs, cuts):
                    out_ref[pl.ds(row, unit), :] = part_ref[k, :, at : at + cut].astype(jnp.float32)
                    at += cut
                place += 1

    return pl.pallas_call(
        body,
        in_specs=[pl.BlockSpec(memory_space=pltpu.SMEM)]
        + [pl.BlockSpec(memory_space=pltpu.VMEM)] * len(parts),
        out_specs=[pl.BlockSpec(memory_space=pltpu.VMEM)] * len(cuts),
        out_shape=[jax.ShapeDtypeStruct((n_places * unit, cut), jnp.float32) for cut in cuts],
        name="finish",
    )(owner, *parts)


def hop_bit(core, stage, bits):
    return 1 + stage if core == 0 else bits - stage


def hop_pairs(n_dp, stage):
    bits = n_dp.bit_length() - 2
    return [(i, i ^ (1 << hop_bit(i % 2, stage, bits))) for i in range(n_dp)]


def swap_core(block, n_dp):
    return lax.ppermute(block, "dp", [(i, i ^ 1) for i in range(n_dp)])


def ahead(block, n_line, step):
    return lax.ppermute(block, "fsdp", [(i, (i + step) % n_line) for i in range(n_line)])


def plane_hops(block, n_dp):
    across = (1 << n_dp.bit_length() - 1) - 2
    both = [(i, i ^ across) for i in range(n_dp)]
    hops = [hop_pairs(n_dp, stage) for stage in range(n_dp.bit_length() - 2)] + [both]
    return [lax.ppermute(block, "dp", pairs) for pairs in hops]


def add_up(terms):
    total = terms[0].astype(jnp.float32)
    for term in terms[1:]:
        total = total + term.astype(jnp.float32)
    return total


def reduce_steps(away, keep, n_dp, n_line):
    (away,) = yield [away]
    (got,) = yield [swap_core(away, n_dp)]
    terms = [keep, got]
    half = keep.shape[0] // 2
    for stage in range(n_dp.bit_length() - 2):
        (send,) = yield [add_up([term[half:] for term in terms]).astype(jnp.bfloat16)]
        (got,) = yield [lax.ppermute(send, "dp", hop_pairs(n_dp, stage))]
        terms = [term[:half] for term in terms] + [got]
        half //= 2
    terms = [term[0] for term in terms]
    sends = yield [
        add_up([term[step] for term in terms]).astype(jnp.bfloat16) for step in range(1, n_line)
    ]
    arrived = yield [ahead(send, n_line, step + 1) for step, send in enumerate(sends)]
    total = add_up([term[0] for term in terms] + arrived)
    (near,) = yield [total.astype(jnp.bfloat16)[None]]
    got = yield plane_hops(near, n_dp)
    (send,) = yield [jnp.concatenate([near] + got)]
    (got,) = yield [swap_core(send, n_dp)]
    return [send, got]


def small_steps(mine, n_dp, n_line):
    (mine,) = yield [mine]
    for bit in range(n_dp.bit_length() - 1):
        pairs = [(i, i ^ (1 << bit)) for i in range(n_dp)]
        (got,) = yield [lax.ppermute(mine, "dp", pairs)]
        (mine,) = yield [mine + got]
    line = lax.axis_index("fsdp")

    def part(step):
        return lax.dynamic_index_in_dim(mine, (line + step) % n_line, 0, keepdims=False)

    arrived = yield [ahead(part(step), n_line, step) for step in range(1, n_line)]
    total = part(0)
    for item in arrived:
        total = total + item
    return [total]


class Reduction:
    def __init__(self, steps, close):
        self.steps = steps
        self.close = close
        self.parts = None
        self.held = None
        self.begin = next(steps)

    def take(self, got):
        try:
            return self.steps.send(got)
        except StopIteration as stop:
            self.parts = stop.value
            return []

    def result(self):
        if self.held is None:
            self.held = self.steps.send(self.begin)
        while self.parts is None:
            sends = self.take(self.held)
            if self.parts is None:
                self.held = self.steps.send(sends)
        return self.close(self.parts)


class Ready:
    def __init__(self, outs):
        self.outs = outs

    def result(self):
        return self.outs


def tick(value, running):
    running = [item for item in running if isinstance(item, Reduction) and item.parts is None]
    old = [item for item in running if item.held is not None]
    value, gots = lax.optimization_barrier((value, [item.held for item in old]))
    sends = [item.take(got) for item, got in zip(old, gots)]
    new = [item for item in running if item.held is None]
    sends = sends + [item.begin for item in new]
    value, sends = lax.optimization_barrier((value, sends))
    for item, send in zip(old + new, sends):
        if item.parts is None:
            item.held = item.steps.send(send)
    return value


def place_of(n_dp, me, flip):
    bits = n_dp.bit_length() - 2
    core = me % 2
    halves = []
    for other in range(2):
        place = jnp.arange(1 << bits, dtype=jnp.int32)
        owner = jnp.full((1 << bits,), me ^ other, jnp.int32)
        for stage in range(bits):
            at = bits - 1 - stage if flip else stage
            low = 1 << hop_bit(0, stage, bits)
            high = 1 << hop_bit(1, stage, bits)
            mask = jnp.where((core ^ other) == 0, low, high)
            owner = owner ^ (((place >> at) & 1) * mask)
        halves.append(owner)
    return jnp.concatenate(halves)


class Wide:
    def __init__(self, shard):
        self.shard = shard

    def gather(self, w_qkv, w_out, w_fc1, w_fc2, smalls):
        def full(matrix):
            return lax.all_gather(matrix, "fsdp", axis=0, tiled=True)

        self.full = [full(w_qkv), full(w_out), full(w_fc1), full(w_fc2)]
        return lax.all_gather(smalls, "fsdp", axis=0)

    def first(self):
        return self.full[:2]

    def second(self):
        return self.full[2]

    def third(self):
        return self.full[3]

    def pass_one(self, gate):
        return gate

    pass_two = pass_three = pass_four = pass_one

    def rows(self, block):
        return block

    def wide_columns(self, block):
        return block

    def total(self, terms):
        bf16 = jnp.bfloat16
        outs = []
        for left, right in terms:
            grad = t_times(left, right).astype(bf16)
            own = lax.psum_scatter(grad, "fsdp", scatter_dimension=0, tiled=True)
            outs.append(lax.psum(own, "dp").astype(jnp.float32))
        return Ready(outs)

    def total_small(self, smalls):
        own = lax.psum_scatter(
            smalls.astype(jnp.bfloat16), "fsdp", scatter_dimension=0, tiled=False
        )
        return Ready(lax.psum(own, "dp").astype(jnp.float32))


class Gather:
    def __init__(self, unit, n_dp, n_line):
        self.n_dp = n_dp
        self.line = [ahead(unit, n_line, step) for step in range(1, n_line)]

    def hop(self, block, stage):
        return lax.ppermute(block, "dp", hop_pairs(self.n_dp, stage))

    def fan(self, gate, columns):
        self.line, gate = lax.optimization_barrier((self.line, gate))
        near = jnp.stack([item[:, :columns] for item in self.line])[None]
        near, gate = lax.optimization_barrier((near, gate))
        self.parts = [near, self.hop(near, 0), self.hop(near, 1)]
        self.cores = [swap_core(near, self.n_dp)]
        return gate

    def forward(self, gate):
        self.parts[1], gate = lax.optimization_barrier((self.parts[1], gate))
        self.parts.append(self.hop(self.parts[1], 1))
        self.cores.append(swap_core(self.parts[1], self.n_dp))
        return gate

    def close(self, gate):
        late, gate = lax.optimization_barrier((self.parts[2:], gate))
        self.cores += [swap_core(item, self.n_dp) for item in late]
        self.parts = self.parts[:2] + late
        return gate


class Staged:
    def __init__(self, n_dp, n_line, dp, line, width):
        self.n_dp = n_dp
        self.n_line = n_line
        self.dp = dp
        self.line = line
        self.unit = width // n_line // n_dp
        steps = jnp.arange(n_line, dtype=jnp.int32)
        owner = place_of(n_dp, dp, False)
        self.owner = owner
        self.unline = (line - steps) % n_line
        first = line * n_dp
        got = self.unline[None, :] * n_dp + owner[:, None]
        self.got_table = jnp.concatenate([got.reshape(-1), first[None]]).astype(jnp.int32)
        send_line = (line + steps) % n_line
        send = send_line[None, :] * n_dp + place_of(n_dp, dp, True)[:, None]
        self.send_table = send.reshape(-1).astype(jnp.int32)
        natural = jnp.arange(width, dtype=jnp.int32)
        arranged = (
            self.send_table[:, None] * self.unit + jnp.arange(self.unit, dtype=jnp.int32)[None, :]
        ).reshape(-1)
        self.order = (natural[:, None] == arranged[None, :]).astype(jnp.bfloat16)

    def pick(self, shard):
        size = shard.shape[0] // self.n_dp
        return lax.dynamic_slice_in_dim(shard, self.dp * size, size, 0)

    def gather(self, w_qkv, w_out, w_fc1, w_fc2, smalls):
        n_dp = self.n_dp
        n_line = self.n_line
        shard = smalls.shape[1]
        size = self.unit
        wide = w_qkv.shape[1] + w_out.shape[1]
        fold = -(-smalls.shape[0] // size)
        padded = jnp.pad(smalls, ((0, size * fold - smalls.shape[0]), (0, 0)))
        packed = [padded[i * size : (i + 1) * size] for i in range(fold)]
        unit_one = jnp.concatenate([self.pick(w_qkv), self.pick(w_out)] + packed, axis=1)
        unit_two, unit_three = (self.pick(w_fc1), self.pick(w_fc2))
        one = Gather(unit_one, n_dp, n_line)
        unit_two = one.fan(unit_two, wide)
        far = jnp.stack([item[:, wide:] for item in one.line])
        two = Gather(unit_two, n_dp, n_line)
        two.line = one.forward(two.line)
        two.line = one.close(two.line)
        table, unit_three = two.fan((self.got_table, unit_three), unit_two.shape[1])
        three = Gather(unit_three, n_dp, n_line)
        full_qkv, full_out = assemble([w_qkv, w_out], one.parts + one.cores, table, n_line, size)
        self.one = (full_qkv, full_out)
        self.two = (w_fc1, two)
        self.three = (w_fc2, three, unit_three.shape)
        far = jnp.concatenate([far[:, :, i * shard : (i + 1) * shard] for i in range(fold)], axis=1)
        return jnp.take(jnp.concatenate([padded[None], far]), self.unline, axis=0)

    def first(self):
        return self.one

    def pass_one(self, gate):
        return self.two[1].forward(gate)

    def pass_two(self, gate):
        return self.three[1].fan(self.two[1].close(gate), self.three[2][1])

    def pass_three(self, gate):
        return self.three[1].forward(gate)

    def pass_four(self, gate):
        return self.three[1].close(gate)

    def second(self):
        own, got = self.two
        return assemble([own], got.parts + got.cores, self.got_table, self.n_line, self.unit)[0]

    def third(self):
        own, got, unit = self.three
        return assemble([own], got.parts + got.cores, self.got_table, self.n_line, unit[0])[0]

    def rows(self, block):
        return jnp.dot(block, self.order, preferred_element_type=jnp.float32).astype(jnp.bfloat16)

    def wide_columns(self, block):
        return column_order(block, self.send_table, block.shape[1] // (self.n_dp * self.n_line))

    def total(self, terms):
        n_dp = self.n_dp
        n_line = self.n_line
        sides = []
        for side in (1, 0):
            grads = []
            for left, right in terms:
                half = left.shape[1] // 2
                grad = t_times(left[:, side * half : (side + 1) * half], right).astype(jnp.bfloat16)
                grads.append(grad.reshape(n_dp // 2, n_line, -1, right.shape[1]))
            sides.append(jnp.concatenate(grads, axis=3) if len(grads) > 1 else grads[0])
        cuts = [right.shape[1] for left, right in terms]
        owner = self.owner.astype(jnp.int32)
        steps = reduce_steps(sides[0], sides[1], n_dp, n_line)
        return Reduction(steps, lambda parts: list(finish(parts, owner, cuts)))

    def total_small(self, smalls):
        n_small = smalls.shape[1]
        padded = jnp.pad(smalls, ((0, 0), (0, -n_small % 8), (0, 0)))
        return Reduction(
            small_steps(padded, self.n_dp, self.n_line), lambda parts: parts[0][:n_small]
        )


def per_device(
    patches,
    cotangent,
    ln1_gain,
    ln1_bias,
    w_qkv,
    w_out,
    ln2_gain,
    ln2_bias,
    w_fc1,
    fc1_bias,
    w_fc2,
    pos_table,
    pos_index,
    pos_weight,
):
    bf16 = jnp.bfloat16
    f32 = jnp.float32
    n_dp = lax.axis_size("dp")
    n_line = lax.axis_size("fsdp")
    dp = lax.axis_index("dp")
    line = lax.axis_index("fsdp")
    low_flag = dp < n_dp * 7 // 16
    rows = patches.shape[0]
    width = patches.shape[1]
    shard = width // n_line
    place, valid, segment = place_rows(rows, low_flag, pos_index, pos_weight)
    if n_dp == 8 and n_line <= 4 and shard % (16 * n_dp) == 0:
        plan = Staged(n_dp, n_line, dp, line, width)
    else:
        plan = Wide(shard)
    n_bias = fc1_bias.size // shard
    smalls = jnp.concatenate(
        [
            jnp.stack([ln1_gain, ln1_bias, ln2_gain, ln2_bias]),
            fc1_bias.reshape(-1, shard),
            pos_table,
        ]
    )
    n_small = smalls.shape[0]
    table = plan.gather(w_qkv, w_out, w_fc1, w_fc2, smalls)
    full_qkv, full_out = plan.first()

    def across(block):
        return block.transpose(1, 0, 2).reshape(block.shape[1], width).astype(f32)

    gain_one, bias_one, gain_two, bias_two = across(table[:, :4])
    full_bias = table[:, 4 : 4 + n_bias].reshape(-1).astype(f32)
    full_table = across(table[:, 4 + n_bias : n_small])

    hidden_in = patches.astype(f32) + jnp.dot(place, full_table, precision=highest)
    normed_one = layer_norm(hidden_in, gain_one, bias_one).astype(bf16)
    projected = jnp.dot(normed_one, full_qkv, preferred_element_type=f32).astype(bf16)
    projected = plan.pass_one(projected)
    attn_rows = plan.pass_two(attend(projected, segment))
    hidden_mid = hidden_in + jnp.dot(attn_rows, full_out, preferred_element_type=f32)
    normed_two = layer_norm(hidden_mid, gain_two, bias_two).astype(bf16)
    normed_two = plan.pass_three(normed_two)
    full_fc1 = plan.second()
    pre_act = jnp.dot(normed_two, full_fc1, preferred_element_type=f32) + full_bias
    share = 0.5 * (1.0 + lax.erf(pre_act * 0.5**0.5))
    bell = jnp.exp(-0.5 * pre_act * pre_act) * (0.5 / jnp.pi) ** 0.5
    activated = (pre_act * share).astype(bf16)
    slope = (share + pre_act * bell).astype(bf16)
    activated = plan.pass_four(activated)
    grad_out = jnp.where(valid[:, None], cotangent, jnp.zeros_like(cotangent))
    run_fc2 = plan.total([(plan.wide_columns(activated), grad_out)])
    activated = tick(activated, [run_fc2])
    full_fc2, activated = tick((plan.third(), activated), [run_fc2])

    grad_pre = (times_t(grad_out, full_fc2) * slope.astype(f32)).astype(bf16)
    grad_fc1_bias = jnp.sum(grad_pre.astype(f32), axis=0)
    run_fc1 = plan.total([(plan.rows(normed_two), grad_pre)])
    grad_pre = tick(grad_pre, [run_fc1])
    grad_norm_two = times_t(grad_pre, full_fc1)
    _, pull_two = jax.vjp(layer_norm, hidden_mid, gain_two, bias_two)
    back_mid, grad_gain_two, grad_bias_two = pull_two(grad_norm_two)
    grad_mid = grad_out.astype(f32) + back_mid
    grad_branch = tick(grad_mid.astype(bf16), [run_fc1])
    run_out = plan.total([(plan.rows(attn_rows), grad_branch)])
    grad_attn = times_t(grad_branch, full_out).astype(bf16)
    grad_attn = tick(grad_attn, [run_fc2, run_out])
    half = HEADS // 4
    back_a = attend_back(projected, grad_attn, segment, 0, half)
    back_a, grad_attn = tick((back_a, grad_attn), [run_fc2, run_fc1, run_out])
    back_b = attend_back(projected, grad_attn, segment, half, half)
    back_a, back_b = tick((back_a, back_b), [run_fc2, run_fc1, run_out])
    side = back_a.shape[1] // 3
    grad_proj = jnp.concatenate(
        [part[:, i * side : (i + 1) * side] for i in range(3) for part in (back_a, back_b)], axis=1
    )
    run_qkv = plan.total([(plan.rows(normed_one), grad_proj)])
    grad_proj = tick(grad_proj, [run_qkv])
    every = [run_fc2, run_fc1, run_out]
    grad_norm_one = tick(times_t(grad_proj, full_qkv), [run_qkv, run_fc2])
    _, pull_one = jax.vjp(layer_norm, hidden_in, gain_one, bias_one)
    back_in, grad_gain_one, grad_bias_one = pull_one(grad_norm_one)
    grad_in = grad_mid + back_in
    grad_table = jnp.dot(place.T, grad_in, precision=highest)
    grad_table, activated = tick((grad_table, activated), [run_qkv] + every)
    branch_out = jnp.dot(activated, full_fc2, preferred_element_type=f32)
    block_out = jnp.where(valid[:, None], hidden_mid + branch_out, 0.0).astype(bf16)
    block_out = tick(block_out, [run_qkv] + every)

    def split(block):
        return block.reshape(-1, n_line, shard).transpose(1, 0, 2)

    rows_small = jnp.concatenate(
        [
            split(jnp.stack([grad_gain_one, grad_bias_one, grad_gain_two, grad_bias_two])),
            grad_fc1_bias.reshape(n_line, -1, shard),
            split(grad_table),
        ],
        axis=1,
    )
    run_small = plan.total_small(rows_small)
    (sum_fc2,) = run_fc2.result()
    (sum_fc1,) = run_fc1.result()
    (sum_out,) = run_out.result()
    (sum_qkv,) = run_qkv.result()
    small = run_small.result()
    return (
        block_out,
        grad_in.astype(bf16),
        small[0],
        small[1],
        sum_qkv,
        sum_out,
        small[2],
        small[3],
        sum_fc1,
        small[4 : 4 + n_bias].reshape(-1),
        sum_fc2,
        small[4 + n_bias :],
    )


def solution(mesh):
    return jax.shard_map(
        per_device,
        mesh=mesh,
        in_specs=(
            P(("dp", "fsdp"), None),
            P(("dp", "fsdp"), None),
            P("fsdp"),
            P("fsdp"),
            P("fsdp", None),
            P("fsdp", None),
            P("fsdp"),
            P("fsdp"),
            P("fsdp", None),
            P("fsdp"),
            P("fsdp", None),
            P(None, "fsdp"),
            P(),
            P(),
        ),
        out_specs=(
            P(("dp", "fsdp"), None),
            P(("dp", "fsdp"), None),
            P("fsdp"),
            P("fsdp"),
            P("fsdp", None),
            P("fsdp", None),
            P("fsdp"),
            P("fsdp"),
            P("fsdp", None),
            P("fsdp"),
            P("fsdp", None),
            P(None, "fsdp"),
        ),
        check_vma=False,
    )
```

```python
import jax
import jax.numpy as jnp
from jax import lax
from jax.experimental import pallas as pl
from jax.experimental.pallas import tpu as pltpu
from jax.sharding import PartitionSpec as P

HEADS = 16
HDIM = 64
POS = 50
HIGH_LEN = 145
TILE = 128


highest = lax.Precision.HIGHEST


def layer_norm(hidden, gain, shift):
    centre = hidden - jnp.mean(hidden, axis=-1, keepdims=True)
    spread = jnp.mean(centre * centre, axis=-1, keepdims=True)
    return centre * lax.rsqrt(spread + 1e-06) * gain + shift


def place_rows(rows, low_flag, pos_index, pos_weight):
    offsets = jnp.arange(rows, dtype=jnp.int32)
    table_ids = jnp.arange(POS, dtype=jnp.int32)
    high_ids = jnp.arange(HIGH_LEN, dtype=jnp.int32)
    picks = (pos_index[:, :, None] == table_ids[None, None, :]).astype(jnp.float32)
    interp = jnp.sum(pos_weight[:, :, None] * picks, axis=1)
    low_valid = offsets < rows // POS * POS
    high_valid = offsets < rows // HIGH_LEN * HIGH_LEN
    low_place = (((offsets % POS)[:, None] == table_ids[None, :]) & low_valid[:, None]).astype(
        jnp.float32
    )
    high_pick = (((offsets % HIGH_LEN)[:, None] == high_ids[None, :]) & high_valid[:, None]).astype(
        jnp.float32
    )
    high_place = jnp.dot(high_pick, interp, precision=highest)
    place = jnp.where(low_flag, low_place, high_place)
    valid = jnp.where(low_flag, low_valid, high_valid)
    segment = jnp.where(
        low_flag,
        jnp.where(low_valid, offsets // POS, -1),
        jnp.where(high_valid, offsets // HIGH_LEN, -1),
    )
    return (place, valid, segment)


def key_windows(rows):
    out = []
    for start in range(0, rows, TILE):
        least, most = rows, 0
        for size in (POS, HIGH_LEN):
            used = rows // size * size
            for row in (start, start + TILE - 1):
                image = row // size
                begin = image * size if row < used else used
                end = begin + size if row < used else rows
                least, most = min(least, begin), max(most, end)
        out.append((start, least // TILE * TILE, -(-most // TILE) * TILE))
    return out


def times_t(left, right):
    return lax.dot_general(left, right, (((1,), (1,)), ((), ())), preferred_element_type=jnp.float32)


def t_times(left, right):
    return lax.dot_general(left, right, (((0,), (0,)), ((), ())), preferred_element_type=jnp.float32)


def halves(block, scale=None):
    lane = lax.broadcasted_iota(jnp.int32, block.shape, 1)
    if scale is not None:
        block = block * jnp.asarray(scale, block.dtype)
    zero = jnp.zeros_like(block)
    return (jnp.where(lane < HDIM, block, zero), jnp.where(lane < HDIM, zero, block))


def soft(query, keys, same):
    scores = jnp.where(same, times_t(query, keys), -1e30)
    expo = jnp.exp(scores - jnp.max(scores, axis=-1, keepdims=True))
    return expo * (1.0 / jnp.sum(expo, axis=-1, keepdims=True))


def attend_body(windows, col_ref, row_ref, q_ref, k_ref, v_ref, out_ref):
    values = halves(v_ref[...])
    for start, lo, hi in windows:
        rows = slice(start, start + TILE)
        same = col_ref[rows, :] == row_ref[:, lo:hi]
        keys = k_ref[lo:hi, :]
        total = None
        for query, value in zip(halves(q_ref[rows, :], HDIM ** (-0.5)), values):
            probs = soft(query, keys, same).astype(jnp.bfloat16)
            part = jnp.dot(probs, value[lo:hi], preferred_element_type=jnp.float32)
            total = part if total is None else total + part
        out_ref[rows, :] = total.astype(jnp.bfloat16)


def attend_back_body(windows, col_ref, row_ref, q_ref, k_ref, v_ref, g_ref, out_ref, dk_ref, dv_ref):
    width = q_ref.shape[1]
    full = out_ref.shape[1] // 3
    at = pl.program_id(0) * width
    dk_ref[...] = jnp.zeros_like(dk_ref)
    dv_ref[...] = jnp.zeros_like(dv_ref)
    scaled = halves(k_ref[...], HDIM ** (-0.5))
    for start, lo, hi in windows:
        rows = slice(start, start + TILE)
        same = col_ref[rows, :] == row_ref[:, lo:hi]
        keys = k_ref[lo:hi, :]
        values = v_ref[lo:hi, :]
        total = None
        queries = halves(q_ref[rows, :], HDIM ** (-0.5))
        grads = halves(g_ref[rows, :])
        for query, grad, key in zip(queries, grads, scaled):
            probs = soft(query, keys, same)
            grad_probs = times_t(grad, values)
            centre = jnp.sum(probs * grad_probs, axis=-1, keepdims=True)
            grad_scores = (probs * (grad_probs - centre)).astype(jnp.bfloat16)
            part = jnp.dot(grad_scores, key[lo:hi], preferred_element_type=jnp.float32)
            total = part if total is None else total + part
            dk_ref[lo:hi, :] += t_times(grad_scores, query)
            dv_ref[lo:hi, :] += t_times(probs.astype(jnp.bfloat16), grad)
        out_ref[rows, pl.ds(pl.multiple_of(at, width), width)] = total.astype(jnp.bfloat16)
    out_ref[:, pl.ds(pl.multiple_of(full + at, width), width)] = dk_ref[...].astype(jnp.bfloat16)
    out_ref[:, pl.ds(pl.multiple_of(2 * full + at, width), width)] = dv_ref[...].astype(jnp.bfloat16)


def pair_specs(rows, pairs, start=0):
    pair = 2 * HDIM
    whole = [
        pl.BlockSpec((rows, 1), lambda i: (0, 0)),
        pl.BlockSpec((1, rows), lambda i: (0, 0)),
    ]
    return whole + [
        pl.BlockSpec((rows, pair), lambda i, j=j: (0, j * pairs + start + i)) for j in range(3)
    ]


def attend(projected, segment):
    rows = projected.shape[0]
    pairs = HEADS // 2
    windows = key_windows(rows)

    def body(*refs):
        attend_body(windows, *refs)

    return pl.pallas_call(
        body,
        grid=(pairs,),
        in_specs=pair_specs(rows, pairs),
        out_specs=pl.BlockSpec((rows, 2 * HDIM), lambda i: (0, i)),
        out_shape=jax.ShapeDtypeStruct((rows, HEADS * HDIM), jnp.bfloat16),
        name="attend",
    )(segment[:, None], segment[None, :], projected, projected, projected)


def attend_back(projected, grad_attn, segment, start, count):
    rows = projected.shape[0]
    pairs = HEADS // 2
    windows = key_windows(rows)
    wide = 3 * count * 2 * HDIM

    def body(*refs):
        attend_back_body(windows, *refs)

    return pl.pallas_call(
        body,
        grid=(count,),
        in_specs=pair_specs(rows, pairs, start)
        + [pl.BlockSpec((rows, 2 * HDIM), lambda i: (0, start + i))],
        out_specs=pl.BlockSpec((rows, wide), lambda i: (0, 0)),
        out_shape=jax.ShapeDtypeStruct((rows, wide), jnp.bfloat16),
        scratch_shapes=[pltpu.VMEM((rows, 2 * HDIM), jnp.float32)] * 2,
        name="attend_back",
    )(segment[:, None], segment[None, :], projected, projected, projected, grad_attn)


def copies(pairs_of, sems):
    moves = [
        pltpu.make_async_copy(source, target, sems.at[i])
        for i, (source, target) in enumerate(pairs_of)
    ]
    for move in moves:
        move.start()
    for move in moves:
        move.wait()


def assemble(owns, parts, table, n_line, unit):
    n_places = sum(part.shape[0] for part in parts)
    n_own = len(owns)
    n_parts = len(parts)
    ends = []
    for own in owns:
        ends.append((ends[-1] if ends else 0) + own.shape[1])
    count = n_own * (1 + n_places * (n_line - 1))

    def body(table_ref, *refs):
        own_refs = refs[:n_own]
        part_refs = refs[n_own : n_own + n_parts]
        out_refs = refs[n_own + n_parts : 2 * n_own + n_parts]
        sems = refs[-1]
        todo = []
        for own_ref, out_ref, end in zip(own_refs, out_refs, ends):
            shard_rows = own_ref.shape[0]
            columns = pl.ds(end - own_ref.shape[1], own_ref.shape[1])
            first = pl.multiple_of(table_ref[n_places * n_line] * unit, unit)
            todo.append((own_ref, out_ref.at[pl.ds(first, shard_rows), :]))
            place = 0
            for part_ref in part_refs:
                for k in range(part_ref.shape[0]):
                    for step in range(1, n_line):
                        row = pl.multiple_of(table_ref[place * n_line + step] * unit, unit)
                        todo.append(
                            (
                                part_ref.at[k, step - 1, pl.ds(0, unit), columns],
                                out_ref.at[pl.ds(row, unit), :],
                            )
                        )
                    place += 1
        copies(todo, sems)

    anywhere = pl.BlockSpec(memory_space=pl.ANY)
    return pl.pallas_call(
        body,
        in_specs=[pl.BlockSpec(memory_space=pltpu.SMEM)] + [anywhere] * (n_own + n_parts),
        out_specs=[pl.BlockSpec(memory_space=pltpu.VMEM)] * n_own,
        out_shape=[
            jax.ShapeDtypeStruct((own.shape[0] * n_line, own.shape[1]), own.dtype) for own in owns
        ],
        scratch_shapes=[pltpu.SemaphoreType.DMA((count,))],
        name="assemble",
    )(table, *owns, *parts)


def column_order(block, table, unit):
    count = block.shape[1] // unit

    def body(table_ref, in_ref, out_ref):
        for i in range(count):
            column = pl.multiple_of(table_ref[i] * unit, unit)
            out_ref[:, i * unit : (i + 1) * unit] = in_ref[:, pl.ds(column, unit)]

    return pl.pallas_call(
        body,
        in_specs=[
            pl.BlockSpec(memory_space=pltpu.SMEM),
            pl.BlockSpec(memory_space=pltpu.VMEM),
        ],
        out_specs=pl.BlockSpec(memory_space=pltpu.VMEM),
        out_shape=jax.ShapeDtypeStruct(block.shape, block.dtype),
        name="column_order",
    )(table, block)


def finish(parts, owner, cuts):
    unit = parts[0].shape[1]
    n_places = sum(part.shape[0] for part in parts)

    def body(owner_ref, *refs):
        part_refs = refs[: len(parts)]
        out_refs = refs[len(parts) :]
        place = 0
        for part_ref in part_refs:
            for k in range(part_ref.shape[0]):
                row = pl.multiple_of(owner_ref[place] * unit, unit)
                at = 0
                for out_ref, cut in zip(out_refs, cuts):
                    out_ref[pl.ds(row, unit), :] = part_ref[k, :, at : at + cut].astype(jnp.float32)
                    at += cut
                place += 1

    return pl.pallas_call(
        body,
        in_specs=[pl.BlockSpec(memory_space=pltpu.SMEM)]
        + [pl.BlockSpec(memory_space=pltpu.VMEM)] * len(parts),
        out_specs=[pl.BlockSpec(memory_space=pltpu.VMEM)] * len(cuts),
        out_shape=[jax.ShapeDtypeStruct((n_places * unit, cut), jnp.float32) for cut in cuts],
        name="finish",
    )(owner, *parts)


def hop_bit(core, stage, bits):
    return 1 + stage if core == 0 else bits - stage


def hop_pairs(n_dp, stage):
    bits = n_dp.bit_length() - 2
    return [(i, i ^ (1 << hop_bit(i % 2, stage, bits))) for i in range(n_dp)]


def swap_core(block, n_dp):
    return lax.ppermute(block, "dp", [(i, i ^ 1) for i in range(n_dp)])


def ahead(block, n_line, step):
    return lax.ppermute(block, "fsdp", [(i, (i + step) % n_line) for i in range(n_line)])


def plane_hops(block, n_dp):
    across = (1 << n_dp.bit_length() - 1) - 2
    both = [(i, i ^ across) for i in range(n_dp)]
    hops = [hop_pairs(n_dp, stage) for stage in range(n_dp.bit_length() - 2)] + [both]
    return [lax.ppermute(block, "dp", pairs) for pairs in hops]


def add_up(terms):
    total = terms[0].astype(jnp.float32)
    for term in terms[1:]:
        total = total + term.astype(jnp.float32)
    return total


def reduce_steps(away, keep, n_dp, n_line):
    (away,) = yield [away]
    (got,) = yield [swap_core(away, n_dp)]
    terms = [keep, got]
    half = keep.shape[0] // 2
    for stage in range(n_dp.bit_length() - 2):
        (send,) = yield [add_up([term[half:] for term in terms]).astype(jnp.bfloat16)]
        (got,) = yield [lax.ppermute(send, "dp", hop_pairs(n_dp, stage))]
        terms = [term[:half] for term in terms] + [got]
        half //= 2
    terms = [term[0] for term in terms]
    sends = yield [
        add_up([term[step] for term in terms]).astype(jnp.bfloat16) for step in range(1, n_line)
    ]
    arrived = yield [ahead(send, n_line, step + 1) for step, send in enumerate(sends)]
    total = add_up([term[0] for term in terms] + arrived)
    (near,) = yield [total.astype(jnp.bfloat16)[None]]
    got = yield plane_hops(near, n_dp)
    (send,) = yield [jnp.concatenate([near] + got)]
    (got,) = yield [swap_core(send, n_dp)]
    return [send, got]


def small_steps(mine, n_dp, n_line):
    (mine,) = yield [mine]
    for bit in range(n_dp.bit_length() - 1):
        pairs = [(i, i ^ (1 << bit)) for i in range(n_dp)]
        (got,) = yield [lax.ppermute(mine, "dp", pairs)]
        (mine,) = yield [mine + got]
    line = lax.axis_index("fsdp")

    def part(step):
        return lax.dynamic_index_in_dim(mine, (line + step) % n_line, 0, keepdims=False)

    arrived = yield [ahead(part(step), n_line, step) for step in range(1, n_line)]
    total = part(0)
    for item in arrived:
        total = total + item
    return [total]


class Reduction:
    def __init__(self, steps, close):
        self.steps = steps
        self.close = close
        self.parts = None
        self.held = None
        self.begin = next(steps)

    def take(self, got):
        try:
            return self.steps.send(got)
        except StopIteration as stop:
            self.parts = stop.value
            return []

    def result(self):
        if self.held is None:
            self.held = self.steps.send(self.begin)
        while self.parts is None:
            sends = self.take(self.held)
            if self.parts is None:
                self.held = self.steps.send(sends)
        return self.close(self.parts)


class Ready:
    def __init__(self, outs):
        self.outs = outs

    def result(self):
        return self.outs


def tick(value, running):
    running = [item for item in running if isinstance(item, Reduction) and item.parts is None]
    old = [item for item in running if item.held is not None]
    value, gots = lax.optimization_barrier((value, [item.held for item in old]))
    sends = [item.take(got) for item, got in zip(old, gots)]
    new = [item for item in running if item.held is None]
    sends = sends + [item.begin for item in new]
    value, sends = lax.optimization_barrier((value, sends))
    for item, send in zip(old + new, sends):
        if item.parts is None:
            item.held = item.steps.send(send)
    return value


def place_of(n_dp, me, flip):
    bits = n_dp.bit_length() - 2
    core = me % 2
    halves = []
    for other in range(2):
        place = jnp.arange(1 << bits, dtype=jnp.int32)
        owner = jnp.full((1 << bits,), me ^ other, jnp.int32)
        for stage in range(bits):
            at = bits - 1 - stage if flip else stage
            low = 1 << hop_bit(0, stage, bits)
            high = 1 << hop_bit(1, stage, bits)
            mask = jnp.where((core ^ other) == 0, low, high)
            owner = owner ^ (((place >> at) & 1) * mask)
        halves.append(owner)
    return jnp.concatenate(halves)


class Wide:
    def __init__(self, shard):
        self.shard = shard

    def gather(self, w_qkv, w_out, w_fc1, w_fc2, smalls):
        def full(matrix):
            return lax.all_gather(matrix, "fsdp", axis=0, tiled=True)

        self.full = [full(w_qkv), full(w_out), full(w_fc1), full(w_fc2)]
        return lax.all_gather(smalls, "fsdp", axis=0)

    def first(self):
        return self.full[:2]

    def second(self):
        return self.full[2]

    def third(self):
        return self.full[3]

    def pass_one(self, gate):
        return gate

    pass_two = pass_three = pass_four = pass_one

    def rows(self, block):
        return block

    def wide_columns(self, block):
        return block

    def total(self, terms):
        bf16 = jnp.bfloat16
        outs = []
        for left, right in terms:
            grad = t_times(left, right).astype(bf16)
            own = lax.psum_scatter(grad, "fsdp", scatter_dimension=0, tiled=True)
            outs.append(lax.psum(own, "dp").astype(jnp.float32))
        return Ready(outs)

    def total_small(self, smalls):
        own = lax.psum_scatter(
            smalls.astype(jnp.bfloat16), "fsdp", scatter_dimension=0, tiled=False
        )
        return Ready(lax.psum(own, "dp").astype(jnp.float32))


class Gather:
    def __init__(self, unit, n_dp, n_line):
        self.n_dp = n_dp
        self.line = [ahead(unit, n_line, step) for step in range(1, n_line)]

    def hop(self, block, stage):
        return lax.ppermute(block, "dp", hop_pairs(self.n_dp, stage))

    def fan(self, gate, columns):
        self.line, gate = lax.optimization_barrier((self.line, gate))
        near = jnp.stack([item[:, :columns] for item in self.line])[None]
        near, gate = lax.optimization_barrier((near, gate))
        self.parts = [near, self.hop(near, 0), self.hop(near, 1)]
        self.cores = [swap_core(near, self.n_dp)]
        return gate

    def forward(self, gate):
        self.parts[1], gate = lax.optimization_barrier((self.parts[1], gate))
        self.parts.append(self.hop(self.parts[1], 1))
        self.cores.append(swap_core(self.parts[1], self.n_dp))
        return gate

    def close(self, gate):
        late, gate = lax.optimization_barrier((self.parts[2:], gate))
        self.cores += [swap_core(item, self.n_dp) for item in late]
        self.parts = self.parts[:2] + late
        return gate


class Staged:
    def __init__(self, n_dp, n_line, dp, line, width):
        self.n_dp = n_dp
        self.n_line = n_line
        self.dp = dp
        self.line = line
        self.unit = width // n_line // n_dp
        steps = jnp.arange(n_line, dtype=jnp.int32)
        owner = place_of(n_dp, dp, False)
        self.owner = owner
        self.unline = (line - steps) % n_line
        first = line * n_dp
        got = self.unline[None, :] * n_dp + owner[:, None]
        self.got_table = jnp.concatenate([got.reshape(-1), first[None]]).astype(jnp.int32)
        send_line = (line + steps) % n_line
        send = send_line[None, :] * n_dp + place_of(n_dp, dp, True)[:, None]
        self.send_table = send.reshape(-1).astype(jnp.int32)
        natural = jnp.arange(width, dtype=jnp.int32)
        arranged = (
            self.send_table[:, None] * self.unit + jnp.arange(self.unit, dtype=jnp.int32)[None, :]
        ).reshape(-1)
        self.order = (natural[:, None] == arranged[None, :]).astype(jnp.bfloat16)

    def pick(self, shard):
        size = shard.shape[0] // self.n_dp
        return lax.dynamic_slice_in_dim(shard, self.dp * size, size, 0)

    def gather(self, w_qkv, w_out, w_fc1, w_fc2, smalls):
        n_dp = self.n_dp
        n_line = self.n_line
        shard = smalls.shape[1]
        size = self.unit
        wide = w_qkv.shape[1] + w_out.shape[1]
        fold = -(-smalls.shape[0] // size)
        padded = jnp.pad(smalls, ((0, size * fold - smalls.shape[0]), (0, 0)))
        packed = [padded[i * size : (i + 1) * size] for i in range(fold)]
        unit_one = jnp.concatenate([self.pick(w_qkv), self.pick(w_out)] + packed, axis=1)
        unit_two, unit_three = (self.pick(w_fc1), self.pick(w_fc2))
        one = Gather(unit_one, n_dp, n_line)
        unit_two = one.fan(unit_two, wide)
        far = jnp.stack([item[:, wide:] for item in one.line])
        two = Gather(unit_two, n_dp, n_line)
        two.line = one.forward(two.line)
        two.line = one.close(two.line)
        table, unit_three = two.fan((self.got_table, unit_three), unit_two.shape[1])
        three = Gather(unit_three, n_dp, n_line)
        full_qkv, full_out = assemble([w_qkv, w_out], one.parts + one.cores, table, n_line, size)
        self.one = (full_qkv, full_out)
        self.two = (w_fc1, two)
        self.three = (w_fc2, three, unit_three.shape)
        far = jnp.concatenate([far[:, :, i * shard : (i + 1) * shard] for i in range(fold)], axis=1)
        return jnp.take(jnp.concatenate([padded[None], far]), self.unline, axis=0)

    def first(self):
        return self.one

    def pass_one(self, gate):
        return self.two[1].forward(gate)

    def pass_two(self, gate):
        return self.three[1].fan(self.two[1].close(gate), self.three[2][1])

    def pass_three(self, gate):
        return self.three[1].forward(gate)

    def pass_four(self, gate):
        return self.three[1].close(gate)

    def second(self):
        own, got = self.two
        return assemble([own], got.parts + got.cores, self.got_table, self.n_line, self.unit)[0]

    def third(self):
        own, got, unit = self.three
        return assemble([own], got.parts + got.cores, self.got_table, self.n_line, unit[0])[0]

    def rows(self, block):
        return jnp.dot(block, self.order, preferred_element_type=jnp.float32).astype(jnp.bfloat16)

    def wide_columns(self, block):
        return column_order(block, self.send_table, block.shape[1] // (self.n_dp * self.n_line))

    def total(self, terms):
        n_dp = self.n_dp
        n_line = self.n_line
        sides = []
        for side in (1, 0):
            grads = []
            for left, right in terms:
                half = left.shape[1] // 2
                grad = t_times(left[:, side * half : (side + 1) * half], right).astype(jnp.bfloat16)
                grads.append(grad.reshape(n_dp // 2, n_line, -1, right.shape[1]))
            sides.append(jnp.concatenate(grads, axis=3) if len(grads) > 1 else grads[0])
        cuts = [right.shape[1] for left, right in terms]
        owner = self.owner.astype(jnp.int32)
        steps = reduce_steps(sides[0], sides[1], n_dp, n_line)
        return Reduction(steps, lambda parts: list(finish(parts, owner, cuts)))

    def total_small(self, smalls):
        n_small = smalls.shape[1]
        padded = jnp.pad(smalls, ((0, 0), (0, -n_small % 8), (0, 0)))
        return Reduction(
            small_steps(padded, self.n_dp, self.n_line), lambda parts: parts[0][:n_small]
        )


def per_device(
    patches,
    cotangent,
    ln1_gain,
    ln1_bias,
    w_qkv,
    w_out,
    ln2_gain,
    ln2_bias,
    w_fc1,
    fc1_bias,
    w_fc2,
    pos_table,
    pos_index,
    pos_weight,
):
    bf16 = jnp.bfloat16
    f32 = jnp.float32
    n_dp = lax.axis_size("dp")
    n_line = lax.axis_size("fsdp")
    dp = lax.axis_index("dp")
    line = lax.axis_index("fsdp")
    low_flag = dp < n_dp * 7 // 16
    rows = patches.shape[0]
    width = patches.shape[1]
    shard = width // n_line
    place, valid, segment = place_rows(rows, low_flag, pos_index, pos_weight)
    if n_dp == 8 and n_line <= 4 and shard % (16 * n_dp) == 0:
        plan = Staged(n_dp, n_line, dp, line, width)
    else:
        plan = Wide(shard)
    n_bias = fc1_bias.size // shard
    smalls = jnp.concatenate(
        [
            jnp.stack([ln1_gain, ln1_bias, ln2_gain, ln2_bias]),
            fc1_bias.reshape(-1, shard),
            pos_table,
        ]
    )
    n_small = smalls.shape[0]
    table = plan.gather(w_qkv, w_out, w_fc1, w_fc2, smalls)
    full_qkv, full_out = plan.first()

    def across(block):
        return block.transpose(1, 0, 2).reshape(block.shape[1], width).astype(f32)

    gain_one, bias_one, gain_two, bias_two = across(table[:, :4])
    full_bias = table[:, 4 : 4 + n_bias].reshape(-1).astype(f32)
    full_table = across(table[:, 4 + n_bias : n_small])

    hidden_in = patches.astype(f32) + jnp.dot(place, full_table, precision=highest)
    normed_one = layer_norm(hidden_in, gain_one, bias_one).astype(bf16)
    projected = jnp.dot(normed_one, full_qkv, preferred_element_type=f32).astype(bf16)
    projected = plan.pass_one(projected)
    attn_rows = plan.pass_two(attend(projected, segment))
    hidden_mid = hidden_in + jnp.dot(attn_rows, full_out, preferred_element_type=f32)
    normed_two = layer_norm(hidden_mid, gain_two, bias_two).astype(bf16)
    normed_two = plan.pass_three(normed_two)
    full_fc1 = plan.second()
    pre_act = jnp.dot(normed_two, full_fc1, preferred_element_type=f32) + full_bias
    share = 0.5 * (1.0 + lax.erf(pre_act * 0.5**0.5))
    bell = jnp.exp(-0.5 * pre_act * pre_act) * (0.5 / jnp.pi) ** 0.5
    activated = (pre_act * share).astype(bf16)
    slope = (share + pre_act * bell).astype(bf16)
    activated = plan.pass_four(activated)
    grad_out = jnp.where(valid[:, None], cotangent, jnp.zeros_like(cotangent))
    run_fc2 = plan.total([(plan.wide_columns(activated), grad_out)])
    activated = tick(activated, [run_fc2])
    full_fc2, activated = tick((plan.third(), activated), [run_fc2])

    grad_pre = (times_t(grad_out, full_fc2) * slope.astype(f32)).astype(bf16)
    grad_fc1_bias = jnp.sum(grad_pre.astype(f32), axis=0)
    run_fc1 = plan.total([(plan.rows(normed_two), grad_pre)])
    grad_pre = tick(grad_pre, [run_fc1])
    grad_norm_two = times_t(grad_pre, full_fc1)
    _, pull_two = jax.vjp(layer_norm, hidden_mid, gain_two, bias_two)
    back_mid, grad_gain_two, grad_bias_two = pull_two(grad_norm_two)
    grad_mid = grad_out.astype(f32) + back_mid
    grad_branch = tick(grad_mid.astype(bf16), [run_fc1])
    run_out = plan.total([(plan.rows(attn_rows), grad_branch)])
    grad_attn = times_t(grad_branch, full_out).astype(bf16)
    grad_attn = tick(grad_attn, [run_fc2, run_out])
    half = HEADS // 4
    back_a = attend_back(projected, grad_attn, segment, 0, half)
    back_a, grad_attn = tick((back_a, grad_attn), [run_fc2, run_fc1, run_out])
    back_b = attend_back(projected, grad_attn, segment, half, half)
    back_a, back_b = tick((back_a, back_b), [run_fc2, run_fc1, run_out])
    side = back_a.shape[1] // 3
    grad_proj = jnp.concatenate(
        [part[:, i * side : (i + 1) * side] for i in range(3) for part in (back_a, back_b)], axis=1
    )
    run_qkv = plan.total([(plan.rows(normed_one), grad_proj)])
    grad_proj = tick(grad_proj, [run_qkv])
    every = [run_fc2, run_fc1, run_out]
    grad_norm_one = tick(times_t(grad_proj, full_qkv), [run_qkv, run_fc2])
    _, pull_one = jax.vjp(layer_norm, hidden_in, gain_one, bias_one)
    back_in, grad_gain_one, grad_bias_one = pull_one(grad_norm_one)
    grad_in = grad_mid + back_in
    grad_table = jnp.dot(place.T, grad_in, precision=highest)
    grad_table, activated = lax.optimization_barrier((grad_table, activated))
    branch_out = jnp.dot(activated, full_fc2, preferred_element_type=f32)
    block_out = jnp.where(valid[:, None], hidden_mid + branch_out, 0.0).astype(bf16)
    grad_table, block_out = tick((grad_table, block_out), [run_qkv] + every)

    def split(block):
        return block.reshape(-1, n_line, shard).transpose(1, 0, 2)

    rows_small = jnp.concatenate(
        [
            split(jnp.stack([grad_gain_one, grad_bias_one, grad_gain_two, grad_bias_two])),
            grad_fc1_bias.reshape(n_line, -1, shard),
            split(grad_table),
        ],
        axis=1,
    )
    rows_small = tick(rows_small, [run_qkv])
    run_small = plan.total_small(rows_small)
    (sum_fc2,) = run_fc2.result()
    (sum_fc1,) = run_fc1.result()
    (sum_out,) = run_out.result()
    (sum_qkv,) = run_qkv.result()
    small = run_small.result()
    return (
        block_out,
        grad_in.astype(bf16),
        small[0],
        small[1],
        sum_qkv,
        sum_out,
        small[2],
        small[3],
        sum_fc1,
        small[4 : 4 + n_bias].reshape(-1),
        sum_fc2,
        small[4 + n_bias :],
    )


def solution(mesh):
    return jax.shard_map(
        per_device,
        mesh=mesh,
        in_specs=(
            P(("dp", "fsdp"), None),
            P(("dp", "fsdp"), None),
            P("fsdp"),
            P("fsdp"),
            P("fsdp", None),
            P("fsdp", None),
            P("fsdp"),
            P("fsdp"),
            P("fsdp", None),
            P("fsdp"),
            P("fsdp", None),
            P(None, "fsdp"),
            P(),
            P(),
        ),
        out_specs=(
            P(("dp", "fsdp"), None),
            P(("dp", "fsdp"), None),
            P("fsdp"),
            P("fsdp"),
            P("fsdp", None),
            P("fsdp", None),
            P("fsdp"),
            P("fsdp"),
            P("fsdp", None),
            P("fsdp"),
            P("fsdp", None),
            P(None, "fsdp"),
        ),
        check_vma=False,
    )
```

```python
import jax
import jax.numpy as jnp
from jax import lax
from jax.experimental import pallas as pl
from jax.experimental.pallas import tpu as pltpu
from jax.sharding import PartitionSpec as P

HEADS = 16
HDIM = 64
POS = 50
HIGH_LEN = 145
TILE = 128


highest = lax.Precision.HIGHEST


def layer_norm(hidden, gain, shift):
    centre = hidden - jnp.mean(hidden, axis=-1, keepdims=True)
    spread = jnp.mean(centre * centre, axis=-1, keepdims=True)
    return centre * lax.rsqrt(spread + 1e-06) * gain + shift


def place_rows(rows, low_flag, pos_index, pos_weight):
    offsets = jnp.arange(rows, dtype=jnp.int32)
    table_ids = jnp.arange(POS, dtype=jnp.int32)
    high_ids = jnp.arange(HIGH_LEN, dtype=jnp.int32)
    picks = (pos_index[:, :, None] == table_ids[None, None, :]).astype(jnp.float32)
    interp = jnp.sum(pos_weight[:, :, None] * picks, axis=1)
    low_valid = offsets < rows // POS * POS
    high_valid = offsets < rows // HIGH_LEN * HIGH_LEN
    low_place = (((offsets % POS)[:, None] == table_ids[None, :]) & low_valid[:, None]).astype(
        jnp.float32
    )
    high_pick = (((offsets % HIGH_LEN)[:, None] == high_ids[None, :]) & high_valid[:, None]).astype(
        jnp.float32
    )
    high_place = jnp.dot(high_pick, interp, precision=highest)
    place = jnp.where(low_flag, low_place, high_place)
    valid = jnp.where(low_flag, low_valid, high_valid)
    segment = jnp.where(
        low_flag,
        jnp.where(low_valid, offsets // POS, -1),
        jnp.where(high_valid, offsets // HIGH_LEN, -1),
    )
    return (place, valid, segment)


def key_windows(rows):
    out = []
    for start in range(0, rows, TILE):
        least, most = rows, 0
        for size in (POS, HIGH_LEN):
            used = rows // size * size
            for row in (start, start + TILE - 1):
                image = row // size
                begin = image * size if row < used else used
                end = begin + size if row < used else rows
                least, most = min(least, begin), max(most, end)
        out.append((start, least // TILE * TILE, -(-most // TILE) * TILE))
    return out


def times_t(left, right):
    return lax.dot_general(left, right, (((1,), (1,)), ((), ())), preferred_element_type=jnp.float32)


def t_times(left, right):
    return lax.dot_general(left, right, (((0,), (0,)), ((), ())), preferred_element_type=jnp.float32)


def halves(block, scale=None):
    lane = lax.broadcasted_iota(jnp.int32, block.shape, 1)
    if scale is not None:
        block = block * jnp.asarray(scale, block.dtype)
    zero = jnp.zeros_like(block)
    return (jnp.where(lane < HDIM, block, zero), jnp.where(lane < HDIM, zero, block))


def soft(query, keys, same):
    scores = jnp.where(same, times_t(query, keys), -1e30)
    expo = jnp.exp(scores - jnp.max(scores, axis=-1, keepdims=True))
    return expo * (1.0 / jnp.sum(expo, axis=-1, keepdims=True))


def attend_body(windows, col_ref, row_ref, q_ref, k_ref, v_ref, out_ref):
    values = halves(v_ref[...])
    for start, lo, hi in windows:
        rows = slice(start, start + TILE)
        same = col_ref[rows, :] == row_ref[:, lo:hi]
        keys = k_ref[lo:hi, :]
        total = None
        for query, value in zip(halves(q_ref[rows, :], HDIM ** (-0.5)), values):
            probs = soft(query, keys, same).astype(jnp.bfloat16)
            part = jnp.dot(probs, value[lo:hi], preferred_element_type=jnp.float32)
            total = part if total is None else total + part
        out_ref[rows, :] = total.astype(jnp.bfloat16)


def attend_back_body(windows, col_ref, row_ref, q_ref, k_ref, v_ref, g_ref, out_ref, dk_ref, dv_ref):
    width = q_ref.shape[1]
    full = out_ref.shape[1] // 3
    at = pl.program_id(0) * width
    dk_ref[...] = jnp.zeros_like(dk_ref)
    dv_ref[...] = jnp.zeros_like(dv_ref)
    scaled = halves(k_ref[...], HDIM ** (-0.5))
    for start, lo, hi in windows:
        rows = slice(start, start + TILE)
        same = col_ref[rows, :] == row_ref[:, lo:hi]
        keys = k_ref[lo:hi, :]
        values = v_ref[lo:hi, :]
        total = None
        queries = halves(q_ref[rows, :], HDIM ** (-0.5))
        grads = halves(g_ref[rows, :])
        for query, grad, key in zip(queries, grads, scaled):
            probs = soft(query, keys, same)
            grad_probs = times_t(grad, values)
            centre = jnp.sum(probs * grad_probs, axis=-1, keepdims=True)
            grad_scores = (probs * (grad_probs - centre)).astype(jnp.bfloat16)
            part = jnp.dot(grad_scores, key[lo:hi], preferred_element_type=jnp.float32)
            total = part if total is None else total + part
            dk_ref[lo:hi, :] += t_times(grad_scores, query)
            dv_ref[lo:hi, :] += t_times(probs.astype(jnp.bfloat16), grad)
        out_ref[rows, pl.ds(pl.multiple_of(at, width), width)] = total.astype(jnp.bfloat16)
    out_ref[:, pl.ds(pl.multiple_of(full + at, width), width)] = dk_ref[...].astype(jnp.bfloat16)
    out_ref[:, pl.ds(pl.multiple_of(2 * full + at, width), width)] = dv_ref[...].astype(jnp.bfloat16)


def pair_specs(rows, pairs, start=0):
    pair = 2 * HDIM
    whole = [
        pl.BlockSpec((rows, 1), lambda i: (0, 0)),
        pl.BlockSpec((1, rows), lambda i: (0, 0)),
    ]
    return whole + [
        pl.BlockSpec((rows, pair), lambda i, j=j: (0, j * pairs + start + i)) for j in range(3)
    ]


def attend(projected, segment):
    rows = projected.shape[0]
    pairs = HEADS // 2
    windows = key_windows(rows)

    def body(*refs):
        attend_body(windows, *refs)

    return pl.pallas_call(
        body,
        grid=(pairs,),
        in_specs=pair_specs(rows, pairs),
        out_specs=pl.BlockSpec((rows, 2 * HDIM), lambda i: (0, i)),
        out_shape=jax.ShapeDtypeStruct((rows, HEADS * HDIM), jnp.bfloat16),
        name="attend",
    )(segment[:, None], segment[None, :], projected, projected, projected)


def attend_back(projected, grad_attn, segment, start, count):
    rows = projected.shape[0]
    pairs = HEADS // 2
    windows = key_windows(rows)
    wide = 3 * count * 2 * HDIM

    def body(*refs):
        attend_back_body(windows, *refs)

    return pl.pallas_call(
        body,
        grid=(count,),
        in_specs=pair_specs(rows, pairs, start)
        + [pl.BlockSpec((rows, 2 * HDIM), lambda i: (0, start + i))],
        out_specs=pl.BlockSpec((rows, wide), lambda i: (0, 0)),
        out_shape=jax.ShapeDtypeStruct((rows, wide), jnp.bfloat16),
        scratch_shapes=[pltpu.VMEM((rows, 2 * HDIM), jnp.float32)] * 2,
        name="attend_back",
    )(segment[:, None], segment[None, :], projected, projected, projected, grad_attn)


def copies(pairs_of, sems):
    moves = [
        pltpu.make_async_copy(source, target, sems.at[i])
        for i, (source, target) in enumerate(pairs_of)
    ]
    for move in moves:
        move.start()
    for move in moves:
        move.wait()


def assemble(owns, parts, table, n_line, unit):
    n_places = sum(part.shape[0] for part in parts)
    n_own = len(owns)
    n_parts = len(parts)
    ends = []
    for own in owns:
        ends.append((ends[-1] if ends else 0) + own.shape[1])
    count = n_own * (1 + n_places * (n_line - 1))

    def body(table_ref, *refs):
        own_refs = refs[:n_own]
        part_refs = refs[n_own : n_own + n_parts]
        out_refs = refs[n_own + n_parts : 2 * n_own + n_parts]
        sems = refs[-1]
        todo = []
        for own_ref, out_ref, end in zip(own_refs, out_refs, ends):
            shard_rows = own_ref.shape[0]
            columns = pl.ds(end - own_ref.shape[1], own_ref.shape[1])
            first = pl.multiple_of(table_ref[n_places * n_line] * unit, unit)
            todo.append((own_ref, out_ref.at[pl.ds(first, shard_rows), :]))
            place = 0
            for part_ref in part_refs:
                for k in range(part_ref.shape[0]):
                    for step in range(1, n_line):
                        row = pl.multiple_of(table_ref[place * n_line + step] * unit, unit)
                        todo.append(
                            (
                                part_ref.at[k, step - 1, pl.ds(0, unit), columns],
                                out_ref.at[pl.ds(row, unit), :],
                            )
                        )
                    place += 1
        copies(todo, sems)

    anywhere = pl.BlockSpec(memory_space=pl.ANY)
    return pl.pallas_call(
        body,
        in_specs=[pl.BlockSpec(memory_space=pltpu.SMEM)] + [anywhere] * (n_own + n_parts),
        out_specs=[pl.BlockSpec(memory_space=pltpu.VMEM)] * n_own,
        out_shape=[
            jax.ShapeDtypeStruct((own.shape[0] * n_line, own.shape[1]), own.dtype) for own in owns
        ],
        scratch_shapes=[pltpu.SemaphoreType.DMA((count,))],
        name="assemble",
    )(table, *owns, *parts)


def column_order(block, table, unit):
    count = block.shape[1] // unit

    def body(table_ref, in_ref, out_ref):
        for i in range(count):
            column = pl.multiple_of(table_ref[i] * unit, unit)
            out_ref[:, i * unit : (i + 1) * unit] = in_ref[:, pl.ds(column, unit)]

    return pl.pallas_call(
        body,
        in_specs=[
            pl.BlockSpec(memory_space=pltpu.SMEM),
            pl.BlockSpec(memory_space=pltpu.VMEM),
        ],
        out_specs=pl.BlockSpec(memory_space=pltpu.VMEM),
        out_shape=jax.ShapeDtypeStruct(block.shape, block.dtype),
        name="column_order",
    )(table, block)


def finish(parts, owner, cuts):
    unit = parts[0].shape[1]
    n_places = sum(part.shape[0] for part in parts)

    def body(owner_ref, *refs):
        part_refs = refs[: len(parts)]
        out_refs = refs[len(parts) :]
        place = 0
        for part_ref in part_refs:
            for k in range(part_ref.shape[0]):
                row = pl.multiple_of(owner_ref[place] * unit, unit)
                at = 0
                for out_ref, cut in zip(out_refs, cuts):
                    out_ref[pl.ds(row, unit), :] = part_ref[k, :, at : at + cut].astype(jnp.float32)
                    at += cut
                place += 1

    return pl.pallas_call(
        body,
        in_specs=[pl.BlockSpec(memory_space=pltpu.SMEM)]
        + [pl.BlockSpec(memory_space=pltpu.VMEM)] * len(parts),
        out_specs=[pl.BlockSpec(memory_space=pltpu.VMEM)] * len(cuts),
        out_shape=[jax.ShapeDtypeStruct((n_places * unit, cut), jnp.float32) for cut in cuts],
        name="finish",
    )(owner, *parts)


def hop_bit(core, stage, bits):
    return 1 + stage if core == 0 else bits - stage


def hop_pairs(n_dp, stage):
    bits = n_dp.bit_length() - 2
    return [(i, i ^ (1 << hop_bit(i % 2, stage, bits))) for i in range(n_dp)]


def swap_core(block, n_dp):
    return lax.ppermute(block, "dp", [(i, i ^ 1) for i in range(n_dp)])


def ahead(block, n_line, step):
    return lax.ppermute(block, "fsdp", [(i, (i + step) % n_line) for i in range(n_line)])


def plane_hops(block, n_dp):
    across = (1 << n_dp.bit_length() - 1) - 2
    both = [(i, i ^ across) for i in range(n_dp)]
    hops = [hop_pairs(n_dp, stage) for stage in range(n_dp.bit_length() - 2)] + [both]
    return [lax.ppermute(block, "dp", pairs) for pairs in hops]


def add_up(terms):
    total = terms[0].astype(jnp.float32)
    for term in terms[1:]:
        total = total + term.astype(jnp.float32)
    return total


def reduce_steps(away, keep, n_dp, n_line):
    (away,) = yield [away]
    (got,) = yield [swap_core(away, n_dp)]
    terms = [keep, got]
    half = keep.shape[0] // 2
    for stage in range(n_dp.bit_length() - 2):
        (send,) = yield [add_up([term[half:] for term in terms]).astype(jnp.bfloat16)]
        (got,) = yield [lax.ppermute(send, "dp", hop_pairs(n_dp, stage))]
        terms = [term[:half] for term in terms] + [got]
        half //= 2
    terms = [term[0] for term in terms]
    sends = yield [
        add_up([term[step] for term in terms]).astype(jnp.bfloat16) for step in range(1, n_line)
    ]
    arrived = yield [ahead(send, n_line, step + 1) for step, send in enumerate(sends)]
    total = add_up([term[0] for term in terms] + arrived)
    (near,) = yield [total.astype(jnp.bfloat16)[None]]
    got = yield plane_hops(near, n_dp)
    (send,) = yield [jnp.concatenate([near] + got)]
    (got,) = yield [swap_core(send, n_dp)]
    return [send, got]


def small_steps(mine, n_dp, n_line):
    (mine,) = yield [mine]
    for bit in range(n_dp.bit_length() - 1):
        pairs = [(i, i ^ (1 << bit)) for i in range(n_dp)]
        (got,) = yield [lax.ppermute(mine, "dp", pairs)]
        (mine,) = yield [mine + got]
    line = lax.axis_index("fsdp")

    def part(step):
        return lax.dynamic_index_in_dim(mine, (line + step) % n_line, 0, keepdims=False)

    arrived = yield [ahead(part(step), n_line, step) for step in range(1, n_line)]
    total = part(0)
    for item in arrived:
        total = total + item
    return [total]


class Reduction:
    def __init__(self, steps, close):
        self.steps = steps
        self.close = close
        self.parts = None
        self.held = None
        self.begin = next(steps)

    def take(self, got):
        try:
            return self.steps.send(got)
        except StopIteration as stop:
            self.parts = stop.value
            return []

    def result(self):
        if self.held is None:
            self.held = self.steps.send(self.begin)
        while self.parts is None:
            sends = self.take(self.held)
            if self.parts is None:
                self.held = self.steps.send(sends)
        return self.close(self.parts)


class Ready:
    def __init__(self, outs):
        self.outs = outs

    def result(self):
        return self.outs


def tick(value, running):
    running = [item for item in running if isinstance(item, Reduction) and item.parts is None]
    old = [item for item in running if item.held is not None]
    value, gots = lax.optimization_barrier((value, [item.held for item in old]))
    sends = [item.take(got) for item, got in zip(old, gots)]
    new = [item for item in running if item.held is None]
    sends = sends + [item.begin for item in new]
    value, sends = lax.optimization_barrier((value, sends))
    for item, send in zip(old + new, sends):
        if item.parts is None:
            item.held = item.steps.send(send)
    return value


def place_of(n_dp, me, flip):
    bits = n_dp.bit_length() - 2
    core = me % 2
    halves = []
    for other in range(2):
        place = jnp.arange(1 << bits, dtype=jnp.int32)
        owner = jnp.full((1 << bits,), me ^ other, jnp.int32)
        for stage in range(bits):
            at = bits - 1 - stage if flip else stage
            low = 1 << hop_bit(0, stage, bits)
            high = 1 << hop_bit(1, stage, bits)
            mask = jnp.where((core ^ other) == 0, low, high)
            owner = owner ^ (((place >> at) & 1) * mask)
        halves.append(owner)
    return jnp.concatenate(halves)


class Wide:
    def __init__(self, shard):
        self.shard = shard

    def gather(self, w_qkv, w_out, w_fc1, w_fc2, smalls):
        def full(matrix):
            return lax.all_gather(matrix, "fsdp", axis=0, tiled=True)

        self.full = [full(w_qkv), full(w_out), full(w_fc1), full(w_fc2)]
        return lax.all_gather(smalls, "fsdp", axis=0)

    def first(self):
        return self.full[:2]

    def second(self):
        return self.full[2]

    def third(self):
        return self.full[3]

    def pass_one(self, gate):
        return gate

    pass_two = pass_three = pass_four = pass_one

    def rows(self, block):
        return block

    def wide_columns(self, block):
        return block

    def total(self, terms):
        bf16 = jnp.bfloat16
        outs = []
        for left, right in terms:
            grad = t_times(left, right).astype(bf16)
            own = lax.psum_scatter(grad, "fsdp", scatter_dimension=0, tiled=True)
            outs.append(lax.psum(own, "dp").astype(jnp.float32))
        return Ready(outs)

    def total_small(self, smalls):
        own = lax.psum_scatter(
            smalls.astype(jnp.bfloat16), "fsdp", scatter_dimension=0, tiled=False
        )
        return Ready(lax.psum(own, "dp").astype(jnp.float32))


class Gather:
    def __init__(self, unit, n_dp, n_line):
        self.n_dp = n_dp
        self.line = [ahead(unit, n_line, step) for step in range(1, n_line)]

    def hop(self, block, stage):
        return lax.ppermute(block, "dp", hop_pairs(self.n_dp, stage))

    def fan(self, gate, columns):
        self.line, gate = lax.optimization_barrier((self.line, gate))
        near = jnp.stack([item[:, :columns] for item in self.line])[None]
        near, gate = lax.optimization_barrier((near, gate))
        self.parts = [near, self.hop(near, 0), self.hop(near, 1)]
        self.cores = [swap_core(near, self.n_dp)]
        return gate

    def forward(self, gate):
        self.parts[1], gate = lax.optimization_barrier((self.parts[1], gate))
        self.parts.append(self.hop(self.parts[1], 1))
        self.cores.append(swap_core(self.parts[1], self.n_dp))
        return gate

    def close(self, gate):
        late, gate = lax.optimization_barrier((self.parts[2:], gate))
        self.cores += [swap_core(item, self.n_dp) for item in late]
        self.parts = self.parts[:2] + late
        return gate


class Staged:
    def __init__(self, n_dp, n_line, dp, line, width):
        self.n_dp = n_dp
        self.n_line = n_line
        self.dp = dp
        self.line = line
        self.unit = width // n_line // n_dp
        steps = jnp.arange(n_line, dtype=jnp.int32)
        owner = place_of(n_dp, dp, False)
        self.owner = owner
        self.unline = (line - steps) % n_line
        first = line * n_dp
        got = self.unline[None, :] * n_dp + owner[:, None]
        self.got_table = jnp.concatenate([got.reshape(-1), first[None]]).astype(jnp.int32)
        send_line = (line + steps) % n_line
        send = send_line[None, :] * n_dp + place_of(n_dp, dp, True)[:, None]
        self.send_table = send.reshape(-1).astype(jnp.int32)
        natural = jnp.arange(width, dtype=jnp.int32)
        arranged = (
            self.send_table[:, None] * self.unit + jnp.arange(self.unit, dtype=jnp.int32)[None, :]
        ).reshape(-1)
        self.order = (natural[:, None] == arranged[None, :]).astype(jnp.bfloat16)

    def pick(self, shard):
        size = shard.shape[0] // self.n_dp
        return lax.dynamic_slice_in_dim(shard, self.dp * size, size, 0)

    def gather(self, w_qkv, w_out, w_fc1, w_fc2, smalls):
        n_dp = self.n_dp
        n_line = self.n_line
        shard = smalls.shape[1]
        size = self.unit
        wide = w_qkv.shape[1] + w_out.shape[1]
        fold = -(-smalls.shape[0] // size)
        padded = jnp.pad(smalls, ((0, size * fold - smalls.shape[0]), (0, 0)))
        packed = [padded[i * size : (i + 1) * size] for i in range(fold)]
        unit_one = jnp.concatenate([self.pick(w_qkv), self.pick(w_out)] + packed, axis=1)
        unit_two, unit_three = (self.pick(w_fc1), self.pick(w_fc2))
        one = Gather(unit_one, n_dp, n_line)
        unit_two = one.fan(unit_two, wide)
        far = jnp.stack([item[:, wide:] for item in one.line])
        two = Gather(unit_two, n_dp, n_line)
        two.line = one.forward(two.line)
        two.line = one.close(two.line)
        table, unit_three = two.fan((self.got_table, unit_three), unit_two.shape[1])
        three = Gather(unit_three, n_dp, n_line)
        full_qkv, full_out = assemble([w_qkv, w_out], one.parts + one.cores, table, n_line, size)
        self.one = (full_qkv, full_out)
        self.two = (w_fc1, two)
        self.three = (w_fc2, three, unit_three.shape)
        far = jnp.concatenate([far[:, :, i * shard : (i + 1) * shard] for i in range(fold)], axis=1)
        return jnp.take(jnp.concatenate([padded[None], far]), self.unline, axis=0)

    def first(self):
        return self.one

    def pass_one(self, gate):
        return self.two[1].forward(gate)

    def pass_two(self, gate):
        return self.three[1].fan(self.two[1].close(gate), self.three[2][1])

    def pass_three(self, gate):
        return self.three[1].forward(gate)

    def pass_four(self, gate):
        return self.three[1].close(gate)

    def second(self):
        own, got = self.two
        return assemble([own], got.parts + got.cores, self.got_table, self.n_line, self.unit)[0]

    def third(self):
        own, got, unit = self.three
        return assemble([own], got.parts + got.cores, self.got_table, self.n_line, unit[0])[0]

    def rows(self, block):
        return jnp.dot(block, self.order, preferred_element_type=jnp.float32).astype(jnp.bfloat16)

    def wide_columns(self, block):
        return column_order(block, self.send_table, block.shape[1] // (self.n_dp * self.n_line))

    def total(self, terms):
        n_dp = self.n_dp
        n_line = self.n_line
        sides = []
        for side in (1, 0):
            grads = []
            for left, right in terms:
                half = left.shape[1] // 2
                grad = t_times(left[:, side * half : (side + 1) * half], right).astype(jnp.bfloat16)
                grads.append(grad.reshape(n_dp // 2, n_line, -1, right.shape[1]))
            sides.append(jnp.concatenate(grads, axis=3) if len(grads) > 1 else grads[0])
        cuts = [right.shape[1] for left, right in terms]
        owner = self.owner.astype(jnp.int32)
        steps = reduce_steps(sides[0], sides[1], n_dp, n_line)
        return Reduction(steps, lambda parts: list(finish(parts, owner, cuts)))

    def total_small(self, smalls):
        n_small = smalls.shape[1]
        padded = jnp.pad(smalls, ((0, 0), (0, -n_small % 8), (0, 0)))
        return Reduction(
            small_steps(padded, self.n_dp, self.n_line), lambda parts: parts[0][:n_small]
        )


def per_device(
    patches,
    cotangent,
    ln1_gain,
    ln1_bias,
    w_qkv,
    w_out,
    ln2_gain,
    ln2_bias,
    w_fc1,
    fc1_bias,
    w_fc2,
    pos_table,
    pos_index,
    pos_weight,
):
    bf16 = jnp.bfloat16
    f32 = jnp.float32
    n_dp = lax.axis_size("dp")
    n_line = lax.axis_size("fsdp")
    dp = lax.axis_index("dp")
    line = lax.axis_index("fsdp")
    low_flag = dp < n_dp * 7 // 16
    rows = patches.shape[0]
    width = patches.shape[1]
    shard = width // n_line
    place, valid, segment = place_rows(rows, low_flag, pos_index, pos_weight)
    if n_dp == 8 and n_line <= 4 and shard % (16 * n_dp) == 0:
        plan = Staged(n_dp, n_line, dp, line, width)
    else:
        plan = Wide(shard)
    n_bias = fc1_bias.size // shard
    smalls = jnp.concatenate(
        [
            jnp.stack([ln1_gain, ln1_bias, ln2_gain, ln2_bias]),
            fc1_bias.reshape(-1, shard),
            pos_table,
        ]
    )
    n_small = smalls.shape[0]
    table = plan.gather(w_qkv, w_out, w_fc1, w_fc2, smalls)
    full_qkv, full_out = plan.first()

    def across(block):
        return block.transpose(1, 0, 2).reshape(block.shape[1], width).astype(f32)

    gain_one, bias_one, gain_two, bias_two = across(table[:, :4])
    full_bias = table[:, 4 : 4 + n_bias].reshape(-1).astype(f32)
    full_table = across(table[:, 4 + n_bias : n_small])

    hidden_in = patches.astype(f32) + jnp.dot(place, full_table, precision=highest)
    normed_one = layer_norm(hidden_in, gain_one, bias_one).astype(bf16)
    projected = jnp.dot(normed_one, full_qkv, preferred_element_type=f32).astype(bf16)
    projected = plan.pass_one(projected)
    attn_rows = plan.pass_two(attend(projected, segment))
    hidden_mid = hidden_in + jnp.dot(attn_rows, full_out, preferred_element_type=f32)
    normed_two = layer_norm(hidden_mid, gain_two, bias_two).astype(bf16)
    normed_two = plan.pass_three(normed_two)
    full_fc1 = plan.second()
    pre_act = jnp.dot(normed_two, full_fc1, preferred_element_type=f32) + full_bias
    share = 0.5 * (1.0 + lax.erf(pre_act * 0.5**0.5))
    bell = jnp.exp(-0.5 * pre_act * pre_act) * (0.5 / jnp.pi) ** 0.5
    activated = (pre_act * share).astype(bf16)
    slope = (share + pre_act * bell).astype(bf16)
    activated = plan.pass_four(activated)
    grad_out = jnp.where(valid[:, None], cotangent, jnp.zeros_like(cotangent))
    run_fc2 = plan.total([(plan.wide_columns(activated), grad_out)])
    activated = tick(activated, [run_fc2])
    full_fc2, activated = tick((plan.third(), activated), [run_fc2])

    grad_pre = (times_t(grad_out, full_fc2) * slope.astype(f32)).astype(bf16)
    grad_fc1_bias = jnp.sum(grad_pre.astype(f32), axis=0)
    run_fc1 = plan.total([(plan.rows(normed_two), grad_pre)])
    grad_pre = tick(grad_pre, [run_fc1])
    grad_norm_two = times_t(grad_pre, full_fc1)
    _, pull_two = jax.vjp(layer_norm, hidden_mid, gain_two, bias_two)
    back_mid, grad_gain_two, grad_bias_two = pull_two(grad_norm_two)
    grad_mid = grad_out.astype(f32) + back_mid
    grad_branch = tick(grad_mid.astype(bf16), [run_fc1])
    run_out = plan.total([(plan.rows(attn_rows), grad_branch)])
    grad_attn = times_t(grad_branch, full_out).astype(bf16)
    grad_attn = tick(grad_attn, [run_fc2, run_out])
    half = HEADS // 4
    back_a = attend_back(projected, grad_attn, segment, 0, half)
    back_a, grad_attn = tick((back_a, grad_attn), [run_fc2, run_fc1, run_out])
    back_b = attend_back(projected, grad_attn, segment, half, half)
    back_a, back_b = tick((back_a, back_b), [run_fc2, run_fc1, run_out])
    side = back_a.shape[1] // 3
    grad_proj = jnp.concatenate(
        [part[:, i * side : (i + 1) * side] for i in range(3) for part in (back_a, back_b)], axis=1
    )
    run_qkv = plan.total([(plan.rows(normed_one), grad_proj)])
    grad_proj = tick(grad_proj, [run_qkv])
    every = [run_fc2, run_fc1, run_out]
    grad_norm_one = tick(times_t(grad_proj, full_qkv), [run_qkv, run_fc2])
    _, pull_one = jax.vjp(layer_norm, hidden_in, gain_one, bias_one)
    back_in, grad_gain_one, grad_bias_one = pull_one(grad_norm_one)
    grad_in = grad_mid + back_in
    grad_table = jnp.dot(place.T, grad_in, precision=highest)
    grad_table, activated = tick((grad_table, activated), [run_qkv] + every)
    branch_out = jnp.dot(activated, full_fc2, preferred_element_type=f32)
    block_out = jnp.where(valid[:, None], hidden_mid + branch_out, 0.0).astype(bf16)
    block_out = tick(block_out, [run_qkv] + every)

    def split(block):
        return block.reshape(-1, n_line, shard).transpose(1, 0, 2)

    rows_small = jnp.concatenate(
        [
            split(jnp.stack([grad_gain_one, grad_bias_one, grad_gain_two, grad_bias_two])),
            grad_fc1_bias.reshape(n_line, -1, shard),
            split(grad_table),
        ],
        axis=1,
    )
    run_small = plan.total_small(rows_small)
    (sum_fc2,) = tick(run_fc2.result(), [run_qkv])
    (sum_fc1,) = tick(run_fc1.result(), [run_qkv])
    (sum_out,) = run_out.result()
    (sum_qkv,) = run_qkv.result()
    small = run_small.result()
    return (
        block_out,
        grad_in.astype(bf16),
        small[0],
        small[1],
        sum_qkv,
        sum_out,
        small[2],
        small[3],
        sum_fc1,
        small[4 : 4 + n_bias].reshape(-1),
        sum_fc2,
        small[4 + n_bias :],
    )


def solution(mesh):
    return jax.shard_map(
        per_device,
        mesh=mesh,
        in_specs=(
            P(("dp", "fsdp"), None),
            P(("dp", "fsdp"), None),
            P("fsdp"),
            P("fsdp"),
            P("fsdp", None),
            P("fsdp", None),
            P("fsdp"),
            P("fsdp"),
            P("fsdp", None),
            P("fsdp"),
            P("fsdp", None),
            P(None, "fsdp"),
            P(),
            P(),
        ),
        out_specs=(
            P(("dp", "fsdp"), None),
            P(("dp", "fsdp"), None),
            P("fsdp"),
            P("fsdp"),
            P("fsdp", None),
            P("fsdp", None),
            P("fsdp"),
            P("fsdp"),
            P("fsdp", None),
            P("fsdp"),
            P("fsdp", None),
            P(None, "fsdp"),
        ),
        check_vma=False,
    )
```

```python
import jax
import jax.numpy as jnp
from jax import lax
from jax.experimental import pallas as pl
from jax.experimental.pallas import tpu as pltpu
from jax.sharding import PartitionSpec as P

HEADS = 16
HDIM = 64
POS = 50
HIGH_LEN = 145
TILE = 128


highest = lax.Precision.HIGHEST


def layer_norm(hidden, gain, shift):
    centre = hidden - jnp.mean(hidden, axis=-1, keepdims=True)
    spread = jnp.mean(centre * centre, axis=-1, keepdims=True)
    return centre * lax.rsqrt(spread + 1e-06) * gain + shift


def place_rows(rows, low_flag, pos_index, pos_weight):
    offsets = jnp.arange(rows, dtype=jnp.int32)
    table_ids = jnp.arange(POS, dtype=jnp.int32)
    high_ids = jnp.arange(HIGH_LEN, dtype=jnp.int32)
    picks = (pos_index[:, :, None] == table_ids[None, None, :]).astype(jnp.float32)
    interp = jnp.sum(pos_weight[:, :, None] * picks, axis=1)
    low_valid = offsets < rows // POS * POS
    high_valid = offsets < rows // HIGH_LEN * HIGH_LEN
    low_place = (((offsets % POS)[:, None] == table_ids[None, :]) & low_valid[:, None]).astype(
        jnp.float32
    )
    high_pick = (((offsets % HIGH_LEN)[:, None] == high_ids[None, :]) & high_valid[:, None]).astype(
        jnp.float32
    )
    high_place = jnp.dot(high_pick, interp, precision=highest)
    place = jnp.where(low_flag, low_place, high_place)
    valid = jnp.where(low_flag, low_valid, high_valid)
    segment = jnp.where(
        low_flag,
        jnp.where(low_valid, offsets // POS, -1),
        jnp.where(high_valid, offsets // HIGH_LEN, -1),
    )
    return (place, valid, segment)


def key_windows(rows):
    out = []
    for start in range(0, rows, TILE):
        least, most = rows, 0
        for size in (POS, HIGH_LEN):
            used = rows // size * size
            for row in (start, start + TILE - 1):
                image = row // size
                begin = image * size if row < used else used
                end = begin + size if row < used else rows
                least, most = min(least, begin), max(most, end)
        out.append((start, least // TILE * TILE, -(-most // TILE) * TILE))
    return out


def times_t(left, right):
    return lax.dot_general(left, right, (((1,), (1,)), ((), ())), preferred_element_type=jnp.float32)


def t_times(left, right):
    return lax.dot_general(left, right, (((0,), (0,)), ((), ())), preferred_element_type=jnp.float32)


def halves(block, scale=None):
    lane = lax.broadcasted_iota(jnp.int32, block.shape, 1)
    if scale is not None:
        block = block * jnp.asarray(scale, block.dtype)
    zero = jnp.zeros_like(block)
    return (jnp.where(lane < HDIM, block, zero), jnp.where(lane < HDIM, zero, block))


def soft(query, keys, same):
    scores = jnp.where(same, times_t(query, keys), -1e30)
    expo = jnp.exp(scores - jnp.max(scores, axis=-1, keepdims=True))
    return expo * (1.0 / jnp.sum(expo, axis=-1, keepdims=True))


def attend_body(windows, col_ref, row_ref, q_ref, k_ref, v_ref, out_ref):
    values = halves(v_ref[...])
    for start, lo, hi in windows:
        rows = slice(start, start + TILE)
        same = col_ref[rows, :] == row_ref[:, lo:hi]
        keys = k_ref[lo:hi, :]
        total = None
        for query, value in zip(halves(q_ref[rows, :], HDIM ** (-0.5)), values):
            probs = soft(query, keys, same).astype(jnp.bfloat16)
            part = jnp.dot(probs, value[lo:hi], preferred_element_type=jnp.float32)
            total = part if total is None else total + part
        out_ref[rows, :] = total.astype(jnp.bfloat16)


def attend_back_body(windows, col_ref, row_ref, q_ref, k_ref, v_ref, g_ref, out_ref, dk_ref, dv_ref):
    width = q_ref.shape[1]
    full = out_ref.shape[1] // 3
    at = pl.program_id(0) * width
    dk_ref[...] = jnp.zeros_like(dk_ref)
    dv_ref[...] = jnp.zeros_like(dv_ref)
    scaled = halves(k_ref[...], HDIM ** (-0.5))
    for start, lo, hi in windows:
        rows = slice(start, start + TILE)
        same = col_ref[rows, :] == row_ref[:, lo:hi]
        keys = k_ref[lo:hi, :]
        values = v_ref[lo:hi, :]
        total = None
        queries = halves(q_ref[rows, :], HDIM ** (-0.5))
        grads = halves(g_ref[rows, :])
        for query, grad, key in zip(queries, grads, scaled):
            probs = soft(query, keys, same)
            grad_probs = times_t(grad, values)
            centre = jnp.sum(probs * grad_probs, axis=-1, keepdims=True)
            grad_scores = (probs * (grad_probs - centre)).astype(jnp.bfloat16)
            part = jnp.dot(grad_scores, key[lo:hi], preferred_element_type=jnp.float32)
            total = part if total is None else total + part
            dk_ref[lo:hi, :] += t_times(grad_scores, query)
            dv_ref[lo:hi, :] += t_times(probs.astype(jnp.bfloat16), grad)
        out_ref[rows, pl.ds(pl.multiple_of(at, width), width)] = total.astype(jnp.bfloat16)
    out_ref[:, pl.ds(pl.multiple_of(full + at, width), width)] = dk_ref[...].astype(jnp.bfloat16)
    out_ref[:, pl.ds(pl.multiple_of(2 * full + at, width), width)] = dv_ref[...].astype(jnp.bfloat16)


def pair_specs(rows, pairs, start=0):
    pair = 2 * HDIM
    whole = [
        pl.BlockSpec((rows, 1), lambda i: (0, 0)),
        pl.BlockSpec((1, rows), lambda i: (0, 0)),
    ]
    return whole + [
        pl.BlockSpec((rows, pair), lambda i, j=j: (0, j * pairs + start + i)) for j in range(3)
    ]


def attend(projected, segment):
    rows = projected.shape[0]
    pairs = HEADS // 2
    windows = key_windows(rows)

    def body(*refs):
        attend_body(windows, *refs)

    return pl.pallas_call(
        body,
        grid=(pairs,),
        in_specs=pair_specs(rows, pairs),
        out_specs=pl.BlockSpec((rows, 2 * HDIM), lambda i: (0, i)),
        out_shape=jax.ShapeDtypeStruct((rows, HEADS * HDIM), jnp.bfloat16),
        name="attend",
    )(segment[:, None], segment[None, :], projected, projected, projected)


def attend_back(projected, grad_attn, segment, start, count):
    rows = projected.shape[0]
    pairs = HEADS // 2
    windows = key_windows(rows)
    wide = 3 * count * 2 * HDIM

    def body(*refs):
        attend_back_body(windows, *refs)

    return pl.pallas_call(
        body,
        grid=(count,),
        in_specs=pair_specs(rows, pairs, start)
        + [pl.BlockSpec((rows, 2 * HDIM), lambda i: (0, start + i))],
        out_specs=pl.BlockSpec((rows, wide), lambda i: (0, 0)),
        out_shape=jax.ShapeDtypeStruct((rows, wide), jnp.bfloat16),
        scratch_shapes=[pltpu.VMEM((rows, 2 * HDIM), jnp.float32)] * 2,
        name="attend_back",
    )(segment[:, None], segment[None, :], projected, projected, projected, grad_attn)


def copies(pairs_of, sems):
    moves = [
        pltpu.make_async_copy(source, target, sems.at[i])
        for i, (source, target) in enumerate(pairs_of)
    ]
    for move in moves:
        move.start()
    for move in moves:
        move.wait()


def assemble(owns, parts, table, n_line, unit):
    n_places = sum(part.shape[0] for part in parts)
    n_own = len(owns)
    n_parts = len(parts)
    ends = []
    for own in owns:
        ends.append((ends[-1] if ends else 0) + own.shape[1])
    count = n_own * (1 + n_places * (n_line - 1))

    def body(table_ref, *refs):
        own_refs = refs[:n_own]
        part_refs = refs[n_own : n_own + n_parts]
        out_refs = refs[n_own + n_parts : 2 * n_own + n_parts]
        sems = refs[-1]
        todo = []
        for own_ref, out_ref, end in zip(own_refs, out_refs, ends):
            shard_rows = own_ref.shape[0]
            columns = pl.ds(end - own_ref.shape[1], own_ref.shape[1])
            first = pl.multiple_of(table_ref[n_places * n_line] * unit, unit)
            todo.append((own_ref, out_ref.at[pl.ds(first, shard_rows), :]))
            place = 0
            for part_ref in part_refs:
                for k in range(part_ref.shape[0]):
                    for step in range(1, n_line):
                        row = pl.multiple_of(table_ref[place * n_line + step] * unit, unit)
                        todo.append(
                            (
                                part_ref.at[k, step - 1, pl.ds(0, unit), columns],
                                out_ref.at[pl.ds(row, unit), :],
                            )
                        )
                    place += 1
        copies(todo, sems)

    anywhere = pl.BlockSpec(memory_space=pl.ANY)
    return pl.pallas_call(
        body,
        in_specs=[pl.BlockSpec(memory_space=pltpu.SMEM)] + [anywhere] * (n_own + n_parts),
        out_specs=[pl.BlockSpec(memory_space=pltpu.VMEM)] * n_own,
        out_shape=[
            jax.ShapeDtypeStruct((own.shape[0] * n_line, own.shape[1]), own.dtype) for own in owns
        ],
        scratch_shapes=[pltpu.SemaphoreType.DMA((count,))],
        name="assemble",
    )(table, *owns, *parts)


def column_order(block, table, unit):
    count = block.shape[1] // unit

    def body(table_ref, in_ref, out_ref):
        for i in range(count):
            column = pl.multiple_of(table_ref[i] * unit, unit)
            out_ref[:, i * unit : (i + 1) * unit] = in_ref[:, pl.ds(column, unit)]

    return pl.pallas_call(
        body,
        in_specs=[
            pl.BlockSpec(memory_space=pltpu.SMEM),
            pl.BlockSpec(memory_space=pltpu.VMEM),
        ],
        out_specs=pl.BlockSpec(memory_space=pltpu.VMEM),
        out_shape=jax.ShapeDtypeStruct(block.shape, block.dtype),
        name="column_order",
    )(table, block)


def finish(parts, owner, cuts):
    unit = parts[0].shape[1]
    n_places = sum(part.shape[0] for part in parts)

    def body(owner_ref, *refs):
        part_refs = refs[: len(parts)]
        out_refs = refs[len(parts) :]
        place = 0
        for part_ref in part_refs:
            for k in range(part_ref.shape[0]):
                row = pl.multiple_of(owner_ref[place] * unit, unit)
                at = 0
                for out_ref, cut in zip(out_refs, cuts):
                    out_ref[pl.ds(row, unit), :] = part_ref[k, :, at : at + cut].astype(jnp.float32)
                    at += cut
                place += 1

    return pl.pallas_call(
        body,
        in_specs=[pl.BlockSpec(memory_space=pltpu.SMEM)]
        + [pl.BlockSpec(memory_space=pltpu.VMEM)] * len(parts),
        out_specs=[pl.BlockSpec(memory_space=pltpu.VMEM)] * len(cuts),
        out_shape=[jax.ShapeDtypeStruct((n_places * unit, cut), jnp.float32) for cut in cuts],
        name="finish",
    )(owner, *parts)


def hop_bit(core, stage, bits):
    return 1 + stage if core == 0 else bits - stage


def hop_pairs(n_dp, stage):
    bits = n_dp.bit_length() - 2
    return [(i, i ^ (1 << hop_bit(i % 2, stage, bits))) for i in range(n_dp)]


def swap_core(block, n_dp):
    return lax.ppermute(block, "dp", [(i, i ^ 1) for i in range(n_dp)])


def ahead(block, n_line, step):
    return lax.ppermute(block, "fsdp", [(i, (i + step) % n_line) for i in range(n_line)])


def plane_hops(block, n_dp):
    across = (1 << n_dp.bit_length() - 1) - 2
    both = [(i, i ^ across) for i in range(n_dp)]
    hops = [hop_pairs(n_dp, stage) for stage in range(n_dp.bit_length() - 2)] + [both]
    return [lax.ppermute(block, "dp", pairs) for pairs in hops]


def add_up(terms):
    total = terms[0].astype(jnp.float32)
    for term in terms[1:]:
        total = total + term.astype(jnp.float32)
    return total


def reduce_steps(away, keep, n_dp, n_line):
    (away,) = yield [away]
    (got,) = yield [swap_core(away, n_dp)]
    terms = [keep, got]
    half = keep.shape[0] // 2
    for stage in range(n_dp.bit_length() - 2):
        (send,) = yield [add_up([term[half:] for term in terms]).astype(jnp.bfloat16)]
        (got,) = yield [lax.ppermute(send, "dp", hop_pairs(n_dp, stage))]
        terms = [term[:half] for term in terms] + [got]
        half //= 2
    terms = [term[0] for term in terms]
    sends = yield [
        add_up([term[step] for term in terms]).astype(jnp.bfloat16) for step in range(1, n_line)
    ]
    arrived = yield [ahead(send, n_line, step + 1) for step, send in enumerate(sends)]
    total = add_up([term[0] for term in terms] + arrived)
    (near,) = yield [total.astype(jnp.bfloat16)[None]]
    got = yield plane_hops(near, n_dp)
    (send,) = yield [jnp.concatenate([near] + got)]
    (got,) = yield [swap_core(send, n_dp)]
    return [send, got]


def small_steps(mine, n_dp, n_line):
    (mine,) = yield [mine]
    for bit in range(n_dp.bit_length() - 1):
        pairs = [(i, i ^ (1 << bit)) for i in range(n_dp)]
        (got,) = yield [lax.ppermute(mine, "dp", pairs)]
        (mine,) = yield [mine + got]
    line = lax.axis_index("fsdp")

    def part(step):
        return lax.dynamic_index_in_dim(mine, (line + step) % n_line, 0, keepdims=False)

    arrived = yield [ahead(part(step), n_line, step) for step in range(1, n_line)]
    total = part(0)
    for item in arrived:
        total = total + item
    return [total]


class Reduction:
    def __init__(self, steps, close):
        self.steps = steps
        self.close = close
        self.parts = None
        self.held = None
        self.begin = next(steps)

    def take(self, got):
        try:
            return self.steps.send(got)
        except StopIteration as stop:
            self.parts = stop.value
            return []

    def result(self):
        if self.held is None:
            self.held = self.steps.send(self.begin)
        while self.parts is None:
            sends = self.take(self.held)
            if self.parts is None:
                self.held = self.steps.send(sends)
        return self.close(self.parts)


class Ready:
    def __init__(self, outs):
        self.outs = outs

    def result(self):
        return self.outs


def tick(value, running):
    running = [item for item in running if isinstance(item, Reduction) and item.parts is None]
    old = [item for item in running if item.held is not None]
    value, gots = lax.optimization_barrier((value, [item.held for item in old]))
    sends = [item.take(got) for item, got in zip(old, gots)]
    new = [item for item in running if item.held is None]
    sends = sends + [item.begin for item in new]
    value, sends = lax.optimization_barrier((value, sends))
    for item, send in zip(old + new, sends):
        if item.parts is None:
            item.held = item.steps.send(send)
    return value


def place_of(n_dp, me, flip):
    bits = n_dp.bit_length() - 2
    core = me % 2
    halves = []
    for other in range(2):
        place = jnp.arange(1 << bits, dtype=jnp.int32)
        owner = jnp.full((1 << bits,), me ^ other, jnp.int32)
        for stage in range(bits):
            at = bits - 1 - stage if flip else stage
            low = 1 << hop_bit(0, stage, bits)
            high = 1 << hop_bit(1, stage, bits)
            mask = jnp.where((core ^ other) == 0, low, high)
            owner = owner ^ (((place >> at) & 1) * mask)
        halves.append(owner)
    return jnp.concatenate(halves)


class Wide:
    def __init__(self, shard):
        self.shard = shard

    def gather(self, w_qkv, w_out, w_fc1, w_fc2, smalls):
        def full(matrix):
            return lax.all_gather(matrix, "fsdp", axis=0, tiled=True)

        self.full = [full(w_qkv), full(w_out), full(w_fc1), full(w_fc2)]
        return lax.all_gather(smalls, "fsdp", axis=0)

    def first(self):
        return self.full[:2]

    def second(self):
        return self.full[2]

    def third(self):
        return self.full[3]

    def pass_one(self, gate):
        return gate

    pass_two = pass_three = pass_four = pass_one

    def rows(self, block):
        return block

    def wide_columns(self, block):
        return block

    def total(self, terms):
        bf16 = jnp.bfloat16
        outs = []
        for left, right in terms:
            grad = t_times(left, right).astype(bf16)
            own = lax.psum_scatter(grad, "fsdp", scatter_dimension=0, tiled=True)
            outs.append(lax.psum(own, "dp").astype(jnp.float32))
        return Ready(outs)

    def total_small(self, smalls):
        own = lax.psum_scatter(
            smalls.astype(jnp.bfloat16), "fsdp", scatter_dimension=0, tiled=False
        )
        return Ready(lax.psum(own, "dp").astype(jnp.float32))


class Gather:
    def __init__(self, unit, n_dp, n_line):
        self.n_dp = n_dp
        self.line = [ahead(unit, n_line, step) for step in range(1, n_line)]

    def hop(self, block, stage):
        return lax.ppermute(block, "dp", hop_pairs(self.n_dp, stage))

    def fan(self, gate, columns):
        self.line, gate = lax.optimization_barrier((self.line, gate))
        near = jnp.stack([item[:, :columns] for item in self.line])[None]
        near, gate = lax.optimization_barrier((near, gate))
        self.parts = [near, self.hop(near, 0), self.hop(near, 1)]
        self.cores = [swap_core(near, self.n_dp)]
        return gate

    def forward(self, gate):
        self.parts[1], gate = lax.optimization_barrier((self.parts[1], gate))
        self.parts.append(self.hop(self.parts[1], 1))
        self.cores.append(swap_core(self.parts[1], self.n_dp))
        return gate

    def close(self, gate):
        late, gate = lax.optimization_barrier((self.parts[2:], gate))
        self.cores += [swap_core(item, self.n_dp) for item in late]
        self.parts = self.parts[:2] + late
        return gate


class Staged:
    def __init__(self, n_dp, n_line, dp, line, width):
        self.n_dp = n_dp
        self.n_line = n_line
        self.dp = dp
        self.line = line
        self.unit = width // n_line // n_dp
        steps = jnp.arange(n_line, dtype=jnp.int32)
        owner = place_of(n_dp, dp, False)
        self.owner = owner
        self.unline = (line - steps) % n_line
        first = line * n_dp
        got = self.unline[None, :] * n_dp + owner[:, None]
        self.got_table = jnp.concatenate([got.reshape(-1), first[None]]).astype(jnp.int32)
        send_line = (line + steps) % n_line
        send = send_line[None, :] * n_dp + place_of(n_dp, dp, True)[:, None]
        self.send_table = send.reshape(-1).astype(jnp.int32)
        natural = jnp.arange(width, dtype=jnp.int32)
        arranged = (
            self.send_table[:, None] * self.unit + jnp.arange(self.unit, dtype=jnp.int32)[None, :]
        ).reshape(-1)
        self.order = (natural[:, None] == arranged[None, :]).astype(jnp.bfloat16)

    def pick(self, shard):
        size = shard.shape[0] // self.n_dp
        return lax.dynamic_slice_in_dim(shard, self.dp * size, size, 0)

    def gather(self, w_qkv, w_out, w_fc1, w_fc2, smalls):
        n_dp = self.n_dp
        n_line = self.n_line
        shard = smalls.shape[1]
        size = self.unit
        wide = w_qkv.shape[1] + w_out.shape[1]
        fold = -(-smalls.shape[0] // size)
        padded = jnp.pad(smalls, ((0, size * fold - smalls.shape[0]), (0, 0)))
        packed = [padded[i * size : (i + 1) * size] for i in range(fold)]
        unit_one = jnp.concatenate([self.pick(w_qkv), self.pick(w_out)] + packed, axis=1)
        unit_two, unit_three = (self.pick(w_fc1), self.pick(w_fc2))
        one = Gather(unit_one, n_dp, n_line)
        unit_two = one.fan(unit_two, wide)
        far = jnp.stack([item[:, wide:] for item in one.line])
        two = Gather(unit_two, n_dp, n_line)
        two.line = one.forward(two.line)
        two.line = one.close(two.line)
        table, unit_three = two.fan((self.got_table, unit_three), unit_two.shape[1])
        three = Gather(unit_three, n_dp, n_line)
        full_qkv, full_out = assemble([w_qkv, w_out], one.parts + one.cores, table, n_line, size)
        self.one = (full_qkv, full_out)
        self.two = (w_fc1, two)
        self.three = (w_fc2, three, unit_three.shape)
        far = jnp.concatenate([far[:, :, i * shard : (i + 1) * shard] for i in range(fold)], axis=1)
        return jnp.take(jnp.concatenate([padded[None], far]), self.unline, axis=0)

    def first(self):
        return self.one

    def pass_one(self, gate):
        return self.two[1].forward(gate)

    def pass_two(self, gate):
        return self.three[1].fan(self.two[1].close(gate), self.three[2][1])

    def pass_three(self, gate):
        return self.three[1].forward(gate)

    def pass_four(self, gate):
        return self.three[1].close(gate)

    def second(self):
        own, got = self.two
        return assemble([own], got.parts + got.cores, self.got_table, self.n_line, self.unit)[0]

    def third(self):
        own, got, unit = self.three
        return assemble([own], got.parts + got.cores, self.got_table, self.n_line, unit[0])[0]

    def rows(self, block):
        return jnp.dot(block, self.order, preferred_element_type=jnp.float32).astype(jnp.bfloat16)

    def wide_columns(self, block):
        return column_order(block, self.send_table, block.shape[1] // (self.n_dp * self.n_line))

    def total(self, terms):
        n_dp = self.n_dp
        n_line = self.n_line
        sides = []
        for side in (1, 0):
            grads = []
            for left, right in terms:
                half = left.shape[1] // 2
                grad = t_times(left[:, side * half : (side + 1) * half], right).astype(jnp.bfloat16)
                grads.append(grad.reshape(n_dp // 2, n_line, -1, right.shape[1]))
            sides.append(jnp.concatenate(grads, axis=3) if len(grads) > 1 else grads[0])
        cuts = [right.shape[1] for left, right in terms]
        owner = self.owner.astype(jnp.int32)
        steps = reduce_steps(sides[0], sides[1], n_dp, n_line)
        return Reduction(steps, lambda parts: list(finish(parts, owner, cuts)))

    def total_small(self, smalls):
        n_small = smalls.shape[1]
        padded = jnp.pad(smalls, ((0, 0), (0, -n_small % 8), (0, 0)))
        return Reduction(
            small_steps(padded, self.n_dp, self.n_line), lambda parts: parts[0][:n_small]
        )


def per_device(
    patches,
    cotangent,
    ln1_gain,
    ln1_bias,
    w_qkv,
    w_out,
    ln2_gain,
    ln2_bias,
    w_fc1,
    fc1_bias,
    w_fc2,
    pos_table,
    pos_index,
    pos_weight,
):
    bf16 = jnp.bfloat16
    f32 = jnp.float32
    n_dp = lax.axis_size("dp")
    n_line = lax.axis_size("fsdp")
    dp = lax.axis_index("dp")
    line = lax.axis_index("fsdp")
    low_flag = dp < n_dp * 7 // 16
    rows = patches.shape[0]
    width = patches.shape[1]
    shard = width // n_line
    place, valid, segment = place_rows(rows, low_flag, pos_index, pos_weight)
    if n_dp == 8 and n_line <= 4 and shard % (16 * n_dp) == 0:
        plan = Staged(n_dp, n_line, dp, line, width)
    else:
        plan = Wide(shard)
    n_bias = fc1_bias.size // shard
    smalls = jnp.concatenate(
        [
            jnp.stack([ln1_gain, ln1_bias, ln2_gain, ln2_bias]),
            fc1_bias.reshape(-1, shard),
            pos_table,
        ]
    )
    n_small = smalls.shape[0]
    table = plan.gather(w_qkv, w_out, w_fc1, w_fc2, smalls)
    full_qkv, full_out = plan.first()

    def across(block):
        return block.transpose(1, 0, 2).reshape(block.shape[1], width).astype(f32)

    gain_one, bias_one, gain_two, bias_two = across(table[:, :4])
    full_bias = table[:, 4 : 4 + n_bias].reshape(-1).astype(f32)
    full_table = across(table[:, 4 + n_bias : n_small])

    hidden_in = patches.astype(f32) + jnp.dot(place, full_table, precision=highest)
    normed_one = layer_norm(hidden_in, gain_one, bias_one).astype(bf16)
    projected = jnp.dot(normed_one, full_qkv, preferred_element_type=f32).astype(bf16)
    projected = plan.pass_one(projected)
    attn_rows = plan.pass_two(attend(projected, segment))
    hidden_mid = hidden_in + jnp.dot(attn_rows, full_out, preferred_element_type=f32)
    normed_two = layer_norm(hidden_mid, gain_two, bias_two).astype(bf16)
    normed_two = plan.pass_three(normed_two)
    full_fc1 = plan.second()
    pre_act = jnp.dot(normed_two, full_fc1, preferred_element_type=f32) + full_bias
    share = 0.5 * (1.0 + lax.erf(pre_act * 0.5**0.5))
    bell = jnp.exp(-0.5 * pre_act * pre_act) * (0.5 / jnp.pi) ** 0.5
    activated = (pre_act * share).astype(bf16)
    slope = (share + pre_act * bell).astype(bf16)
    activated = plan.pass_four(activated)
    grad_out = jnp.where(valid[:, None], cotangent, jnp.zeros_like(cotangent))
    run_fc2 = plan.total([(plan.wide_columns(activated), grad_out)])
    activated = tick(activated, [run_fc2])
    full_fc2, activated = tick((plan.third(), activated), [run_fc2])

    grad_pre = (times_t(grad_out, full_fc2) * slope.astype(f32)).astype(bf16)
    grad_fc1_bias = jnp.sum(grad_pre.astype(f32), axis=0)
    run_fc1 = plan.total([(plan.rows(normed_two), grad_pre)])
    grad_pre = tick(grad_pre, [run_fc1])
    grad_norm_two = times_t(grad_pre, full_fc1)
    _, pull_two = jax.vjp(layer_norm, hidden_mid, gain_two, bias_two)
    back_mid, grad_gain_two, grad_bias_two = pull_two(grad_norm_two)
    grad_mid = grad_out.astype(f32) + back_mid
    grad_branch = tick(grad_mid.astype(bf16), [run_fc1])
    run_out = plan.total([(plan.rows(attn_rows), grad_branch)])
    grad_attn = times_t(grad_branch, full_out).astype(bf16)
    grad_attn = tick(grad_attn, [run_fc2, run_out])
    half = HEADS // 4
    back_a = attend_back(projected, grad_attn, segment, 0, half)
    back_a, grad_attn = tick((back_a, grad_attn), [run_fc2, run_fc1, run_out])
    back_b = attend_back(projected, grad_attn, segment, half, half)
    back_a, back_b = tick((back_a, back_b), [run_fc2, run_fc1, run_out])
    side = back_a.shape[1] // 3
    grad_proj = jnp.concatenate(
        [part[:, i * side : (i + 1) * side] for i in range(3) for part in (back_a, back_b)], axis=1
    )
    run_qkv = plan.total([(plan.rows(normed_one), grad_proj)])
    grad_proj = tick(grad_proj, [run_qkv])
    every = [run_fc2, run_fc1, run_out]
    grad_norm_one = tick(times_t(grad_proj, full_qkv), [run_qkv, run_fc2])
    _, pull_one = jax.vjp(layer_norm, hidden_in, gain_one, bias_one)
    back_in, grad_gain_one, grad_bias_one = pull_one(grad_norm_one)
    grad_in = grad_mid + back_in
    grad_table = jnp.dot(place.T, grad_in, precision=highest)
    grad_table, activated = tick((grad_table, activated), [run_qkv] + every)
    branch_out = jnp.dot(activated, full_fc2, preferred_element_type=f32)
    block_out = jnp.where(valid[:, None], hidden_mid + branch_out, 0.0).astype(bf16)
    block_out = tick(block_out, [run_qkv] + every)

    def split(block):
        return block.reshape(-1, n_line, shard).transpose(1, 0, 2)

    rows_small = jnp.concatenate(
        [
            split(jnp.stack([grad_gain_one, grad_bias_one, grad_gain_two, grad_bias_two])),
            grad_fc1_bias.reshape(n_line, -1, shard),
            split(grad_table),
        ],
        axis=1,
    )
    rows_small, block_out = lax.optimization_barrier((rows_small, block_out))
    run_small = plan.total_small(rows_small)
    (sum_fc2,) = tick(run_fc2.result(), [run_qkv])
    (sum_fc1,) = tick(run_fc1.result(), [run_qkv])
    (sum_out,) = run_out.result()
    (sum_qkv,) = run_qkv.result()
    small = run_small.result()
    return (
        block_out,
        grad_in.astype(bf16),
        small[0],
        small[1],
        sum_qkv,
        sum_out,
        small[2],
        small[3],
        sum_fc1,
        small[4 : 4 + n_bias].reshape(-1),
        sum_fc2,
        small[4 + n_bias :],
    )


def solution(mesh):
    return jax.shard_map(
        per_device,
        mesh=mesh,
        in_specs=(
            P(("dp", "fsdp"), None),
            P(("dp", "fsdp"), None),
            P("fsdp"),
            P("fsdp"),
            P("fsdp", None),
            P("fsdp", None),
            P("fsdp"),
            P("fsdp"),
            P("fsdp", None),
            P("fsdp"),
            P("fsdp", None),
            P(None, "fsdp"),
            P(),
            P(),
        ),
        out_specs=(
            P(("dp", "fsdp"), None),
            P(("dp", "fsdp"), None),
            P("fsdp"),
            P("fsdp"),
            P("fsdp", None),
            P("fsdp", None),
            P("fsdp"),
            P("fsdp"),
            P("fsdp", None),
            P("fsdp"),
            P("fsdp", None),
            P(None, "fsdp"),
        ),
        check_vma=False,
    )
```
